32 devices in a mesh: dp: 16 (over z, y, x), mp: 2 (over core).
Axes of the slice: x: 2, y: 2, z: 4, core: 2. Of those that a mesh axis runs over, the one named last changes fastest.
Arguments:
- image_codes: int32 [2, 16, 128], P(None, 'dp'), may hold values from 0 to 8191
- masked: int32 [2, 16, 128], P(None, 'dp'), may hold values from 0 to 1
- null_caption: int32 [2, 16], P(None, 'dp'), may hold values 0 or 1
- captions: bfloat16 [2, 16, 32, 4096], P(None, 'dp'), may hold values from -6 to 6
- step_count: int32 [1], replicated, may hold values from 2 to 20
- code_table: float32 [8192, 2048], P(('mp', 'dp')), may hold values from -0.625 to 0.625
- table_first: float32 [8192, 2048], P(('mp', 'dp')), may hold values from -1.66893e-06 to 1.66893e-06
- table_second: float32 [8192, 2048], P(('mp', 'dp')), may hold values from 5.402178e-16 to 8.643485e-15
- vectors: float32 [137, 2048], replicated, may hold values from -1 to 2
- vectors_first: float32 [137, 2048], replicated, may hold values from -6.67572e-06 to 6.67572e-06
- vectors_second: float32 [137, 2048], replicated, may hold values from 8.643485e-15 to 1.3829576e-13
- projections: float32 [4, 2048, 2048], P(None, 'dp', 'mp'), may hold values from -0.125 to 0.125
- projections_first: float32 [4, 2048, 2048], P(None, 'dp', 'mp'), may hold values from -1.66893e-06 to 1.66893e-06
- projections_second: float32 [4, 2048, 2048], P(None, 'dp', 'mp'), may hold values from 5.402178e-16 to 8.643485e-15
- text_maps: float32 [2, 4096, 2048], P(None, 'dp', 'mp'), may hold values from -0.09375 to 0.09375
- text_maps_first: float32 [2, 4096, 2048], P(None, 'dp', 'mp'), may hold values from -1.66893e-06 to 1.66893e-06
- text_maps_second: float32 [2, 4096, 2048], P(None, 'dp', 'mp'), may hold values from 5.402178e-16 to 8.643485e-15
- out_maps: float32 [2, 2048, 2048], P(None, ('mp', 'dp')), may hold values from -0.375 to 0.375
- out_maps_first: float32 [2, 2048, 2048], P(None, ('mp', 'dp')), may hold values from -1.66893e-06 to 1.66893e-06
- out_maps_second: float32 [2, 2048, 2048], P(None, ('mp', 'dp')), may hold values from 5.402178e-16 to 8.643485e-15
- expand: float32 [2048, 8192], P('dp', 'mp'), may hold values from -0.125 to 0.125
- expand_first: float32 [2048, 8192], P('dp', 'mp'), may hold values from -1.66893e-06 to 1.66893e-06
- expand_second: float32 [2048, 8192], P('dp', 'mp'), may hold values from 5.402178e-16 to 8.643485e-15
- contract: float32 [8192, 2048], P(('mp', 'dp')), may hold values from -0.0625 to 0.0625
- contract_first: float32 [8192, 2048], P(('mp', 'dp')), may hold values from -1.66893e-06 to 1.66893e-06
- contract_second: float32 [8192, 2048], P(('mp', 'dp')), may hold values from 5.402178e-16 to 8.643485e-15
Outputs:
- loss_value: float32 [], replicated
- grad_norm: float32 [], replicated
- new_code_table: float32 [8192, 2048], P(('mp', 'dp'))
- new_table_first: float32 [8192, 2048], P(('mp', 'dp'))
- new_table_second: float32 [8192, 2048], P(('mp', 'dp'))
- new_vectors: float32 [137, 2048], replicated
- new_vectors_first: float32 [137, 2048], replicated
- new_vectors_second: float32 [137, 2048], replicated
- new_projections: float32 [4, 2048, 2048], P(None, 'dp', 'mp')
- new_projections_first: float32 [4, 2048, 2048], P(None, 'dp', 'mp')
- new_projections_second: float32 [4, 2048, 2048], P(None, 'dp', 'mp')
- new_text_maps: float32 [2, 4096, 2048], P(None, 'dp', 'mp')
- new_text_maps_first: float32 [2, 4096, 2048], P(None, 'dp', 'mp')
- new_text_maps_second: float32 [2, 4096, 2048], P(None, 'dp', 'mp')
- new_out_maps: float32 [2, 2048, 2048], P(None, ('mp', 'dp'))
- new_out_maps_first: float32 [2, 2048, 2048], P(None, ('mp', 'dp'))
- new_out_maps_second: float32 [2, 2048, 2048], P(None, ('mp', 'dp'))
- new_expand: float32 [2048, 8192], P('dp', 'mp')
- new_expand_first: float32 [2048, 8192], P('dp', 'mp')
- new_expand_second: float32 [2048, 8192], P('dp', 'mp')
- new_contract: float32 [8192, 2048], P(('mp', 'dp'))
- new_contract_first: float32 [8192, 2048], P(('mp', 'dp'))
- new_contract_second: float32 [8192, 2048], P(('mp', 'dp'))
The draws below stay inside these ranges and needn't reach their ends.
All inputs are finite; a program needn't handle non-finite values. No bound on the sum of `null_caption` on one device may be relied on, other than what follows from the above.
Results may differ from the reference program's by a relative error of at most 0.0055.
The reference program's roundings to bfloat16 on the way count: a program that leaves them out, or rounds other values in their place, can miss the bound.
Values may be sent and summed in bfloat16 or wider, within the bound.
A program may use at most 576 MiB of HBM per device.

```python
import math
import jax
import jax.numpy as jnp
from jax import lax

D = 2048
HEADS = 16
HD = 128
FF = 8192
V = 8192
TD = 4096
S = 128
TEXT = 32
MICRO = 2
IMAGES = 16
PARAMS = 92555264


def draw_masked(key, part):
    first_key, second_key = jax.random.split(key)
    row_total = MICRO * IMAGES
    order = jnp.tile(jnp.arange(S, dtype=jnp.int32), (row_total, 1))
    ranks = jax.random.permutation(first_key, order, axis=1, independent=True)
    image = jnp.tile(jnp.arange(IMAGES, dtype=jnp.int32), MICRO)
    rising = (S - S // 4 - S // 8) * image // max(IMAGES - 1, 1)
    extra = jax.random.randint(second_key, (row_total,), 0, S // 8 + 1, dtype=jnp.int32)
    limit = S // 4 + rising + extra
    return (ranks < limit[:, None]).astype(jnp.int32).reshape(MICRO, IMAGES, S)


def draw_vectors(key, part):
    keys = jax.random.split(key, 3)
    leading = jax.random.normal(keys[0], (S + 1, D), jnp.float32) * (2.0 / D ** 0.5)
    gain_rows = 1.0 + jax.random.uniform(keys[1], (4, D), jnp.float32, -0.3, 0.3)
    bias_rows = 0.1 * jax.random.normal(keys[2], (4, D), jnp.float32)
    norm_rows = jnp.stack([gain_rows, bias_rows], 1).reshape(8, D)
    return jnp.concatenate([leading, norm_rows], 0).astype(jnp.float32)


def place_ends(entries, key, smallest, top_value):
    shape = entries.shape
    index_at = [jax.random.randint(jax.random.fold_in(key, axis), (), 0, shape[axis]) for axis in range(len(shape))]
    entries = entries.at[tuple(index_at)].set(smallest)
    longest = shape.index(max(shape))
    index_at[longest] = (index_at[longest] + 1) % shape[longest]
    return entries.at[tuple(index_at)].set(top_value)


def block_scale(rng, shape, shards, low, high):
    def one(dim, shards_of):
        heights = jax.random.uniform(jax.random.fold_in(jax.random.fold_in(rng, 6), dim), (shards_of,), jnp.float32, low / len(shards), high / len(shards))
        return jnp.repeat(jnp.exp(heights), shape[dim] // shards_of).reshape((-1,) + (1,) * (len(shape) - dim - 1))

    factor_of = one(*shards[0])
    for cut in shards[1:]:
        factor_of = factor_of * one(*cut)
    return factor_of


def noise(rng, extent, width, most, cuts=(), kind=jnp.bfloat16):
    level = block_scale(rng, extent, cuts, -0.22, 0.18) if cuts else 1.0
    result = jax.random.normal(rng, extent, jnp.float32) * width * level
    return jnp.minimum(jnp.maximum(result, -most), most).astype(kind)


def setup_inputs(seed: int = 0) -> dict:
    arg_keys = jax.random.split(jax.random.key(seed), 27)
    return {
        "image_codes": place_ends(jax.random.randint(arg_keys[0], (MICRO, IMAGES, S), 0, V), jax.random.fold_in(arg_keys[0], 1), 0, V - 1).astype(jnp.int32),
        "masked": draw_masked(jax.random.fold_in(arg_keys[26], 71), 0),
        "null_caption": place_ends((jax.random.randint(arg_keys[2], (MICRO, IMAGES), 0, 4) < 1).astype(jnp.int32), jax.random.fold_in(arg_keys[2], 1), 0, 1),
        "captions": noise(arg_keys[3], (MICRO, IMAGES, TEXT, TD), 1.0, 6.0, ((1, 16),)),
        "step_count": jax.random.randint(arg_keys[4], (1,), 2, 21).astype(jnp.int32),
        "code_table": noise(arg_keys[5], (V, D), (2.0 / D ** 0.5), 0.625, ((0, 32),), jnp.float32),
        "table_first": noise(arg_keys[6], (V, D), (0.0011 / PARAMS ** 0.5), 1.6689300537109375e-06, ((0, 32),), jnp.float32),
        "table_second": jnp.clip(jnp.exp(math.log(8.643485029818411e-15) - 2.7725887 * jax.random.uniform(arg_keys[7], (V, D), jnp.float32) ** block_scale(arg_keys[7], (V, D), ((0, 32),), -0.2, 0.2)), 5.402178143636507e-16, 8.643485029818411e-15),
        "vectors": draw_vectors(jax.random.fold_in(arg_keys[26], 71), 0),
        "vectors_first": noise(arg_keys[9], (S + 9, D), (0.0044 / PARAMS ** 0.5), 6.67572021484375e-06, (), jnp.float32),
        "vectors_second": jnp.clip(jnp.exp(jax.random.uniform(arg_keys[10], (S + 9, D), jnp.float32, math.log(8.643485029818411e-15), math.log(1.3829576047709458e-13))), 8.643485029818411e-15, 1.3829576047709458e-13),
        "projections": noise(arg_keys[11], (4, D, D), D ** -0.5, 0.125, ((1, 16), (2, 2)), jnp.float32),
        "projections_first": noise(arg_keys[12], (4, D, D), (0.0011 / PARAMS ** 0.5), 1.6689300537109375e-06, ((1, 16), (2, 2)), jnp.float32),
        "projections_second": jnp.clip(jnp.exp(math.log(8.643485029818411e-15) - 2.7725887 * jax.random.uniform(arg_keys[13], (4, D, D), jnp.float32) ** block_scale(arg_keys[13], (4, D, D), ((1, 16), (2, 2)), -0.2, 0.2)), 5.402178143636507e-16, 8.643485029818411e-15),
        "text_maps": noise(arg_keys[14], (2, TD, D), TD ** -0.5, 0.09375, ((1, 16), (2, 2)), jnp.float32),
        "text_maps_first": noise(arg_keys[15], (2, TD, D), (0.0011 / PARAMS ** 0.5), 1.6689300537109375e-06, ((1, 16), (2, 2)), jnp.float32),
        "text_maps_second": jnp.clip(jnp.exp(math.log(8.643485029818411e-15) - 2.7725887 * jax.random.uniform(arg_keys[16], (2, TD, D), jnp.float32) ** block_scale(arg_keys[16], (2, TD, D), ((1, 16), (2, 2)), -0.2, 0.2)), 5.402178143636507e-16, 8.643485029818411e-15),
        "out_maps": noise(arg_keys[17], (2, D, D), (D // 8) ** -0.5, 0.375, ((1, 32),), jnp.float32),
        "out_maps_first": noise(arg_keys[18], (2, D, D), (0.0011 / PARAMS ** 0.5), 1.6689300537109375e-06, ((1, 32),), jnp.float32),
        "out_maps_second": jnp.clip(jnp.exp(math.log(8.643485029818411e-15) - 2.7725887 * jax.random.uniform(arg_keys[19], (2, D, D), jnp.float32) ** block_scale(arg_keys[19], (2, D, D), ((1, 32),), -0.2, 0.2)), 5.402178143636507e-16, 8.643485029818411e-15),
        "expand": noise(arg_keys[20], (D, FF), D ** -0.5, 0.125, ((0, 16), (1, 2)), jnp.float32),
        "expand_first": noise(arg_keys[21], (D, FF), (0.0011 / PARAMS ** 0.5), 1.6689300537109375e-06, ((0, 16), (1, 2)), jnp.float32),
        "expand_second": jnp.clip(jnp.exp(math.log(8.643485029818411e-15) - 2.7725887 * jax.random.uniform(arg_keys[22], (D, FF), jnp.float32) ** block_scale(arg_keys[22], (D, FF), ((0, 16), (1, 2)), -0.2, 0.2)), 5.402178143636507e-16, 8.643485029818411e-15),
        "contract": noise(arg_keys[23], (FF, D), FF ** -0.5, 0.0625, ((0, 32),), jnp.float32),
        "contract_first": noise(arg_keys[24], (FF, D), (0.0011 / PARAMS ** 0.5), 1.6689300537109375e-06, ((0, 32),), jnp.float32),
        "contract_second": jnp.clip(jnp.exp(math.log(8.643485029818411e-15) - 2.7725887 * jax.random.uniform(arg_keys[25], (FF, D), jnp.float32) ** block_scale(arg_keys[25], (FF, D), ((0, 32),), -0.2, 0.2)), 5.402178143636507e-16, 8.643485029818411e-15),
    }


@jax.custom_vjp
def low(v):
    return lax.optimization_barrier(v.astype(jnp.bfloat16)).astype(jnp.float32)

@jax.custom_vjp
def low_back(v):
    return v

def low_keep(v):
    return (low(v), None)

def low_pass(kept, grad):
    return (grad,)

def back_keep(v):
    return (v, None)

def back_low(kept, grad):
    return (low(grad),)
low.defvjp(low_keep, low_pass)
low_back.defvjp(back_keep, back_low)
HIGH = lax.Precision.HIGHEST
EPS_NORM = 1e-05
CLIP = 0.01
BETA_ONE = 0.9
BETA_TWO = 0.999
ADAM_EPS = 1e-08
DECAY = 0.01
RATE_MATRIX = 0.02
RATE_VECTOR = 0.2

def rounded(value):
    return low_back(low(value))

def layer_norm(inputs, gain, bias):
    average = lax.optimization_barrier(jnp.mean(inputs, -1, keepdims=True))
    centred = inputs - average
    spread = lax.optimization_barrier(jnp.mean(centred * centred, -1, keepdims=True))
    return centred * lax.rsqrt(spread + EPS_NORM) * gain + bias

def split_heads(inputs):
    return inputs.reshape(inputs.shape[0], inputs.shape[1], HEADS, HD)

def attend(queries, key_rows, value_rows):
    scores = low_back(jnp.einsum('bqhe,bkhe->bhqk', split_heads(queries), split_heads(key_rows), precision=HIGH) * HD ** (-0.5))
    attn_probs = low(jax.nn.softmax(scores, axis=-1))
    mixed = jnp.einsum('bhqk,bkhe->bqhe', attn_probs, split_heads(value_rows), precision=HIGH)
    return rounded(mixed.reshape(queries.shape))

def project(inputs, matrix):
    return jnp.einsum('bsd,de->bse', inputs, matrix, precision=HIGH)

def micro_loss(lowered, vectors, codes, masked, keep_image, caption_values):
    code_low, proj_low, text_low, out_low, expand_low, contract_low = lowered
    norm_rows = vectors[S + 1:]
    chosen = (masked == 1)[..., None]
    x_zero = jnp.where(chosen, vectors[S], code_low[codes]) + vectors[:S]
    a_one = low(layer_norm(x_zero, norm_rows[0], norm_rows[1]))
    attn_one = attend(rounded(project(a_one, proj_low[0])), rounded(project(a_one, proj_low[1])), rounded(project(a_one, proj_low[2])))
    x_one = x_zero + low_back(project(attn_one, out_low[0]))
    a_two = low(layer_norm(x_one, norm_rows[2], norm_rows[3]))
    attn_two = attend(rounded(project(a_two, proj_low[3])), rounded(project(caption_values, text_low[0])), rounded(project(caption_values, text_low[1])))
    x_two = x_one + low_back(keep_image[:, None, None] * project(attn_two, out_low[1]))
    a_three = low(layer_norm(x_two, norm_rows[4], norm_rows[5]))
    preact = low_back(project(a_three, expand_low))
    hidden = low(jax.nn.gelu(preact, approximate=True))
    x_three = x_two + low_back(project(hidden, contract_low))
    a_four = low(layer_norm(x_three, norm_rows[6], norm_rows[7]))
    logits = low_back(jnp.einsum('bsd,vd->bsv', a_four, code_low, precision=HIGH))
    logsum = jax.nn.logsumexp(logits, axis=-1)
    target = jnp.take_along_axis(logits, codes[..., None], axis=-1)[..., 0]
    return jnp.sum(masked.astype(jnp.float32) * (logsum - target))

def adamw(master, first, second, grad, rate, decay, fix_one, fix_two):
    first_new = BETA_ONE * first + (1.0 - BETA_ONE) * grad
    second_new = BETA_TWO * second + (1.0 - BETA_TWO) * grad * grad
    update = first_new / fix_one / (jnp.sqrt(second_new / fix_two) + ADAM_EPS)
    return (master - rate * (update + decay * master), first_new, second_new)

def reference(image_codes, masked, null_caption, captions, step_count, code_table, table_first, table_second, vectors, vectors_first, vectors_second, projections, projections_first, projections_second, text_maps, text_maps_first, text_maps_second, out_maps, out_maps_first, out_maps_second, expand, expand_first, expand_second, contract, contract_first, contract_second):
    mask_total = jnp.sum(masked).astype(jnp.float32)
    masters = (code_table, vectors, projections, text_maps, out_maps, expand, contract)
    caption_values = captions.astype(jnp.float32)
    keep_all = 1.0 - null_caption.astype(jnp.float32)

    def total_loss(params):
        lowered = (low(params[0]), low(params[2]), low(params[3]), low(params[4]), low(params[5]), low(params[6]))
        loss_sum = jnp.zeros((), jnp.float32)
        for micro in range(MICRO):
            loss_sum = loss_sum + micro_loss(lowered, params[1], image_codes[micro], masked[micro], keep_all[micro], caption_values[micro])
        return loss_sum / mask_total
    loss_value, pull = jax.vjp(total_loss, masters)
    gradients = pull(jnp.ones_like(loss_value))[0]
    grad_norm = jnp.sqrt(sum((jnp.sum(piece * piece) for piece in gradients)))
    clip_scale = CLIP / jnp.maximum(grad_norm, CLIP)
    count_step = step_count[0].astype(jnp.float32)
    fix_one = 1.0 - BETA_ONE ** count_step
    fix_two = 1.0 - BETA_TWO ** count_step
    states = ((code_table, table_first, table_second), (vectors, vectors_first, vectors_second), (projections, projections_first, projections_second), (text_maps, text_maps_first, text_maps_second), (out_maps, out_maps_first, out_maps_second), (expand, expand_first, expand_second), (contract, contract_first, contract_second))
    updated = []
    for position in range(7):
        state = states[position]
        rate = RATE_VECTOR if position == 1 else RATE_MATRIX
        decay = 0.0 if position == 1 else DECAY
        updated.extend(adamw(state[0], state[1], state[2], gradients[position] * clip_scale, rate, decay, fix_one, fix_two))
    return (loss_value, grad_norm, updated[0], updated[1], updated[2], updated[3], updated[4], updated[5], updated[6], updated[7], updated[8], updated[9], updated[10], updated[11], updated[12], updated[13], updated[14], updated[15], updated[16], updated[17], updated[18], updated[19], updated[20])
```

```python
from functools import partial

import jax
import jax.numpy as jnp
from jax import lax
from jax.experimental import pallas as pl
from jax.experimental.pallas import tpu as pltpu
from jax.sharding import Mesh, PartitionSpec as P

HD = 128
EPS_NORM = 1e-05
CLIP = 0.01
BETA_ONE = 0.9
BETA_TWO = 0.999
ADAM_EPS = 1e-08
DECAY = 0.01
RATE_MATRIX = 0.02
RATE_VECTOR = 0.2
SCALE = HD ** (-0.5)
F32 = jnp.float32
BF16 = jnp.bfloat16
WIRE = jnp.bfloat16

AX, BX, EX, DX, CX = "a", "b", "e", "d", "c"
DP = (AX, BX, EX, DX)
QX = (BX, EX)
MX = (AX, DX)
SWAP = [(0, 1), (1, 0)]
MESH = pl.DeviceIdType.MESH


def dot(x, y, dims):
    return lax.dot_general(x, y, (dims, ((), ())), preferred_element_type=F32)


def nn(x, y):
    return dot(x, y, ((1,), (0,)))


def nt(x, y):
    return dot(x, y, ((1,), (1,)))


def tn(x, y):
    return dot(x, y, ((0,), (0,)))


def place(b, e, c):
    return (b * 2 + e) * 2 + c


def greet(peers):
    barrier = pltpu.get_barrier_semaphore()
    for peer in peers:
        pl.semaphore_signal(barrier, inc=1, device_id=peer, device_id_type=MESH)
    pl.semaphore_wait(barrier, len(peers))


def gather_kernel(x_ref, o_ref, local, send, recv):
    b, e, c = lax.axis_index(BX), lax.axis_index(EX), lax.axis_index(CX)
    to_b, to_e, to_c = {BX: 1 - b}, {EX: 1 - e}, {CX: 1 - c}
    greet((to_b, to_e, to_c))
    me, beside, across, far = (
        place(b, e, c),
        place(b, 1 - e, c),
        place(1 - b, e, c),
        place(1 - b, 1 - e, c),
    )

    def copy(number, source, target, peer):
        made = pltpu.make_async_remote_copy(
            src_ref=source,
            dst_ref=target,
            send_sem=send.at[number],
            recv_sem=recv.at[number],
            device_id=peer,
            device_id_type=MESH,
        )
        made.start()
        return made

    own = pltpu.make_async_copy(x_ref, o_ref.at[me], local)
    e_first = copy(0, x_ref.at[0], o_ref.at[me, 0], to_e)
    b_first = copy(1, x_ref.at[1], o_ref.at[me, 1], to_b)
    e_second = copy(2, x_ref.at[1], o_ref.at[me, 1], to_e)
    b_second = copy(3, x_ref.at[0], o_ref.at[me, 0], to_b)
    started = [copy(4, x_ref, o_ref.at[me], to_c)]
    own.start()
    e_first.wait_recv()
    block = o_ref.at[beside, 0]
    b_third = copy(5, block, block, to_b)
    started.append(copy(6, block, block, to_c))
    b_first.wait_recv()
    block = o_ref.at[across, 1]
    e_third = copy(7, block, block, to_e)
    started.append(copy(8, block, block, to_c))
    e_second.wait_recv()
    block = o_ref.at[beside, 1]
    started.append(copy(9, block, block, to_c))
    b_second.wait_recv()
    block = o_ref.at[across, 0]
    started.append(copy(10, block, block, to_c))
    b_third.wait_recv()
    block = o_ref.at[far, 0]
    started.append(copy(11, block, block, to_c))
    e_third.wait_recv()
    block = o_ref.at[far, 1]
    started.append(copy(12, block, block, to_c))
    own.wait()
    for made in (e_first, b_first, e_second, b_second, b_third, e_third):
        made.wait_send()
    for made in started:
        made.wait()


def gather_eight(x, number, cost):
    return pl.pallas_call(
        gather_kernel,
        out_shape=jax.ShapeDtypeStruct((8,) + x.shape, x.dtype),
        in_specs=[pl.BlockSpec(memory_space=pl.ANY)],
        out_specs=pl.BlockSpec(memory_space=pl.ANY),
        scratch_shapes=[
            pltpu.SemaphoreType.DMA,
            pltpu.SemaphoreType.DMA((13,)),
            pltpu.SemaphoreType.DMA((13,)),
        ],
        compiler_params=pltpu.CompilerParams(collective_id=number, has_side_effects=True),
        cost_estimate=pl.CostEstimate(flops=0, bytes_accessed=cost, transcendentals=0),
    )(x)


def scatter_kernel(p_ref, o_ref, paired, held, from_b, from_e, last, send, recv):
    b, e, c = lax.axis_index(BX), lax.axis_index(EX), lax.axis_index(CX)
    to_b, to_e, to_c = {BX: 1 - b}, {EX: 1 - e}, {CX: 1 - c}
    greet((to_b, to_e, to_c))
    order = ((1 - b, 1 - e), (1 - b, e), (b, 1 - e), (b, e))

    def copy(number, source, target, peer):
        made = pltpu.make_async_remote_copy(
            src_ref=source,
            dst_ref=target,
            send_sem=send.at[number],
            recv_sem=recv.at[number],
            device_id=peer,
            device_id_type=MESH,
        )
        made.start()
        return made

    pairs = [
        copy(k, p_ref.at[place(bb, ee, 1 - c)], paired.at[k], to_c)
        for k, (bb, ee) in enumerate(order)
    ]
    pairs[0].wait_recv()
    held[0] = p_ref[place(1 - b, 1 - e, c)] + paired[0]
    b_first = copy(4, held.at[0, 0], from_b.at[0], to_b)
    e_first = copy(5, held.at[0, 1], from_e.at[0], to_e)
    pairs[1].wait_recv()
    held[1] = p_ref[place(1 - b, e, c)] + paired[1]
    b_second = copy(6, held.at[1, 0], from_b.at[1], to_b)
    pairs[2].wait_recv()
    held[2] = p_ref[place(b, 1 - e, c)] + paired[2]
    e_second = copy(7, held.at[2, 1], from_e.at[1], to_e)
    pairs[3].wait_recv()
    o_ref[...] = p_ref[place(b, e, c)] + paired[3]
    b_first.wait_recv()
    held[2, 0] = held[2, 0] + from_b[0]
    e_third = copy(8, held.at[2, 0], last.at[0], to_e)
    e_first.wait_recv()
    held[1, 1] = held[1, 1] + from_e[0]
    b_third = copy(9, held.at[1, 1], last.at[1], to_b)
    b_second.wait_recv()
    o_ref[0] = o_ref[0] + from_b[1]
    e_second.wait_recv()
    o_ref[1] = o_ref[1] + from_e[1]
    e_third.wait_recv()
    o_ref[0] = o_ref[0] + last[0]
    b_third.wait_recv()
    o_ref[1] = o_ref[1] + last[1]
    for made in pairs + [b_first, e_first, b_second, e_second, b_third, e_third]:
        made.wait_send()


def scatter_eight(parts, number, cost):
    shape = parts.shape[1:]
    half = shape[1:]
    kind = parts.dtype
    return pl.pallas_call(
        scatter_kernel,
        out_shape=jax.ShapeDtypeStruct(shape, kind),
        in_specs=[pl.BlockSpec(memory_space=pltpu.VMEM)],
        out_specs=pl.BlockSpec(memory_space=pltpu.VMEM),
        scratch_shapes=[
            pltpu.VMEM((4,) + shape, kind),
            pltpu.VMEM((3,) + shape, kind),
            pltpu.VMEM((2,) + half, kind),
            pltpu.VMEM((2,) + half, kind),
            pltpu.VMEM((2,) + half, kind),
            pltpu.SemaphoreType.DMA((10,)),
            pltpu.SemaphoreType.DMA((10,)),
        ],
        compiler_params=pltpu.CompilerParams(
            collective_id=number, has_side_effects=True, vmem_limit_bytes=40 << 20
        ),
        cost_estimate=pl.CostEstimate(flops=0, bytes_accessed=cost, transcendentals=0),
    )(parts)


def spread(rows, number):
    count, width = rows.shape
    full = gather_eight(rows.reshape(2, count // 2, width), number, 80_000_000)
    return full.reshape(8 * count, width)


def collect(parts, number):
    count, width = parts.shape
    part = scatter_eight(parts.reshape(8, 2, count // 16, width), number, 150_000_000)
    return part.reshape(count // 8, width)


def share_gather(block):
    a, d, extent = lax.axis_index(AX), lax.axis_index(DX), lax.axis_size(DX)
    other = lax.ppermute(block, AX, SWAP)
    full = jnp.zeros((2, extent) + block.shape, block.dtype)
    zeros = (0,) * block.ndim

    def put(full, piece, row, column):
        return lax.dynamic_update_slice(full, piece[None, None], (row, column) + zeros)

    full = put(full, block, a, d)
    full = put(full, other, 1 - a, d)
    for step in range(1, extent):
        ring = [(k, (k + step) % extent) for k in range(extent)]
        column = lax.rem(d + extent - step, extent)
        full = put(full, lax.ppermute(block, DX, ring), a, column)
        full = put(full, lax.ppermute(other, DX, ring), 1 - a, column)
    return full


def share_scatter(grad):
    a, d, extent = lax.axis_index(AX), lax.axis_index(DX), lax.axis_size(DX)

    def column(k):
        return lax.dynamic_index_in_dim(grad, k, 1, False)

    total = column(d)
    for step in range(1, extent):
        ring = [(k, (k + step) % extent) for k in range(extent)]
        piece = column(lax.rem(d + step, extent)).astype(WIRE)
        total = total + lax.ppermute(piece, DX, ring).astype(F32)
    piece = lax.dynamic_index_in_dim(total, 1 - a, 0, False).astype(WIRE)
    return lax.dynamic_index_in_dim(total, a, 0, False) + lax.ppermute(piece, AX, SWAP).astype(F32)


def exchange(pieces):
    q = lax.axis_index(QX)
    zeros = (0,) * (pieces.ndim - 1)
    full = jnp.zeros_like(pieces)

    def take(k):
        return lax.dynamic_index_in_dim(pieces, k, 0, False)

    full = lax.dynamic_update_slice(full, take(q)[None], (q,) + zeros)
    for step in (1, 2, 3):
        there = jnp.bitwise_xor(q, step)
        moved = lax.ppermute(take(there), QX, [(k, k ^ step) for k in range(4)])
        full = lax.dynamic_update_slice(full, moved[None], (there,) + zeros)
    return full


def layer_norm(inputs, gain, bias):
    average = jnp.mean(inputs, -1, keepdims=True)
    centred = inputs - average
    factor = lax.rsqrt(jnp.mean(centred * centred, -1, keepdims=True) + EPS_NORM)
    normed = centred * factor
    return (normed * gain + bias).astype(BF16), (normed, factor)


def norm_back(upstream, saved, gain):
    normed, factor = saved
    inner = upstream * gain
    back = factor * (
        inner
        - jnp.mean(inner, -1, keepdims=True)
        - normed * jnp.mean(inner * normed, -1, keepdims=True)
    )
    return back, jnp.sum(upstream * normed, 0), jnp.sum(upstream, 0)


def heads(x, images):
    return x.reshape(images, -1, x.shape[-1] // HD, HD)


def flat(x):
    return x.reshape(x.shape[0] * x.shape[1], -1).astype(BF16)


def ein(text, x, y):
    return jnp.einsum(text, x, y, preferred_element_type=F32)


SCORE = "bqhe,bkhe->bhqk"
MIX = "bhqk,bkhe->bqhe"
TURN = "bhqk,bqhe->bkhe"


def attend(queries, keys, values):
    scores = ein(SCORE, queries, keys) * SCALE
    top = jnp.max(scores, -1, keepdims=True)
    logsum = top + jnp.log(jnp.sum(jnp.exp(scores - top), -1, keepdims=True))
    probs = jnp.exp(scores - logsum)
    return flat(ein(MIX, probs.astype(BF16), values)), probs


def attend_back(upstream, queries, keys, values, probs, images):
    grad_out = heads(upstream, images)
    grad_probs = ein(SCORE, grad_out, values)
    inner = jnp.sum(probs * grad_probs, -1, keepdims=True)
    grad_scores = (probs * (grad_probs - inner)).astype(BF16)
    return (
        flat(ein(MIX, grad_scores, keys) * SCALE),
        flat(ein(TURN, grad_scores, queries) * SCALE),
        flat(ein(TURN, probs.astype(BF16), grad_out)),
    )


def adamw(state, grad, rate, decay, fix_one, fix_two):
    master, first, second = state
    first_new = BETA_ONE * first + (1.0 - BETA_ONE) * grad
    second_new = BETA_TWO * second + (1.0 - BETA_TWO) * grad * grad
    update = first_new / fix_one / (jnp.sqrt(second_new / fix_two) + ADAM_EPS)
    return master - rate * (update + decay * master), first_new, second_new


def body(image_codes, masked, null_caption, captions, step_count, *states):
    table_state, vector_state, proj_state, text_state, out_state, expand_state, contract_state = (
        states[k : k + 3] for k in range(0, 21, 3)
    )
    a, b, e, c = (lax.axis_index(k) for k in (AX, BX, EX, CX))
    extent = lax.axis_size(DX)
    vectors = vector_state[0]
    length = vectors.shape[0] - 9
    norm_rows = vectors[length + 1 :]
    width = vectors.shape[1]

    block = table_state[0].shape[0]
    table = share_gather(table_state[0].astype(BF16)).reshape(-1, width)
    codes_here = table.shape[0]

    kinds, in_rows, half = proj_state[0].shape
    deep = kinds
    pieces = proj_state[0].astype(BF16).reshape(kinds, in_rows, 2, 4, HD)
    pieces = exchange(pieces.transpose(3, 0, 1, 2, 4).reshape(4, kinds, in_rows, 2 * HD))
    proj = share_gather(pieces).transpose(3, 0, 2, 1, 4, 5).reshape(kinds, width, 2 * HD)
    w_qkv = proj[:3].transpose(1, 0, 2).reshape(width, 6 * HD)
    w_cross = proj[3]

    out_maps = share_gather(out_state[0].astype(BF16))
    out_maps = out_maps.transpose(2, 0, 1, 3, 4).reshape(2, 2 * HD, width)

    text_rows = text_state[0].shape[1]
    pieces = text_state[0].astype(BF16).reshape(2, text_rows, 2, 4, HD)
    pieces = exchange(pieces.transpose(3, 1, 0, 2, 4).reshape(4, text_rows, 4 * HD))
    w_text = share_gather(pieces).transpose(0, 2, 1, 3, 4).reshape(-1, 4 * HD)

    hidden_width = extent * block
    pieces = expand_state[0].astype(BF16).reshape(in_rows, 2, 4, hidden_width)
    pieces = exchange(pieces.transpose(2, 0, 1, 3).reshape(4, in_rows, 2 * hidden_width))
    expand = share_gather(pieces).transpose(0, 2, 1, 3, 4).reshape(width, 2 * hidden_width)

    contract = share_gather(contract_state[0].astype(BF16)).reshape(-1, width)

    mask_total = lax.psum(jnp.sum(masked).astype(F32), DP)
    group_codes = lax.all_gather(image_codes, QX).reshape(-1)
    group_mask = lax.all_gather(masked, QX).reshape(-1)
    group_captions = lax.all_gather(captions, QX).reshape(-1, captions.shape[-1])
    images = group_codes.shape[0] // length
    chosen = lax.dynamic_index_in_dim(masked, c, 0, False).reshape(-1)[:, None] == 1
    keep = 1.0 - lax.dynamic_index_in_dim(null_caption, c, 0, False).astype(F32)
    keep_rows = jnp.repeat(keep, length)[:, None]
    own_images = keep.shape[0]

    in_half = lax.rem(group_codes, 2 * 4 * hidden_width)
    outer = in_half // block
    inside = (
        (group_codes // (2 * 4 * hidden_width) == c)
        & (lax.rem(outer // extent, 2) == e)
        & (lax.rem(outer // (2 * extent), 2) == b)
    )
    outer = (outer // (4 * extent)) * extent + lax.rem(outer, extent)
    local_code = jnp.where(inside, outer * block + lax.rem(in_half, block), -1)
    at_code = jnp.arange(codes_here)[None, :] == local_code[:, None]

    looked = collect(nn(at_code.astype(BF16), table).astype(BF16), 1).astype(F32)
    x_zero = jnp.where(chosen, vectors[length], looked)
    x_zero = x_zero + jnp.tile(vectors[:length], (own_images, 1))
    a_one, norm_one = layer_norm(x_zero, norm_rows[0], norm_rows[1])
    a_one = spread(a_one, 2)
    triple = nn(a_one, w_qkv).astype(BF16)
    queries, keys, values = (
        heads(triple[:, k : k + 2 * HD], images) for k in (0, 2 * HD, 4 * HD)
    )
    attn_one, probs_one = attend(queries, keys, values)
    x_one = x_zero + collect(nn(attn_one, out_maps[0]), 3)

    pair = nn(group_captions, w_text).astype(BF16)
    text_keys, text_values = heads(pair[:, : 2 * HD], images), heads(pair[:, 2 * HD :], images)
    a_two, norm_two = layer_norm(x_one, norm_rows[2], norm_rows[3])
    a_two = spread(a_two, 2)
    cross = heads(nn(a_two, w_cross).astype(BF16), images)
    attn_two, probs_two = attend(cross, text_keys, text_values)
    x_two = x_one + keep_rows * collect(nn(attn_two, out_maps[1]), 3)

    a_three, norm_three = layer_norm(x_two, norm_rows[4], norm_rows[5])
    a_three = spread(a_three, 2)
    preact = nn(a_three, expand)
    hidden = jax.nn.gelu(preact, approximate=True).astype(BF16)
    x_three = x_two + collect(nn(hidden, contract), 3)

    a_four, norm_four = layer_norm(x_three, norm_rows[6], norm_rows[7])
    a_four = spread(a_four, 2)
    logits = nt(a_four, table)
    target = jnp.sum(jnp.where(at_code, logits, 0.0), 1)
    top = jnp.max(logits, 1)
    total = jnp.sum(jnp.exp(logits - top[:, None]), 1)
    count = target.shape[0]
    stats = jnp.stack([top, total, target, target])
    stats = gather_eight(stats.reshape(2, 8, count // 4), 4, 20_000_000).reshape(8, 4, count)
    peak = jnp.max(stats[:, 0], 0)
    total = jnp.sum(stats[:, 1] * jnp.exp(stats[:, 0] - peak), 0)
    head_logsum = peak + jnp.log(total)
    weight = group_mask.astype(F32)
    loss_sum = jnp.sum(weight * (head_logsum - jnp.sum(stats[:, 2], 0)))

    head_probs = jnp.exp(logits - head_logsum[:, None])
    logit_grad = (head_probs - at_code.astype(F32)) * (weight / mask_total)[:, None]
    logit_grad = logit_grad.astype(BF16)
    upstream = collect(nn(logit_grad, table), 3)
    table_grad = tn(logit_grad, a_four)
    grad_three, gain_six, gain_seven = norm_back(upstream, norm_four, norm_rows[6])
    branch_three = spread(grad_three.astype(BF16), 2)
    hidden_grad = nt(branch_three, contract)
    gelu_pull = jax.vjp(partial(jax.nn.gelu, approximate=True), preact)[1]
    preact_grad = gelu_pull(hidden_grad)[0].astype(BF16)
    back = collect(nt(preact_grad, expand), 3)
    contract_grad = tn(hidden, branch_three)
    contract_shard = share_scatter(contract_grad.reshape(2, extent, block, width))
    expand_grad = tn(a_three, preact_grad).reshape(2, 4, extent, in_rows, 2 * hidden_width)
    expand_shard = exchange(share_scatter(expand_grad.transpose(0, 2, 1, 3, 4)))
    expand_shard = expand_shard.reshape(4, in_rows, 2, hidden_width).transpose(1, 2, 0, 3)
    expand_shard = expand_shard.reshape(expand_state[0].shape)

    back, gain_four, gain_five = norm_back(back, norm_three, norm_rows[4])
    grad_two = grad_three + back
    branch_two = spread(grad_two.astype(BF16) * keep_rows.astype(BF16), 2)
    attn_grad = nt(branch_two, out_maps[1]).astype(BF16)
    cross_grad, key_grad, value_grad = attend_back(
        attn_grad, cross, text_keys, text_values, probs_two, images
    )
    back = collect(nt(cross_grad, w_cross), 3)
    text_grad = tn(group_captions, jnp.concatenate([key_grad, value_grad], 1))
    text_grad = text_grad.reshape(2, 4, extent, text_rows, 4 * HD).transpose(0, 2, 1, 3, 4)
    text_shard = exchange(share_scatter(text_grad)).reshape(4, text_rows, 2, 2, HD)
    text_shard = text_shard.transpose(2, 1, 3, 0, 4).reshape(text_state[0].shape)

    back, gain_two, gain_three = norm_back(back, norm_two, norm_rows[2])
    grad_one = grad_two + back
    branch_one = spread(grad_one.astype(BF16), 2)
    attn_grad = nt(branch_one, out_maps[0]).astype(BF16)
    triple_grad = jnp.concatenate(
        attend_back(attn_grad, queries, keys, values, probs_one, images), 1
    )
    back = collect(nt(triple_grad, w_qkv), 3)
    out_grad = jnp.stack([tn(attn_one, branch_one), tn(attn_two, branch_two)])
    out_grad = out_grad.reshape(2, 2, extent, HD // extent, width).transpose(1, 2, 0, 3, 4)
    out_shard = share_scatter(out_grad)
    proj_grad = jnp.concatenate([tn(a_one, triple_grad), tn(a_two, cross_grad)], 1)
    proj_grad = proj_grad.reshape(2, 4, extent, in_rows, kinds, 2 * HD)
    proj_shard = exchange(share_scatter(proj_grad.transpose(0, 2, 1, 3, 4, 5)))
    proj_shard = proj_shard.reshape(4, in_rows, kinds, 2, HD).transpose(2, 1, 3, 0, 4)
    proj_shard = proj_shard.reshape(proj_state[0].shape)

    back, gain_zero, gain_one = norm_back(back, norm_one, norm_rows[0])
    grad_zero = grad_one + back
    unmasked = jnp.where(chosen, 0.0, grad_zero)
    high = unmasked.astype(BF16)
    low = (unmasked - high.astype(F32)).astype(BF16)
    looked_grad = spread(jnp.concatenate([high, low], 1), 5)
    looked_grad = tn(at_code.astype(BF16), looked_grad)
    table_grad = table_grad + looked_grad[:, :width] + looked_grad[:, width:]
    table_shard = share_scatter(table_grad.reshape(2, extent, block, width))

    position_grad = jnp.sum(grad_zero.reshape(own_images, length, -1), 0)
    mask_grad = jnp.sum(jnp.where(chosen, grad_zero, 0.0), 0)
    vector_grad = jnp.concatenate(
        [
            position_grad,
            jnp.stack(
                [
                    mask_grad,
                    gain_zero,
                    gain_one,
                    gain_two,
                    gain_three,
                    gain_four,
                    gain_five,
                    gain_six,
                    gain_seven,
                ]
            ),
        ],
        0,
    )
    vector_grad = lax.psum(vector_grad, DP + (CX,))
    loss_value = lax.psum(loss_sum, MX) / mask_total

    shards = (table_shard, proj_shard, text_shard, out_shard, expand_shard, contract_shard)
    squares = sum((jnp.sum(piece * piece) for piece in shards))
    grad_norm = jnp.sqrt(lax.psum(squares, DP + (CX,)) + jnp.sum(vector_grad * vector_grad))
    clip_scale = CLIP / jnp.maximum(grad_norm, CLIP)
    count_step = step_count[0].astype(F32)
    fix_one = 1.0 - BETA_ONE**count_step
    fix_two = 1.0 - BETA_TWO**count_step
    results = [loss_value, grad_norm]
    matrices = (table_state, proj_state, text_state, out_state, expand_state, contract_state)
    updated = [
        adamw(state, grad * clip_scale, RATE_MATRIX, DECAY, fix_one, fix_two)
        for state, grad in zip(matrices, shards)
    ]
    vector_new = adamw(
        vector_state, vector_grad * clip_scale, RATE_VECTOR, 0.0, fix_one, fix_two
    )
    updated.insert(1, vector_new)
    for entry in updated:
        results.extend(entry)
    return tuple(results)


def solution(mesh):
    grid = mesh.devices
    extent = grid.shape[0] // 8
    fine = Mesh(grid.reshape(2, 2, 2, extent, grid.shape[1]), (AX, BX, EX, DX, CX))
    rows = P((CX,) + DP, None)
    both = P(None, DP, CX)
    kinds = (rows, P(), both, both, P(None, (CX,) + DP, None), P(DP, CX), rows)
    states = tuple(kind for kind in kinds for _ in range(3))
    batch = P(None, DP, None)
    return jax.shard_map(
        body,
        mesh=fine,
        in_specs=(batch, batch, P(None, DP), P(None, DP, None, None), P()) + states,
        out_specs=(P(), P()) + states,
        check_vma=False,
    )
```

```python
from functools import partial

import jax
import jax.numpy as jnp
from jax import lax
from jax.experimental import pallas as pl
from jax.experimental.layout import Layout, with_layout_constraint
from jax.experimental.pallas import tpu as pltpu
from jax.sharding import Mesh, PartitionSpec as P

HD = 128
EPS_NORM = 1e-05
CLIP = 0.01
BETA_ONE = 0.9
BETA_TWO = 0.999
ADAM_EPS = 1e-08
DECAY = 0.01
RATE_MATRIX = 0.02
RATE_VECTOR = 0.2
SCALE = HD ** (-0.5)
F32 = jnp.float32
BF16 = jnp.bfloat16
WIRE = jnp.bfloat16

AX, BX, EX, DX, CX = "a", "b", "e", "d", "c"
DP = (AX, BX, EX, DX)
QX = (BX, EX)
MX = (AX, DX)
SWAP = [(0, 1), (1, 0)]
MESH = pl.DeviceIdType.MESH


def dot(x, y, dims):
    return lax.dot_general(x, y, (dims, ((), ())), preferred_element_type=F32)


def nn(x, y):
    return dot(x, y, ((1,), (0,)))


def nt(x, y):
    return dot(x, y, ((1,), (1,)))


def tn(x, y):
    return dot(x, y, ((0,), (0,)))


def place(b, e, c):
    return (b * 2 + e) * 2 + c


def greet(peers):
    barrier = pltpu.get_barrier_semaphore()
    for peer in peers:
        pl.semaphore_signal(barrier, inc=1, device_id=peer, device_id_type=MESH)
    pl.semaphore_wait(barrier, len(peers))


def gather_kernel(x_ref, o_ref, local, send, recv):
    b, e, c = lax.axis_index(BX), lax.axis_index(EX), lax.axis_index(CX)
    to_b, to_e, to_c = {BX: 1 - b}, {EX: 1 - e}, {CX: 1 - c}
    greet((to_b, to_e, to_c))
    me, beside, across, far = (
        place(b, e, c),
        place(b, 1 - e, c),
        place(1 - b, e, c),
        place(1 - b, 1 - e, c),
    )

    def copy(number, source, target, peer):
        made = pltpu.make_async_remote_copy(
            src_ref=source,
            dst_ref=target,
            send_sem=send.at[number],
            recv_sem=recv.at[number],
            device_id=peer,
            device_id_type=MESH,
        )
        made.start()
        return made

    own = pltpu.make_async_copy(x_ref, o_ref.at[me], local)
    e_first = copy(0, x_ref.at[0], o_ref.at[me, 0], to_e)
    b_first = copy(1, x_ref.at[1], o_ref.at[me, 1], to_b)
    e_second = copy(2, x_ref.at[1], o_ref.at[me, 1], to_e)
    b_second = copy(3, x_ref.at[0], o_ref.at[me, 0], to_b)
    started = [copy(4, x_ref, o_ref.at[me], to_c)]
    own.start()
    e_first.wait_recv()
    block = o_ref.at[beside, 0]
    b_third = copy(5, block, block, to_b)
    started.append(copy(6, block, block, to_c))
    b_first.wait_recv()
    block = o_ref.at[across, 1]
    e_third = copy(7, block, block, to_e)
    started.append(copy(8, block, block, to_c))
    e_second.wait_recv()
    block = o_ref.at[beside, 1]
    started.append(copy(9, block, block, to_c))
    b_second.wait_recv()
    block = o_ref.at[across, 0]
    started.append(copy(10, block, block, to_c))
    b_third.wait_recv()
    block = o_ref.at[far, 0]
    started.append(copy(11, block, block, to_c))
    e_third.wait_recv()
    block = o_ref.at[far, 1]
    started.append(copy(12, block, block, to_c))
    own.wait()
    for made in (e_first, b_first, e_second, b_second, b_third, e_third):
        made.wait_send()
    for made in started:
        made.wait()


def gather_eight(x, number, cost):
    return pl.pallas_call(
        gather_kernel,
        out_shape=jax.ShapeDtypeStruct((8,) + x.shape, x.dtype),
        in_specs=[pl.BlockSpec(memory_space=pl.ANY)],
        out_specs=pl.BlockSpec(memory_space=pl.ANY),
        scratch_shapes=[
            pltpu.SemaphoreType.DMA,
            pltpu.SemaphoreType.DMA((13,)),
            pltpu.SemaphoreType.DMA((13,)),
        ],
        compiler_params=pltpu.CompilerParams(collective_id=number, has_side_effects=True),
        cost_estimate=pl.CostEstimate(flops=0, bytes_accessed=cost, transcendentals=0),
    )(x)


def scatter_kernel(p_ref, o_ref, paired, held, from_b, from_e, last, send, recv):
    b, e, c = lax.axis_index(BX), lax.axis_index(EX), lax.axis_index(CX)
    to_b, to_e, to_c = {BX: 1 - b}, {EX: 1 - e}, {CX: 1 - c}
    greet((to_b, to_e, to_c))
    order = ((1 - b, 1 - e), (1 - b, e), (b, 1 - e), (b, e))

    def copy(number, source, target, peer):
        made = pltpu.make_async_remote_copy(
            src_ref=source,
            dst_ref=target,
            send_sem=send.at[number],
            recv_sem=recv.at[number],
            device_id=peer,
            device_id_type=MESH,
        )
        made.start()
        return made

    pairs = [
        copy(k, p_ref.at[place(bb, ee, 1 - c)], paired.at[k], to_c)
        for k, (bb, ee) in enumerate(order)
    ]
    pairs[0].wait_recv()
    held[0] = p_ref[place(1 - b, 1 - e, c)] + paired[0]
    b_first = copy(4, held.at[0, 0], from_b.at[0], to_b)
    e_first = copy(5, held.at[0, 1], from_e.at[0], to_e)
    pairs[1].wait_recv()
    held[1] = p_ref[place(1 - b, e, c)] + paired[1]
    b_second = copy(6, held.at[1, 0], from_b.at[1], to_b)
    pairs[2].wait_recv()
    held[2] = p_ref[place(b, 1 - e, c)] + paired[2]
    e_second = copy(7, held.at[2, 1], from_e.at[1], to_e)
    pairs[3].wait_recv()
    o_ref[...] = p_ref[place(b, e, c)] + paired[3]
    b_first.wait_recv()
    held[2, 0] = held[2, 0] + from_b[0]
    e_third = copy(8, held.at[2, 0], last.at[0], to_e)
    e_first.wait_recv()
    held[1, 1] = held[1, 1] + from_e[0]
    b_third = copy(9, held.at[1, 1], last.at[1], to_b)
    b_second.wait_recv()
    o_ref[0] = o_ref[0] + from_b[1]
    e_second.wait_recv()
    o_ref[1] = o_ref[1] + from_e[1]
    e_third.wait_recv()
    o_ref[0] = o_ref[0] + last[0]
    b_third.wait_recv()
    o_ref[1] = o_ref[1] + last[1]
    for made in pairs + [b_first, e_first, b_second, e_second, b_third, e_third]:
        made.wait_send()


def scatter_eight(parts, number, cost):
    shape = parts.shape[1:]
    half = shape[1:]
    kind = parts.dtype
    return pl.pallas_call(
        scatter_kernel,
        out_shape=jax.ShapeDtypeStruct(shape, kind),
        in_specs=[pl.BlockSpec(memory_space=pltpu.VMEM)],
        out_specs=pl.BlockSpec(memory_space=pltpu.VMEM),
        scratch_shapes=[
            pltpu.VMEM((4,) + shape, kind),
            pltpu.VMEM((3,) + shape, kind),
            pltpu.VMEM((2,) + half, kind),
            pltpu.VMEM((2,) + half, kind),
            pltpu.VMEM((2,) + half, kind),
            pltpu.SemaphoreType.DMA((10,)),
            pltpu.SemaphoreType.DMA((10,)),
        ],
        compiler_params=pltpu.CompilerParams(
            collective_id=number, has_side_effects=True, vmem_limit_bytes=40 << 20
        ),
        cost_estimate=pl.CostEstimate(flops=0, bytes_accessed=cost, transcendentals=0),
    )(parts)


def total_kernel(extent, x_ref, o_ref, held, sums, send, recv):
    names = (AX, BX, EX, DX, CX)
    here = dict((name, lax.axis_index(name)) for name in names)
    near = [
        {BX: lax.rem(here[BX] + k // 4, 2), EX: lax.rem(here[EX] + k // 2 % 2, 2), CX: lax.rem(here[CX] + k % 2, 2)}
        for k in range(1, 8)
    ]
    away = [
        {AX: lax.rem(here[AX] + k // extent, 2), DX: lax.rem(here[DX] + k % extent, extent)}
        for k in range(1, 2 * extent)
    ]
    greet(near + away)

    def copy(number, source, target, peer):
        made = pltpu.make_async_remote_copy(
            src_ref=source,
            dst_ref=target,
            send_sem=send.at[number],
            recv_sem=recv.at[number],
            device_id=peer,
            device_id_type=MESH,
        )
        made.start()
        return made

    first = [copy(k, x_ref, held.at[k], peer) for k, peer in enumerate(near)]
    for made in first:
        made.wait_recv()
    terms = [x_ref[...]] + [held[k] for k in range(7)]
    while len(terms) > 1:
        terms = [terms[k] + terms[k + 1] for k in range(0, len(terms), 2)]
    sums[...] = terms[0]
    mine = 7 + here[AX] * extent + here[DX]
    second = [copy(7 + k, sums, held.at[mine], peer) for k, peer in enumerate(away)]
    held[mine] = terms[0]
    for made in second:
        made.wait_recv()
    total = held[7]
    for k in range(1, 2 * extent):
        total = total + held[7 + k]
    o_ref[...] = total
    for made in first + second:
        made.wait_send()


def total_all(tile):
    extent = lax.axis_size(DX)
    peers = 6 + 2 * extent
    return pl.pallas_call(
        partial(total_kernel, extent),
        out_shape=jax.ShapeDtypeStruct(tile.shape, tile.dtype),
        in_specs=[pl.BlockSpec(memory_space=pltpu.VMEM)],
        out_specs=pl.BlockSpec(memory_space=pltpu.VMEM),
        scratch_shapes=[
            pltpu.VMEM((peers + 1,) + tile.shape, tile.dtype),
            pltpu.VMEM(tile.shape, tile.dtype),
            pltpu.SemaphoreType.DMA((peers,)),
            pltpu.SemaphoreType.DMA((peers,)),
        ],
        compiler_params=pltpu.CompilerParams(collective_id=9, has_side_effects=True),
        cost_estimate=pl.CostEstimate(flops=0, bytes_accessed=30_000_000, transcendentals=0),
    )(tile)


def spread(rows, number):
    count, width = rows.shape
    full = gather_eight(rows.reshape(2, count // 2, width), number, 80_000_000)
    return full.reshape(8 * count, width)


def collect(parts, number):
    count, width = parts.shape
    part = scatter_eight(parts.reshape(8, 2, count // 16, width), number, 150_000_000)
    return part.reshape(count // 8, width)


def after(value, *needed):
    return lax.optimization_barrier((value, needed))[0]


def plain(x):
    return with_layout_constraint(x, Layout(tuple(range(x.ndim))))


def send(block, axis, step, extent):
    ring = [(k, (k + step) % extent) for k in range(extent)]
    return plain(lax.ppermute(plain(block), axis, ring))


def own_sends(block):
    extent = lax.axis_size(DX)
    across = send(block, AX, 1, 2)
    return across, [send(block, DX, step, extent) for step in range(1, extent)]


def far_sends(across):
    extent = lax.axis_size(DX)
    return [send(across, DX, step, extent) for step in range(1, extent)]


def assemble(block, across, beside, far, a_axis, d_axis):
    a, d, extent = lax.axis_index(AX), lax.axis_index(DX), lax.axis_size(DX)
    shape = list(block.shape)
    shape[a_axis], shape[d_axis] = 2, extent
    full = jnp.zeros(shape, block.dtype)

    def put(full, piece, row, column):
        start = [0] * block.ndim
        start[a_axis], start[d_axis] = row, column
        return lax.dynamic_update_slice(full, piece, start)

    full = put(put(full, block, a, d), across, 1 - a, d)
    for step, (near_piece, far_piece) in enumerate(zip(beside, far)):
        column = lax.rem(d + extent - step - 1, extent)
        full = put(put(full, near_piece, a, column), far_piece, 1 - a, column)
    return full


def pick(array, index, axis):
    return lax.dynamic_slice_in_dim(array, index, 1, axis)


def grad_kernel(with_base, d_ref, left_ref, right_ref, *refs):
    base_ref = refs[0] if with_base else None
    keep_ref, piece_ref = refs[-2:]
    product = tn(left_ref[...], right_ref[...])
    if with_base:
        product = product + base_ref[...]

    @pl.when(pl.program_id(0) == 0)
    def _():
        keep_ref[0] = product

    @pl.when(pl.program_id(0) > 0)
    def _():
        piece_ref[0, 0] = product.astype(piece_ref.dtype)


def weight_grad(left, right, rows, wire, base=None):
    extent = lax.axis_size(DX)
    count, columns = right.shape
    lead = left.shape[1] // (rows * extent)
    if rows % 128:
        full = tn(left, right) if base is None else tn(left, right) + base
        full = full.reshape(lead, extent, rows, columns)
        split = [
            lax.dynamic_index_in_dim(full, lax.rem(lax.axis_index(DX) + s, extent), 1, False)
            for s in range(extent)
        ]
        return split[0], jnp.stack(split[1:]).astype(wire)

    def block(s, k, d):
        return k * extent + lax.rem(d[0] + s, extent)

    in_specs = [
        pl.BlockSpec((left.shape[0], rows), lambda s, k, d: (0, block(s, k, d))),
        pl.BlockSpec((count, columns), lambda s, k, d: (0, 0)),
    ]
    operands = [left, right]
    if base is not None:
        in_specs.append(pl.BlockSpec((rows, columns), lambda s, k, d: (block(s, k, d), 0)))
        operands.append(base)
    keep_spec = pl.BlockSpec(
        (1, rows, columns), lambda s, k, d: (jnp.where(s == 0, k, lead - 1), 0, 0)
    )
    piece_spec = pl.BlockSpec(
        (1, 1, rows, columns),
        lambda s, k, d: (jnp.maximum(s - 1, 0), jnp.where(s == 0, 0, k), 0, 0),
    )
    return pl.pallas_call(
        partial(grad_kernel, base is not None),
        out_shape=(
            jax.ShapeDtypeStruct((lead, rows, columns), F32),
            jax.ShapeDtypeStruct((extent - 1, lead, rows, columns), wire),
        ),
        grid_spec=pltpu.PrefetchScalarGridSpec(
            num_scalar_prefetch=1,
            grid=(extent, lead),
            in_specs=in_specs,
            out_specs=(keep_spec, piece_spec),
        ),
        compiler_params=pltpu.CompilerParams(vmem_limit_bytes=48 << 20),
        cost_estimate=pl.CostEstimate(
            flops=2 * count * left.shape[1] * columns,
            bytes_accessed=left.size * 2 + right.size * 2 + left.shape[1] * columns * 4,
            transcendentals=0,
        ),
    )(lax.axis_index(DX).reshape(1), *operands)


def product_kernel(left_ref, right_ref, out_ref):
    out_ref[...] = tn(left_ref[...], right_ref[...])


def product(left, right, rows):
    count, columns = right.shape
    return pl.pallas_call(
        product_kernel,
        out_shape=jax.ShapeDtypeStruct((left.shape[1], columns), F32),
        grid=(left.shape[1] // rows,),
        in_specs=[
            pl.BlockSpec((count, rows), lambda k: (0, k)),
            pl.BlockSpec((count, columns), lambda k: (0, 0)),
        ],
        out_specs=pl.BlockSpec((rows, columns), lambda k: (k, 0)),
        compiler_params=pltpu.CompilerParams(vmem_limit_bytes=48 << 20),
        cost_estimate=pl.CostEstimate(
            flops=2 * count * left.shape[1] * columns,
            bytes_accessed=left.size * 2 + right.size * 2 + left.shape[1] * columns * 4,
            transcendentals=0,
        ),
    )(left, right)


def d_sends(pieces):
    extent = lax.axis_size(DX)
    return [send(pieces[step - 1], DX, step, extent) for step in range(1, extent)]


def total_at(index, keep, pieces):
    total = pick(keep.reshape((2, -1) + keep.shape[1:]), index, 0)
    for piece in pieces:
        total = total + pick(piece.reshape((2, -1) + piece.shape[1:]), index, 0).astype(F32)
    return total[0]


def a_send(keep, pieces, wire):
    return send(total_at(1 - lax.axis_index(AX), keep, pieces).astype(wire), AX, 1, 2)


def a_total(keep, pieces, across):
    return total_at(lax.axis_index(AX), keep, pieces) + across.astype(F32)


def exchange(pieces):
    return plain(lax.all_to_all(plain(pieces), QX, 0, 0))


def layer_norm(inputs, gain, bias):
    average = jnp.mean(inputs, -1, keepdims=True)
    centred = inputs - average
    factor = lax.rsqrt(jnp.mean(centred * centred, -1, keepdims=True) + EPS_NORM)
    normed = centred * factor
    return (normed * gain + bias).astype(BF16), (normed, factor)


def norm_back(upstream, saved, gain):
    normed, factor = saved
    inner = upstream * gain
    back = factor * (
        inner
        - jnp.mean(inner, -1, keepdims=True)
        - normed * jnp.mean(inner * normed, -1, keepdims=True)
    )
    return back, jnp.sum(upstream * normed, 0), jnp.sum(upstream, 0)


def dot_images(x, y, x_side, y_side):
    dims = (((x_side,), (y_side,)), ((0,), (0,)))
    return lax.dot_general(x, y, dims, preferred_element_type=F32)


def heads(x, images):
    x = x.reshape(images, -1, x.shape[-1])
    return [x[..., k : k + HD] for k in range(0, x.shape[-1], HD)]


def flat(parts):
    joined = jnp.concatenate([part.astype(BF16) for part in parts], -1)
    return joined.reshape(-1, joined.shape[-1])


def attend(queries, keys, values):
    mixed, saved = [], []
    for query, key, value in zip(queries, keys, values):
        scores = dot_images(query, key, 2, 2) * SCALE
        top = jnp.max(scores, -1, keepdims=True)
        logsum = top + jnp.log(jnp.sum(jnp.exp(scores - top), -1, keepdims=True))
        probs = jnp.exp(scores - logsum)
        mixed.append(dot_images(probs.astype(BF16), value, 2, 1))
        saved.append(probs)
    return flat(mixed), saved


def attend_back(upstream, queries, keys, values, saved, images):
    grads = []
    for grad_out, query, key, value, probs in zip(
        heads(upstream, images), queries, keys, values, saved
    ):
        grad_probs = dot_images(grad_out, value, 2, 2)
        inner = jnp.sum(probs * grad_probs, -1, keepdims=True)
        grad_scores = (probs * (grad_probs - inner)).astype(BF16)
        grads.append(
            (
                dot_images(grad_scores, key, 2, 1) * SCALE,
                dot_images(grad_scores, query, 1, 1) * SCALE,
                dot_images(probs.astype(BF16), grad_out, 1, 1),
            )
        )
    return tuple(flat(parts) for parts in zip(*grads))


def adamw(state, grad, rate, decay, fix_one, fix_two):
    master, first, second = state
    first_new = BETA_ONE * first + (1.0 - BETA_ONE) * grad
    second_new = BETA_TWO * second + (1.0 - BETA_TWO) * grad * grad
    update = first_new / fix_one / (jnp.sqrt(second_new / fix_two) + ADAM_EPS)
    return master - rate * (update + decay * master), first_new, second_new


def body(image_codes, masked, null_caption, captions, step_count, *states):
    table_state, vector_state, proj_state, text_state, out_state, expand_state, contract_state = (
        states[k : k + 3] for k in range(0, 21, 3)
    )
    b, e, c = (lax.axis_index(k) for k in (BX, EX, CX))
    extent = lax.axis_size(DX)
    vectors = vector_state[0]
    length = vectors.shape[0] - 9
    norm_rows = vectors[length + 1 :]
    width = vectors.shape[1]
    block = table_state[0].shape[0]
    kinds, in_rows, half = proj_state[0].shape
    text_rows = text_state[0].shape[1]
    hidden_width = extent * block
    pair = 2 * HD

    own_images = image_codes.shape[1]
    tokens = own_images * length
    small = jnp.concatenate(
        [
            image_codes.reshape(2, -1),
            masked.reshape(2, -1),
            jnp.broadcast_to(null_caption.reshape(2, -1, 1), masked.shape).reshape(2, -1),
        ],
        1,
    )
    small = lax.dynamic_index_in_dim(small, c, 0, False)
    small = jnp.pad(small, (0, 16 * 128 - small.shape[0] % (16 * 128)))
    own_mask, own_null = small[tokens : 2 * tokens], small[2 * tokens : 3 * tokens]
    gathered = gather_eight(small.reshape(2, 8, -1), 6, 20_000_000).reshape(8, -1)
    group_codes = gathered[:, :tokens].reshape(-1)
    weight = gathered[:, tokens : 2 * tokens].reshape(-1).astype(F32)
    chosen = own_mask[:, None] == 1
    keep_rows = 1.0 - own_null[:, None].astype(F32)
    images = 8 * own_images
    group_captions = lax.all_gather(captions, QX).reshape(-1, captions.shape[-1])

    table_block = table_state[0].astype(BF16)[None, None]
    contract_block = contract_state[0].astype(BF16)[None, None]
    out_block = out_state[0].astype(BF16)[:, None, None]
    table_own = own_sends(table_block)

    pieces = proj_state[0].astype(BF16).reshape(kinds, in_rows, 2, 4, HD).transpose(3, 1, 0, 2, 4)
    proj_block = exchange(pieces.reshape(4, in_rows, kinds * pair))[None, :, None]
    proj_own = own_sends(proj_block)
    pieces = text_state[0].astype(BF16).reshape(2, text_rows, 2, 4, HD).transpose(3, 1, 0, 2, 4)
    text_block = exchange(pieces.reshape(4, text_rows, 2 * pair))[None, :, None]
    pieces = expand_state[0].astype(BF16).reshape(in_rows, 2, 4, hidden_width)
    pieces = pieces.transpose(2, 0, 1, 3).reshape(4, in_rows, 2 * hidden_width)
    expand_block = exchange(pieces)[None, :, None]
    out_block = after(out_block, table_own[0])
    out_own = own_sends(out_block)
    table_far = far_sends(table_own[0])
    table = assemble(table_block, *table_own, table_far, 0, 1).reshape(-1, width)
    codes_here = table.shape[0]

    in_half = lax.rem(group_codes, 8 * hidden_width)
    outer = in_half // block
    inside = (
        (group_codes // (8 * hidden_width) == c)
        & (lax.rem(outer // extent, 2) == e)
        & (lax.rem(outer // (2 * extent), 2) == b)
    )
    outer = (outer // (4 * extent)) * extent + lax.rem(outer, extent)
    local_code = jnp.where(inside, outer * block + lax.rem(in_half, block), -1)
    at_code = jnp.arange(codes_here)[None, :] == local_code[:, None]

    looked = collect(nn(at_code.astype(BF16), table).astype(BF16), 1).astype(F32)
    x_zero = jnp.where(chosen, vectors[length], looked)
    x_zero = x_zero + jnp.tile(vectors[:length], (own_images, 1))
    a_one, norm_one = layer_norm(x_zero, norm_rows[0], norm_rows[1])
    proj_far = far_sends(proj_own[0])
    text_block = after(text_block, proj_own[0], a_one)
    text_own = own_sends(text_block)
    a_one = spread(after(a_one, proj_own[0]), 2)
    proj = assemble(proj_block, *proj_own, proj_far, 0, 2).reshape(width, kinds * pair)
    w_qkv, w_cross = proj[:, : 3 * pair], proj[:, 3 * pair :]
    out_far = far_sends(out_own[0])
    triple = nn(a_one, after(w_qkv, out_own[0])).astype(BF16)
    queries, keys, values = (
        heads(triple[:, k : k + pair], images) for k in (0, pair, 2 * pair)
    )
    attn_one, probs_one = attend(queries, keys, values)
    out_maps = assemble(out_block, *out_own, out_far, 1, 2).reshape(2, pair, width)
    part = nn(attn_one, out_maps[0])
    expand_block = after(expand_block, part)
    expand_own = own_sends(expand_block)
    x_one = x_zero + collect(part, 3)

    a_two, norm_two = layer_norm(x_one, norm_rows[2], norm_rows[3])
    text_far = far_sends(text_own[0])
    contract_block = after(contract_block, a_two)
    contract_own = own_sends(contract_block)
    a_two = spread(after(a_two, text_own[0]), 2)
    w_text = assemble(text_block, *text_own, text_far, 0, 2).reshape(-1, 2 * pair)
    text_pair = nn(group_captions, w_text).astype(BF16)
    text_keys, text_values = heads(text_pair[:, :pair], images), heads(text_pair[:, pair:], images)
    cross = heads(nn(a_two, w_cross).astype(BF16), images)
    attn_two, probs_two = attend(cross, text_keys, text_values)
    part = nn(attn_two, out_maps[1])
    expand_far = far_sends(expand_own[0])
    x_two = x_one + keep_rows * collect(after(part, expand_own[0]), 3)

    mask_total = after(jnp.broadcast_to(jnp.sum(weight), (8, 128)), x_one)
    mask_total = mask_total + send(mask_total, AX, 1, 2)
    mask_total = (mask_total + sum(far_sends(mask_total)))[0, 0]
    a_three, norm_three = layer_norm(x_two, norm_rows[4], norm_rows[5])
    contract_far = far_sends(contract_own[0])
    a_three = spread(after(a_three, contract_own[0]), 2)
    expand = assemble(expand_block, *expand_own, expand_far, 0, 2).reshape(width, -1)
    preact = nn(a_three, expand)
    hidden = jax.nn.gelu(preact, approximate=True).astype(BF16)
    contract = assemble(contract_block, *contract_own, contract_far, 0, 1).reshape(-1, width)
    x_three = x_two + collect(nn(hidden, contract), 3)

    a_four, norm_four = layer_norm(x_three, norm_rows[6], norm_rows[7])
    a_four = spread(a_four, 2)
    logits = nt(a_four, table)
    target = jnp.sum(jnp.where(at_code, logits, 0.0), 1)
    top = jnp.max(logits, 1)
    total = jnp.sum(jnp.exp(logits - top[:, None]), 1)
    count = target.shape[0]
    stats = jnp.stack([top, total, target, target])
    stats = gather_eight(stats.reshape(2, 8, count // 4), 4, 20_000_000).reshape(8, 4, count)
    peak = jnp.max(stats[:, 0], 0)
    total = jnp.sum(stats[:, 1] * jnp.exp(stats[:, 0] - peak), 0)
    head_logsum = peak + jnp.log(total)
    loss_sum = jnp.sum(weight * (head_logsum - jnp.sum(stats[:, 2], 0)))

    head_probs = jnp.exp(logits - head_logsum[:, None])
    logit_grad = (head_probs - at_code.astype(F32)) * (weight / mask_total)[:, None]
    logit_grad = logit_grad.astype(BF16)
    upstream = collect(nn(logit_grad, table), 3)
    grad_three, gain_six, gain_seven = norm_back(upstream, norm_four, norm_rows[6])
    branch_three = spread(grad_three.astype(BF16), 2)

    contract_keep, pieces = weight_grad(hidden, branch_three, block, BF16)
    contract_pieces = d_sends(pieces)
    hidden_grad = nt(branch_three, contract)
    gelu_pull = jax.vjp(partial(jax.nn.gelu, approximate=True), preact)[1]
    preact_grad = gelu_pull(hidden_grad)[0].astype(BF16)
    expand_keep, pieces = weight_grad(a_three, preact_grad, in_rows, BF16)
    part = nt(preact_grad, expand)
    back = collect(after(part, pieces), 3)
    expand_pieces = d_sends(pieces)

    back, gain_four, gain_five = norm_back(back, norm_three, norm_rows[4])
    grad_two = grad_three + back
    branch_two = grad_two.astype(BF16) * keep_rows.astype(BF16)
    table_head = product(logit_grad, a_four, 256)
    branch_two = spread(after(branch_two, table_head), 2)
    attn_grad = nt(branch_two, out_maps[1]).astype(BF16)
    cross_grad, key_grad, value_grad = attend_back(
        attn_grad, cross, text_keys, text_values, probs_two, images
    )
    pair_grad = jnp.concatenate([key_grad, value_grad], 1)
    text_keep, text_wire = weight_grad(group_captions, pair_grad, text_rows, WIRE)
    part = nt(cross_grad, w_cross)
    contract_across = a_send(contract_keep, after(contract_pieces, part), BF16)
    back = collect(after(part, text_wire, *contract_pieces), 3)
    text_pieces = d_sends(text_wire)

    back, gain_two, gain_three = norm_back(back, norm_two, norm_rows[2])
    grad_one = grad_two + back
    expand_across = a_send(expand_keep, after(expand_pieces, grad_one), BF16)
    branch_one = spread(after(grad_one.astype(BF16), *expand_pieces), 2)
    attn_grad = nt(branch_one, out_maps[0]).astype(BF16)
    triple_grad = jnp.concatenate(
        attend_back(attn_grad, queries, keys, values, probs_one, images), 1
    )
    cross_keep, cross_wire = weight_grad(a_two, cross_grad, in_rows, WIRE)
    cross_pieces = d_sends(cross_wire)
    triple_keep, triple_wire = weight_grad(a_one, triple_grad, in_rows, WIRE)
    part = nt(triple_grad, w_qkv)
    contract_shard = a_total(contract_keep, contract_pieces, contract_across).reshape(block, width)
    text_across = a_send(text_keep, after(text_pieces, part), WIRE)
    back = collect(after(part, triple_wire, contract_shard, *text_pieces), 3)
    triple_pieces = d_sends(triple_wire)

    back, gain_zero, gain_one = norm_back(back, norm_one, norm_rows[0])
    grad_zero = grad_one + back
    looked_grad = jnp.where(chosen, 0.0, grad_zero).astype(BF16)
    expand_shard = a_total(expand_keep, expand_pieces, expand_across)
    expand_shard = exchange(expand_shard)
    cross_across = a_send(cross_keep, after(cross_pieces, grad_zero), WIRE)
    looked_grad = spread(after(looked_grad, *cross_pieces), 2)
    table_keep, table_wire = weight_grad(
        at_code.astype(BF16), looked_grad, block, BF16, table_head
    )
    table_pieces = d_sends(table_wire)
    triple_across = a_send(triple_keep, after(triple_pieces, table_keep), WIRE)
    text_shard = exchange(a_total(text_keep, text_pieces, text_across))
    out_grad = [tn(attn_one, branch_one), tn(attn_two, branch_two)]
    out_grad = plain(jnp.stack(out_grad).reshape(2, 2, extent, HD // extent, width))
    d = lax.axis_index(DX)
    out_grad = out_grad.transpose(2, 1, 0, 3, 4)
    out_wire = [
        lax.dynamic_index_in_dim(out_grad, lax.rem(d + step, extent), 0, False)
        for step in range(extent)
    ]
    out_pieces = d_sends([wire.astype(BF16) for wire in out_wire[1:]])
    out_across = a_send(out_wire[0], out_pieces, BF16)
    table_across = a_send(table_keep, table_pieces, BF16)
    triple_shard = a_total(triple_keep, triple_pieces, triple_across)
    cross_shard = a_total(cross_keep, cross_pieces, cross_across)
    proj_shard = exchange(jnp.concatenate([triple_shard, cross_shard], 2))
    out_shard = a_total(out_wire[0], out_pieces, out_across).reshape(out_state[0].shape)
    table_shard = a_total(table_keep, table_pieces, table_across).reshape(block, width)

    def by_head(shard, count):
        return jnp.stack(
            [
                jnp.concatenate(
                    [
                        shard[q, :, (kind * 2 + row) * HD : (kind * 2 + row + 1) * HD]
                        for row in range(2)
                        for q in range(4)
                    ],
                    1,
                )
                for kind in range(count)
            ]
        )

    expand_shard = jnp.concatenate(
        [
            expand_shard[q, :, row * hidden_width : (row + 1) * hidden_width]
            for row in range(2)
            for q in range(4)
        ],
        1,
    )
    text_shard = by_head(text_shard, 2)
    proj_shard = by_head(proj_shard, kinds)

    position_grad = jnp.sum(grad_zero.reshape(own_images, length, -1), 0)
    mask_grad = jnp.sum(jnp.where(chosen, grad_zero, 0.0), 0)
    gains = [gain_zero, gain_one, gain_two, gain_three, gain_four, gain_five, gain_six, gain_seven]
    vector_grad = jnp.concatenate([position_grad, jnp.stack([mask_grad] + gains)], 0)
    rows = vector_grad.shape[0]
    padded = -(-rows // 16) * 16
    vector_grad = jnp.pad(vector_grad, ((0, padded - rows), (0, 0)))
    vector_grad = after(vector_grad, table_keep)
    vector_part = scatter_eight(vector_grad.reshape(8, 2, 8, -1), 7, 40_000_000)
    vector_part = vector_part + send(vector_part, AX, 1, 2)
    if extent == 2:
        vector_part = vector_part + far_sends(vector_part)[0]
    else:
        vector_part = lax.psum(vector_part, DX)

    shards = (table_shard, proj_shard, text_shard, out_shard, expand_shard, contract_shard)
    squares = sum((jnp.sum(piece * piece) for piece in shards))
    squares = squares + jnp.sum(vector_part * vector_part) / (2 * extent)
    lanes = jnp.arange(128)[None, :]
    numbers = jnp.where(lanes == 0, squares, jnp.where(lanes == 1, loss_sum, 0.0))
    numbers = total_all(jnp.broadcast_to(numbers, (8, 128)))
    loss_value = numbers[0, 1] / 8.0 / mask_total
    grad_norm = jnp.sqrt(numbers[0, 0])
    vector_grad = gather_eight(vector_part, 8, 40_000_000).reshape(padded, width)[:rows]
    clip_scale = CLIP / jnp.maximum(grad_norm, CLIP)
    count_step = step_count[0].astype(F32)
    fix_one = 1.0 - BETA_ONE**count_step
    fix_two = 1.0 - BETA_TWO**count_step
    results = [loss_value, grad_norm]
    matrices = (table_state, proj_state, text_state, out_state, expand_state, contract_state)
    updated = [
        adamw(state, grad * clip_scale, RATE_MATRIX, DECAY, fix_one, fix_two)
        for state, grad in zip(matrices, shards)
    ]
    vector_new = adamw(
        vector_state, vector_grad * clip_scale, RATE_VECTOR, 0.0, fix_one, fix_two
    )
    updated.insert(1, vector_new)
    for entry in updated:
        results.extend(entry)
    return tuple(results)


def solution(mesh):
    grid = mesh.devices
    extent = grid.shape[0] // 8
    fine = Mesh(grid.reshape(2, 2, 2, extent, grid.shape[1]), (AX, BX, EX, DX, CX))
    rows = P((CX,) + DP, None)
    both = P(None, DP, CX)
    kinds = (rows, P(), both, both, P(None, (CX,) + DP, None), P(DP, CX), rows)
    states = tuple(kind for kind in kinds for _ in range(3))
    batch = P(None, DP, None)
    return jax.shard_map(
        body,
        mesh=fine,
        in_specs=(batch, batch, P(None, DP), P(None, DP, None, None), P()) + states,
        out_specs=(P(), P()) + states,
        check_vma=False,
    )
```

```python
from functools import partial

import jax
import jax.numpy as jnp
from jax import lax
from jax.experimental import pallas as pl
from jax.experimental.layout import Layout, with_layout_constraint
from jax.experimental.pallas import tpu as pltpu
from jax.sharding import Mesh, PartitionSpec as P

HD = 128
EPS_NORM = 1e-05
CLIP = 0.01
BETA_ONE = 0.9
BETA_TWO = 0.999
ADAM_EPS = 1e-08
DECAY = 0.01
RATE_MATRIX = 0.02
RATE_VECTOR = 0.2
SCALE = HD ** (-0.5)
F32 = jnp.float32
BF16 = jnp.bfloat16
WIRE = jnp.bfloat16

AX, BX, EX, DX, CX = "a", "b", "e", "d", "c"
DP = (AX, BX, EX, DX)
QX = (BX, EX)
MX = (AX, DX)
SWAP = [(0, 1), (1, 0)]
MESH = pl.DeviceIdType.MESH


def dot(x, y, dims):
    return lax.dot_general(x, y, (dims, ((), ())), preferred_element_type=F32)


def nn(x, y):
    return dot(x, y, ((1,), (0,)))


def nt(x, y):
    return dot(x, y, ((1,), (1,)))


def tn(x, y):
    return dot(x, y, ((0,), (0,)))


SHARE, RING, SWAP, EXCHANGE = range(4)
START, FAR, THROUGH = range(3)
GATHER, SCATTER = range(2)


class Here:
    def __init__(self, extent, send, recv, local):
        self.a, self.b, self.e, self.d, self.c = (
            lax.axis_index(name) for name in (AX, BX, EX, DX, CX)
        )
        self.extent = extent
        self.to_a, self.to_b, self.to_e, self.to_c = (
            {AX: 1 - self.a},
            {BX: 1 - self.b},
            {EX: 1 - self.e},
            {CX: 1 - self.c},
        )
        self.to_far = {BX: 1 - self.b, EX: 1 - self.e}
        self.to_d = [{DX: lax.rem(self.d + step, extent)} for step in range(1, extent)]
        self.send, self.recv, self.local = send, recv, local
        self.count = self.local_count = 0
        self.waits = []

    def greet(self, peers):
        barrier = pltpu.get_barrier_semaphore()
        for peer in peers:
            pl.semaphore_signal(barrier, inc=1, device_id=peer, device_id_type=MESH)
        pl.semaphore_wait(barrier, len(peers))

    def copy(self, source, target, peer, hold=False):
        made = pltpu.make_async_remote_copy(
            src_ref=source,
            dst_ref=target,
            send_sem=self.send.at[self.count],
            recv_sem=self.recv.at[self.count],
            device_id=peer,
            device_id_type=MESH,
        )
        self.count += 1
        made.start()
        if not hold:
            self.waits.append(made.wait_send)
        return made

    def late(self, made):
        self.waits.append(made.wait_recv)

    def keep(self, source, target):
        made = pltpu.make_async_copy(source, target, self.local.at[self.local_count])
        self.local_count += 1
        made.start()
        return made

    def finish(self):
        for wait in self.waits:
            wait()


def place(b, e, c):
    return (b * 2 + e) * 2 + c


def spot(array, mode, row, column, first, count):
    if mode == 0:
        return array.at[row, column, pl.ds(first, count)]
    if mode == 1:
        return array.at[row, pl.ds(first, count), column]
    return array.at[pl.ds(first, count), row, column]


def share_start(here, block, array, mode, first, count):
    source = block.at[pl.ds(first, count)]
    target = spot(array, mode, here.a, here.d, first, count)
    here.waits.append(here.keep(source, target).wait)
    across = here.copy(source, target, here.to_a)
    for peer in here.to_d:
        here.late(here.copy(source, target, peer))
    return across


def share_far(here, array, mode, first, count):
    block = spot(array, mode, 1 - here.a, here.d, first, count)
    for peer in here.to_d:
        here.late(here.copy(block, block, peer))


def exchange_start(here, pieces, out, width=0):
    mine = here.b * 2 + here.e
    peers = (
        (None, mine),
        (here.to_e, here.b * 2 + 1 - here.e),
        (here.to_b, (1 - here.b) * 2 + here.e),
        (here.to_far, (1 - here.b) * 2 + 1 - here.e),
    )
    started = []
    for peer, there in peers:
        if width:
            moves = []
            for k in range(pieces.shape[2] // width):
                column = pl.multiple_of((k % 2 * 4 + mine) * width, 128)
                target = out.at[k // 2, :, pl.ds(column, width)]
                moves.append((pieces.at[there, :, pl.ds(k * width, width)], target))
        else:
            moves = [(pieces.at[there], out.at[mine])]
        for source, target in moves:
            if peer is None:
                started.append(here.keep(source, target).wait)
            else:
                started.append(here.copy(source, target, peer).wait_recv)
    return started


def gather_start(here, x_ref, o_ref, cut):
    first, second = pl.ds(0, cut), pl.ds(cut, x_ref.shape[0] - cut)
    me = place(here.b, here.e, here.c)
    e_first = here.copy(x_ref.at[first], o_ref.at[me, first], here.to_e)
    b_first = here.copy(x_ref.at[second], o_ref.at[me, second], here.to_b)
    here.late(here.copy(x_ref, o_ref.at[me], here.to_c))
    e_second = here.copy(x_ref.at[second], o_ref.at[me, second], here.to_e)
    b_second = here.copy(x_ref.at[first], o_ref.at[me, first], here.to_b)
    here.waits.append(here.keep(x_ref, o_ref.at[me]).wait)
    return e_first, b_first, e_second, b_second


def gather_rest(here, o_ref, cut, started):
    first, second = pl.ds(0, cut), pl.ds(cut, o_ref.shape[1] - cut)
    e_first, b_first, e_second, b_second = started
    beside = place(here.b, 1 - here.e, here.c)
    across = place(1 - here.b, here.e, here.c)
    far = place(1 - here.b, 1 - here.e, here.c)

    def on(block, peer):
        return here.copy(block, block, peer)

    e_first.wait_recv()
    b_third = on(o_ref.at[beside, first], here.to_b)
    here.late(on(o_ref.at[beside, first], here.to_c))
    b_first.wait_recv()
    e_third = on(o_ref.at[across, second], here.to_e)
    here.late(on(o_ref.at[across, second], here.to_c))
    e_second.wait_recv()
    here.late(on(o_ref.at[beside, second], here.to_c))
    b_second.wait_recv()
    here.late(on(o_ref.at[across, first], here.to_c))
    b_third.wait_recv()
    here.late(on(o_ref.at[far, first], here.to_c))
    e_third.wait_recv()
    here.late(on(o_ref.at[far, second], here.to_c))


def scatter_start(here, p_ref, paired):
    b, e, c = here.b, here.e, here.c
    order = ((1 - b, 1 - e), (1 - b, e), (b, 1 - e), (b, e))
    return [
        here.copy(p_ref.at[place(bb, ee, 1 - c)], paired.at[k], here.to_c)
        for k, (bb, ee) in enumerate(order)
    ]


def scatter_rest(here, p_ref, o_ref, cut, pairs, paired, held, from_b, from_e, last_b, last_e):
    b, e, c = here.b, here.e, here.c
    first, second = pl.ds(0, cut), pl.ds(cut, o_ref.shape[0] - cut)
    pairs[0].wait_recv()
    held[0] = p_ref[place(1 - b, 1 - e, c)] + paired[0]
    e_first = here.copy(held.at[0, second], from_e.at[0], here.to_e, hold=True)
    b_first = here.copy(held.at[0, first], from_b.at[0], here.to_b, hold=True)
    pairs[2].wait_recv()
    held[2] = p_ref[place(b, 1 - e, c)] + paired[2]
    pairs[1].wait_recv()
    held[1] = p_ref[place(1 - b, e, c)] + paired[1]
    pairs[3].wait_recv()
    o_ref[...] = p_ref[place(b, e, c)] + paired[3]
    b_first.wait_send()
    b_second = here.copy(held.at[1, first], from_b.at[1], here.to_b)
    e_first.wait_send()
    e_second = here.copy(held.at[2, second], from_e.at[1], here.to_e)
    e_first.wait_recv()
    held[1, second] = held[1, second] + from_e[0]
    b_third = here.copy(held.at[1, second], last_b, here.to_b)
    b_first.wait_recv()
    held[2, first] = held[2, first] + from_b[0]
    e_third = here.copy(held.at[2, first], last_e, here.to_e)
    b_second.wait_recv()
    o_ref[first] = o_ref[first] + from_b[1]
    e_second.wait_recv()
    o_ref[second] = o_ref[second] + from_e[1]
    e_third.wait_recv()
    o_ref[first] = o_ref[first] + last_e[...]
    b_third.wait_recv()
    o_ref[second] = o_ref[second] + last_b[...]


def group_kernel(kind, cut, plan, extent, in_count, out_count, *refs):
    ins, outs = list(refs[:in_count]), list(refs[in_count : in_count + out_count])
    scratch = refs[in_count + out_count :]
    here = Here(extent, *scratch[:3])
    x_ref, o_ref = ins.pop(0), outs.pop(0)
    peers = [here.to_b, here.to_e, here.to_c]
    if any(entry[0] == EXCHANGE for entry in plan):
        peers.append(here.to_far)
    if any(
        entry[0] == SWAP or entry[0] == SHARE and any(do[0] != FAR for do in entry[2])
        for entry in plan
    ):
        peers.append(here.to_a)
    if any(entry[0] in (SHARE, RING) for entry in plan):
        peers.extend(here.to_d)
    here.greet(peers)
    if kind == GATHER:
        started = gather_start(here, x_ref, o_ref, cut)
    else:
        started = scatter_start(here, x_ref, scratch[3])
    through = []
    for entry in plan:
        source, out = ins.pop(0), outs.pop(0)
        if entry[3]:
            ins.pop(0)
        if entry[0] == SHARE:
            for action, first, count in entry[2]:
                if action == FAR:
                    share_far(here, out, entry[1], first, count)
                else:
                    across = share_start(here, source, out, entry[1], first, count)
                    if action == THROUGH:
                        through.append((across, out, entry[1], first, count))
                    else:
                        here.late(across)
        elif entry[0] == RING:
            lead = source.shape[1]
            for half in entry[2]:
                row, count = {0: (1 - here.a, lead // 2), 1: (here.a, lead // 2), 2: (0, lead)}[half]
                for step, peer in enumerate(here.to_d):
                    part = pl.ds(row * count, count)
                    here.late(here.copy(source.at[step, part], out.at[step, part], peer))
        elif entry[0] == SWAP:
            for first, count in entry[2]:
                part = pl.ds(first, count)
                here.late(here.copy(source.at[part], out.at[part], here.to_a))
        else:
            here.waits.extend(exchange_start(here, source, out, entry[1]))
    if kind == GATHER:
        gather_rest(here, o_ref, cut, started)
    else:
        scatter_rest(here, x_ref, o_ref, cut, started, *scratch[3:])
    for across, out, mode, first, count in through:
        across.wait_recv()
        share_far(here, out, mode, first, count)
    here.finish()


def share(mode, actions, block, array=None):
    return (SHARE, mode, actions, block, array)


def ring(halves, pieces, array=None):
    return (RING, 0, halves, pieces, array)


def swap(parts, piece, array=None):
    return (SWAP, 0, parts, piece, array)


def exchange(pieces, width=0):
    return (EXCHANGE, width, (), pieces, None)


def group_call(kind, x, number, *moves, cut=2):
    extent = lax.axis_size(DX)
    if kind == GATHER:
        out = jax.ShapeDtypeStruct((8,) + x.shape, x.dtype)
        space, scratch = pl.ANY, []
        cut = x.shape[0] // cut
    else:
        shape = x.shape[1:]
        out = jax.ShapeDtypeStruct(shape, x.dtype)
        space = pltpu.VMEM
        cut = shape[0] // cut
        first, second = (cut,) + shape[1:], (shape[0] - cut,) + shape[1:]
        sizes = ((4,) + shape, (3,) + shape, (2,) + first, (2,) + second, second, first)
        scratch = [pltpu.VMEM(size, x.dtype) for size in sizes]
    operands, outs, aliases, plan, copies, locals_ = [x], [out], {}, [], 13, 2
    for what, mode, actions, source, array in moves:
        operands.append(source)
        if array is not None:
            aliases[len(operands)] = len(outs)
            operands.append(array)
            outs.append(jax.ShapeDtypeStruct(array.shape, array.dtype))
        elif what == SHARE:
            lead, block = source.shape[:1], source.shape[1:]
            full = ((2, extent) + lead, (2,) + lead + (extent,), lead + (2, extent))[mode]
            outs.append(jax.ShapeDtypeStruct(full + block, source.dtype))
        elif what == EXCHANGE and mode:
            parts = source.shape[2] // mode
            shape = (parts // 2, source.shape[1], 8 * mode)
            outs.append(jax.ShapeDtypeStruct(shape, source.dtype))
            copies += 3 * parts
            locals_ += parts
        else:
            outs.append(jax.ShapeDtypeStruct(source.shape, source.dtype))
        plan.append((what, mode, actions, array is not None))
        copies += 3 + 2 * extent * len(actions)
        locals_ += 1 + len(actions)
    anywhere = pl.BlockSpec(memory_space=pl.ANY)
    results = pl.pallas_call(
        partial(group_kernel, kind, cut, plan, extent, len(operands), len(outs)),
        out_shape=tuple(outs),
        in_specs=[pl.BlockSpec(memory_space=space)] + [anywhere] * (len(operands) - 1),
        out_specs=tuple([pl.BlockSpec(memory_space=space)] + [anywhere] * (len(outs) - 1)),
        scratch_shapes=[
            pltpu.SemaphoreType.DMA((copies,)),
            pltpu.SemaphoreType.DMA((copies,)),
            pltpu.SemaphoreType.DMA((locals_,)),
        ]
        + scratch,
        input_output_aliases=aliases,
        compiler_params=pltpu.CompilerParams(
            collective_id=number, has_side_effects=True, vmem_limit_bytes=40 << 20
        ),
        cost_estimate=pl.CostEstimate(
            flops=0, bytes_accessed=80_000_000, transcendentals=0
        ),
    )(*operands)
    return results[0] if not moves else results


def first_kernel(extent, *refs):
    small, text, table_ref, out_ref, proj_ref, text_ref, expand_ref, contract_ref = refs[:8]
    small_out, text_out, proj_block, table, outs = refs[8:13]
    text_pieces, expand_pieces, contract_block, out_block = refs[13:17]
    table_block, proj_pieces = refs[17:19]
    here = Here(extent, *refs[19:])
    peers = [here.to_b, here.to_e, here.to_c, here.to_far, here.to_a] + here.to_d
    here.greet(peers)
    units, rows = table_block.shape[:2]

    def table_unit(k):
        table_block[k] = table_ref[pl.ds(k * rows, rows)].astype(BF16)
        return share_start(here, table_block, table, 0, k, 1)

    def by_head(source, target):
        kinds = source.shape[0]
        for q in range(4):
            for kind in range(kinds):
                for row in range(2):
                    target[q, :, pl.ds((kind * 2 + row) * HD, HD)] = source[
                        kind, :, pl.ds((row * 4 + q) * HD, HD)
                    ].astype(BF16)

    across = [table_unit(0), table_unit(1), table_unit(2)]
    small_started = gather_start(here, small, small_out, small.shape[0] // 2)
    by_head(proj_ref, proj_pieces)
    here.waits.extend(exchange_start(here, proj_pieces, proj_block))
    gather_rest(here, small_out, small.shape[0] // 2, small_started)
    text_started = gather_start(here, text, text_out, text.shape[0] // 2)
    for k in range(units):
        across[k].wait_recv()
        share_far(here, table, 0, k, 1)
        if k + 3 < units:
            across.append(table_unit(k + 3))
        elif k + 3 == units:
            out_block[...] = out_ref[...].astype(BF16)
            across.append(share_start(here, out_block, outs, 2, 0, 1))
        if k == 0:
            by_head(text_ref, text_pieces)
        elif k == 1:
            gather_rest(here, text_out, text.shape[0] // 2, text_started)
            width = expand_ref.shape[1] // 8
            for q in range(4):
                for row in range(2):
                    expand_pieces[q, :, pl.ds(row * width, width)] = expand_ref[
                        :, pl.ds((row * 4 + q) * width, width)
                    ].astype(BF16)
        elif k == 2:
            for unit in range(units):
                contract_block[unit] = contract_ref[pl.ds(unit * rows, rows)].astype(BF16)
    across[units].wait_recv()
    share_far(here, outs, 2, 0, 1)
    here.finish()


def first_call(small, text, table, outs, proj, text_maps, expand, contract):
    extent = lax.axis_size(DX)
    rows, width = table.shape
    kinds, in_rows, half = proj.shape

    def like(shape, kind=BF16):
        return jax.ShapeDtypeStruct(shape, kind)

    table_shape = (4, rows // 4, width)
    proj_shape = (4, in_rows, kinds * 2 * HD)
    out_shape = [
        like((8,) + small.shape, small.dtype),
        like((8,) + text.shape),
        like(proj_shape),
        like((2, extent) + table_shape),
        like((2, 2, extent) + outs.shape[1:]),
        like((4, text_maps.shape[1], 4 * HD)),
        like((4, in_rows, expand.shape[1] // 4)),
        like(table_shape),
        like(outs.shape),
    ]
    copies = 36 + 12 * extent
    anywhere, vmem = pl.BlockSpec(memory_space=pl.ANY), pl.BlockSpec(memory_space=pltpu.VMEM)
    return pl.pallas_call(
        partial(first_kernel, extent),
        out_shape=tuple(out_shape),
        in_specs=[anywhere] * 2 + [vmem] * 6,
        out_specs=tuple([anywhere] * 5 + [vmem] * 4),
        scratch_shapes=[
            pltpu.VMEM(table_shape, BF16),
            pltpu.VMEM(proj_shape, BF16),
            pltpu.SemaphoreType.DMA((copies,)),
            pltpu.SemaphoreType.DMA((copies,)),
            pltpu.SemaphoreType.DMA((12,)),
        ],
        compiler_params=pltpu.CompilerParams(
            collective_id=1, has_side_effects=True, vmem_limit_bytes=48 << 20
        ),
    )(small, text, table, outs, proj, text_maps, expand, contract)


def last_kernel(extent, tile_ref, x_ref, total_ref, o_ref, send, recv, local, held, sums):
    here = Here(extent, send, recv, local)
    near = [
        {
            BX: lax.rem(here.b + k // 4, 2),
            EX: lax.rem(here.e + k // 2 % 2, 2),
            CX: lax.rem(here.c + k % 2, 2),
        }
        for k in range(1, 8)
    ]
    away = [
        {AX: lax.rem(here.a + k // extent, 2), DX: lax.rem(here.d + k % extent, extent)}
        for k in range(1, 2 * extent)
    ]
    here.greet(near + away)
    first = [here.copy(tile_ref, held.at[k], peer) for k, peer in enumerate(near)]
    cut = x_ref.shape[0] // 3
    started = gather_start(here, x_ref, o_ref, cut)
    for made in first:
        made.wait_recv()
    terms = [tile_ref[...]] + [held[k] for k in range(7)]
    while len(terms) > 1:
        terms = [terms[k] + terms[k + 1] for k in range(0, len(terms), 2)]
    sums[...] = terms[0]
    mine = 7 + here.a * extent + here.d
    second = [here.copy(sums, held.at[mine], peer) for peer in away]
    held[mine] = terms[0]
    gather_rest(here, o_ref, cut, started)
    for made in second:
        made.wait_recv()
    total = held[7]
    for k in range(1, 2 * extent):
        total = total + held[7 + k]
    total_ref[...] = total
    here.finish()


def last_call(tile, x):
    extent = lax.axis_size(DX)
    peers = 6 + 2 * extent
    vmem, anywhere = pl.BlockSpec(memory_space=pltpu.VMEM), pl.BlockSpec(memory_space=pl.ANY)
    return pl.pallas_call(
        partial(last_kernel, extent),
        out_shape=(
            jax.ShapeDtypeStruct(tile.shape, tile.dtype),
            jax.ShapeDtypeStruct((8,) + x.shape, x.dtype),
        ),
        in_specs=[vmem, anywhere],
        out_specs=(vmem, anywhere),
        scratch_shapes=[
            pltpu.SemaphoreType.DMA((peers + 13,)),
            pltpu.SemaphoreType.DMA((peers + 13,)),
            pltpu.SemaphoreType.DMA((1,)),
            pltpu.VMEM((peers + 1,) + tile.shape, tile.dtype),
            pltpu.VMEM(tile.shape, tile.dtype),
        ],
        compiler_params=pltpu.CompilerParams(collective_id=19, has_side_effects=True),
    )(tile, x)


def spread(rows, number, *moves, cut=2):
    count, width = rows.shape
    full = group_call(GATHER, rows, number, *moves, cut=cut)
    if moves:
        return (full[0].reshape(8 * count, width),) + tuple(full[1:])
    return full.reshape(8 * count, width)


def collect(parts, number, *moves, cut=2):
    count, width = parts.shape
    parts = parts.reshape(8, count // 8, width)
    return group_call(SCATTER, parts, number, *moves, cut=cut)


def after(value, *needed):
    return lax.optimization_barrier((value, needed))[0]


def plain(x):
    return with_layout_constraint(x, Layout(tuple(range(x.ndim))))


def send(block, axis, step, extent):
    ring = [(k, (k + step) % extent) for k in range(extent)]
    return plain(lax.ppermute(plain(block), axis, ring))


def pick(array, index, axis):
    return lax.dynamic_slice_in_dim(array, index, 1, axis)


def grad_kernel(with_base, extent, rows, d_ref, left_ref, right_ref, *refs):
    keep_ref, piece_ref = refs[-2:]
    product = tn(left_ref[...], right_ref[...])
    if with_base:
        product = product + refs[0][...]
    for k in range(keep_ref.shape[0]):
        for column in range(extent):
            start = (k * extent + column) * rows
            part = product[start : start + rows]
            step = lax.rem(column - d_ref[0] + extent, extent)

            @pl.when(step == 0)
            def _():
                keep_ref[k] = part

            @pl.when(step > 0)
            def _():
                piece_ref[step - 1, k] = part.astype(piece_ref.dtype)


def weight_grad(left, right, rows, wire, base=None):
    extent = lax.axis_size(DX)
    count, columns = right.shape
    lead = left.shape[1] // (rows * extent)
    if rows % 128:
        full = tn(left, right) if base is None else tn(left, right) + base
        full = full.reshape(lead, extent, rows, columns)
        split = [
            lax.dynamic_index_in_dim(full, lax.rem(lax.axis_index(DX) + s, extent), 1, False)
            for s in range(extent)
        ]
        return split[0], jnp.stack(split[1:]).astype(wire)

    chunk = max(1, lead // 4) if rows * extent * (lead // 4) >= 512 else max(1, 512 // (rows * extent))
    deep = chunk * extent * rows
    wide = columns if columns <= 1024 else columns // 2
    in_specs = [
        pl.BlockSpec((count, deep), lambda k, j, d: (0, k)),
        pl.BlockSpec((count, wide), lambda k, j, d: (0, j)),
    ]
    operands = [left, right]
    if base is not None:
        in_specs.append(pl.BlockSpec((deep, wide), lambda k, j, d: (k, j)))
        operands.append(base)
    return pl.pallas_call(
        partial(grad_kernel, base is not None, extent, rows),
        out_shape=(
            jax.ShapeDtypeStruct((lead, rows, columns), F32),
            jax.ShapeDtypeStruct((extent - 1, lead, rows, columns), wire),
        ),
        grid_spec=pltpu.PrefetchScalarGridSpec(
            num_scalar_prefetch=1,
            grid=(lead // chunk, columns // wide),
            in_specs=in_specs,
            out_specs=(
                pl.BlockSpec((chunk, rows, wide), lambda k, j, d: (k, 0, j)),
                pl.BlockSpec((extent - 1, chunk, rows, wide), lambda k, j, d: (0, k, 0, j)),
            ),
        ),
        compiler_params=pltpu.CompilerParams(vmem_limit_bytes=48 << 20),
        cost_estimate=pl.CostEstimate(
            flops=2 * count * left.shape[1] * columns,
            bytes_accessed=left.size * 2 + right.size * 2 + left.shape[1] * columns * 4,
            transcendentals=0,
        ),
    )(lax.axis_index(DX).reshape(1), *operands)


def product_kernel(left_ref, right_ref, out_ref):
    out_ref[...] = tn(left_ref[...], right_ref[...])


def product(left, right):
    count, columns = right.shape
    deep, wide = left.shape[1] // 2, columns // 2
    return pl.pallas_call(
        product_kernel,
        out_shape=jax.ShapeDtypeStruct((left.shape[1], columns), F32),
        grid=(2, 2),
        in_specs=[
            pl.BlockSpec((count, deep), lambda k, j: (0, k)),
            pl.BlockSpec((count, wide), lambda k, j: (0, j)),
        ],
        out_specs=pl.BlockSpec((deep, wide), lambda k, j: (k, j)),
        compiler_params=pltpu.CompilerParams(vmem_limit_bytes=48 << 20),
        cost_estimate=pl.CostEstimate(
            flops=2 * count * left.shape[1] * columns,
            bytes_accessed=left.size * 2 + right.size * 2 + left.shape[1] * columns * 4,
            transcendentals=0,
        ),
    )(left, right)


def total_at(index, keep, pieces):
    total = pick(keep.reshape((2, -1) + keep.shape[1:]), index, 0)
    for step in range(pieces.shape[0]):
        piece = pieces[step].reshape((2, -1) + pieces.shape[2:])
        total = total + pick(piece, index, 0).astype(F32)
    return total[0]


def other_half(keep, pieces, wire):
    return total_at(1 - lax.axis_index(AX), keep, pieces).astype(wire)


def own_half(keep, pieces, across):
    return total_at(lax.axis_index(AX), keep, pieces) + across.astype(F32)


def layer_norm(inputs, gain, bias):
    average = jnp.mean(inputs, -1, keepdims=True)
    centred = inputs - average
    factor = lax.rsqrt(jnp.mean(centred * centred, -1, keepdims=True) + EPS_NORM)
    normed = centred * factor
    return (normed * gain + bias).astype(BF16), (normed, factor)


def norm_back(upstream, saved, gain):
    normed, factor = saved
    inner = upstream * gain
    back = factor * (
        inner
        - jnp.mean(inner, -1, keepdims=True)
        - normed * jnp.mean(inner * normed, -1, keepdims=True)
    )
    return back, jnp.sum(upstream * normed, 0), jnp.sum(upstream, 0)


def dot_images(x, y, x_side, y_side):
    dims = (((x_side,), (y_side,)), ((0,), (0,)))
    return lax.dot_general(x, y, dims, preferred_element_type=F32)


def heads(x, images):
    x = x.reshape(images, -1, x.shape[-1])
    return [x[..., k : k + HD] for k in range(0, x.shape[-1], HD)]


def flat(parts):
    joined = jnp.concatenate([part.astype(BF16) for part in parts], -1)
    return joined.reshape(-1, joined.shape[-1])


def attend(queries, keys, values):
    mixed, saved = [], []
    for query, key, value in zip(queries, keys, values):
        scores = dot_images(query, key, 2, 2) * SCALE
        top = jnp.max(scores, -1, keepdims=True)
        logsum = top + jnp.log(jnp.sum(jnp.exp(scores - top), -1, keepdims=True))
        probs = jnp.exp(scores - logsum)
        mixed.append(dot_images(probs.astype(BF16), value, 2, 1))
        saved.append(probs)
    return flat(mixed), saved


def attend_back(upstream, queries, keys, values, saved, images):
    grads = []
    for grad_out, query, key, value, probs in zip(
        heads(upstream, images), queries, keys, values, saved
    ):
        grad_probs = dot_images(grad_out, value, 2, 2)
        inner = jnp.sum(probs * grad_probs, -1, keepdims=True)
        grad_scores = (probs * (grad_probs - inner)).astype(BF16)
        grads.append(
            (
                dot_images(grad_scores, key, 2, 1) * SCALE,
                dot_images(grad_scores, query, 1, 1) * SCALE,
                dot_images(probs.astype(BF16), grad_out, 1, 1),
            )
        )
    return tuple(flat(parts) for parts in zip(*grads))


def adamw(state, grad, rate, decay, fix_one, fix_two):
    master, first, second = state
    first_new = BETA_ONE * first + (1.0 - BETA_ONE) * grad
    second_new = BETA_TWO * second + (1.0 - BETA_TWO) * grad * grad
    update = first_new / fix_one / (jnp.sqrt(second_new / fix_two) + ADAM_EPS)
    return master - rate * (update + decay * master), first_new, second_new


def body(image_codes, masked, null_caption, captions, step_count, *states):
    table_state, vector_state, proj_state, text_state, out_state, expand_state, contract_state = (
        states[k : k + 3] for k in range(0, 21, 3)
    )
    b, e, c = (lax.axis_index(k) for k in (BX, EX, CX))
    extent = lax.axis_size(DX)
    vectors = vector_state[0]
    length = vectors.shape[0] - 9
    norm_rows = vectors[length + 1 :]
    width = vectors.shape[1]
    block = table_state[0].shape[0]
    kinds, in_rows, half = proj_state[0].shape
    text_rows = text_state[0].shape[1]
    hidden_width = extent * block
    pair = 2 * HD

    own_images = image_codes.shape[1]
    tokens = own_images * length
    small = jnp.concatenate(
        [
            image_codes.reshape(2, -1),
            masked.reshape(2, -1),
            jnp.broadcast_to(null_caption.reshape(2, -1, 1), masked.shape).reshape(2, -1),
        ],
        1,
    )
    small = lax.dynamic_index_in_dim(small, c, 0, False)
    small = jnp.pad(small, (0, -small.shape[0] % (16 * 128)))
    own_mask, own_null = small[tokens : 2 * tokens], small[2 * tokens : 3 * tokens]
    text = lax.dynamic_index_in_dim(captions, c, 0, False)
    text = text.reshape(-1, text.shape[-1])
    gathered, group_captions, proj_block, table, outs, *rest = first_call(
        small.reshape(16, -1),
        text,
        table_state[0],
        out_state[0],
        proj_state[0],
        text_state[0],
        expand_state[0],
        contract_state[0],
    )
    text_pieces, expand_pieces, contract_block, out_block = rest
    gathered = gathered.reshape(8, -1)
    group_captions = group_captions.reshape(-1, group_captions.shape[-1])
    group_codes = gathered[:, :tokens].reshape(-1)
    weight = gathered[:, tokens : 2 * tokens].reshape(-1).astype(F32)
    chosen = own_mask[:, None] == 1
    keep_rows = 1.0 - own_null[:, None].astype(F32)
    images = 8 * own_images
    table = table.reshape(-1, width)
    codes_here = table.shape[0]

    in_half = lax.rem(group_codes, 8 * hidden_width)
    outer = in_half // block
    inside = (
        (group_codes // (8 * hidden_width) == c)
        & (lax.rem(outer // extent, 2) == e)
        & (lax.rem(outer // (2 * extent), 2) == b)
    )
    outer = (outer // (4 * extent)) * extent + lax.rem(outer, extent)
    local_code = jnp.where(inside, outer * block + lax.rem(in_half, block), -1)
    at_code = jnp.arange(codes_here)[None, :] == local_code[:, None]

    part = nn(at_code.astype(BF16), table).astype(BF16)
    looked, proj, text_block = collect(
        part, 2, share(1, ((START, 0, 3),), proj_block), exchange(text_pieces), cut=4
    )
    x_zero = jnp.where(chosen, vectors[length], looked.astype(F32))
    x_zero = x_zero + jnp.tile(vectors[:length], (own_images, 1))
    a_one, norm_one = layer_norm(x_zero, norm_rows[0], norm_rows[1])
    a_one, proj, w_text, expand_block = spread(
        a_one,
        3,
        share(1, ((THROUGH, 3, 1), (FAR, 0, 3)), proj_block, proj),
        share(1, ((START, 0, 1),), text_block),
        exchange(expand_pieces),
        cut=4,
    )
    proj = proj.reshape(width, kinds * pair)
    w_qkv, w_cross = proj[:, : 3 * pair], proj[:, 3 * pair :]
    triple = nn(a_one, w_qkv).astype(BF16)
    queries, keys, values = (
        heads(triple[:, k : k + pair], images) for k in (0, pair, 2 * pair)
    )
    attn_one, probs_one = attend(queries, keys, values)
    part = nn(attn_one, outs[0].reshape(pair, width))
    back, w_text, outs = collect(
        part,
        4,
        share(1, ((START, 1, 3), (FAR, 0, 1)), text_block, w_text),
        share(2, ((START, 1, 1),), out_block, outs),
        cut=4,
    )
    x_one = x_zero + back

    a_two, norm_two = layer_norm(x_one, norm_rows[2], norm_rows[3])
    a_two, w_text, outs, expand = spread(
        a_two,
        5,
        share(1, ((FAR, 1, 3),), text_block, w_text),
        share(2, ((FAR, 1, 1),), out_block, outs),
        share(1, ((START, 0, 2),), expand_block),
        cut=4,
    )
    w_text = w_text.reshape(-1, 2 * pair)
    out_maps = outs.reshape(2, pair, width)
    text_pair = nn(group_captions, w_text).astype(BF16)
    text_keys, text_values = heads(text_pair[:, :pair], images), heads(text_pair[:, pair:], images)
    cross = heads(nn(a_two, w_cross).astype(BF16), images)
    attn_two, probs_two = attend(cross, text_keys, text_values)
    part = nn(attn_two, out_maps[1])
    back, expand, contract = collect(
        part,
        6,
        share(1, ((START, 2, 2), (FAR, 0, 2)), expand_block, expand),
        share(0, ((START, 0, 2),), contract_block),
        cut=4,
    )
    x_two = x_one + keep_rows * back

    a_three, norm_three = layer_norm(x_two, norm_rows[4], norm_rows[5])
    a_three, expand, contract = spread(
        a_three,
        7,
        share(1, ((FAR, 2, 2),), expand_block, expand),
        share(0, ((FAR, 0, 2), (THROUGH, 2, 1), (THROUGH, 3, 1)), contract_block, contract),
        cut=4,
    )
    expand, contract = expand.reshape(width, -1), contract.reshape(-1, width)
    mask_total = after(jnp.broadcast_to(jnp.sum(weight), (8, 128)), x_two)
    mask_total = mask_total + send(mask_total, AX, 1, 2)
    mask_total = mask_total + sum(send(mask_total, DX, step, extent) for step in range(1, extent))
    mask_total = mask_total[0, 0]
    preact = nn(a_three, expand)
    hidden = jax.nn.gelu(preact, approximate=True).astype(BF16)
    x_three = x_two + collect(nn(hidden, contract), 8)

    a_four, norm_four = layer_norm(x_three, norm_rows[6], norm_rows[7])
    a_four = spread(a_four, 9)
    logits = nt(a_four, table)
    target = jnp.sum(jnp.where(at_code, logits, 0.0), 1)
    top = jnp.max(logits, 1)
    total = jnp.sum(jnp.exp(logits - top[:, None]), 1)
    count = target.shape[0]
    stats = jnp.stack([top, total, target, target])
    stats = group_call(GATHER, stats.reshape(16, count // 4), 10).reshape(8, 4, count)
    peak = jnp.max(stats[:, 0], 0)
    total = jnp.sum(stats[:, 1] * jnp.exp(stats[:, 0] - peak), 0)
    head_logsum = peak + jnp.log(total)
    loss_sum = jnp.sum(weight * (head_logsum - jnp.sum(stats[:, 2], 0)))

    head_probs = jnp.exp(logits - head_logsum[:, None])
    logit_grad = (head_probs - at_code.astype(F32)) * (weight / mask_total)[:, None]
    logit_grad = logit_grad.astype(BF16)
    upstream = collect(nn(logit_grad, table), 8)
    grad_three, gain_six, gain_seven = norm_back(upstream, norm_four, norm_rows[6])
    branch_three = spread(grad_three.astype(BF16), 9)

    contract_keep, contract_wire = weight_grad(hidden, branch_three, block, BF16)
    hidden_grad = nt(branch_three, contract)
    gelu_pull = jax.vjp(partial(jax.nn.gelu, approximate=True), preact)[1]
    preact_grad = gelu_pull(hidden_grad)[0].astype(BF16)
    expand_keep, expand_wire = weight_grad(a_three, preact_grad, in_rows, BF16)
    part = nt(preact_grad, expand)
    back, contract_came = collect(part, 11, ring((0,), contract_wire))

    back, gain_four, gain_five = norm_back(back, norm_three, norm_rows[4])
    grad_two = grad_three + back
    branch_two = grad_two.astype(BF16) * keep_rows.astype(BF16)
    table_head = product(logit_grad, a_four)
    contract_half = other_half(contract_keep, contract_came, BF16)
    contract_half = contract_half.reshape(2, block // 2, width)
    branch_two, expand_came, contract_across = spread(
        after(branch_two, table_head),
        12,
        ring((0,), expand_wire),
        swap(((0, 1),), contract_half),
        cut=4,
    )
    attn_grad = nt(branch_two, out_maps[1]).astype(BF16)
    cross_grad, key_grad, value_grad = attend_back(
        attn_grad, cross, text_keys, text_values, probs_two, images
    )
    pair_grad = jnp.concatenate([key_grad, value_grad], 1)
    text_keep, text_wire = weight_grad(group_captions, pair_grad, text_rows, WIRE)
    expand_half = other_half(expand_keep, expand_came, BF16)
    part = nt(cross_grad, w_cross)
    back, contract_across, contract_came, expand_across, text_came = collect(
        part,
        13,
        swap(((1, 1),), contract_half, contract_across),
        ring((1,), contract_wire, contract_came),
        swap(((0, 2),), expand_half),
        ring((0,), text_wire),
        cut=4,
    )

    back, gain_two, gain_three = norm_back(back, norm_two, norm_rows[2])
    grad_one = grad_two + back
    cross_keep, cross_wire = weight_grad(a_two, cross_grad, in_rows, WIRE)
    branch_one, expand_across, expand_came, cross_came = spread(
        after(grad_one.astype(BF16), cross_keep),
        14,
        swap(((2, 2),), expand_half, expand_across),
        ring((1,), expand_wire, expand_came),
        ring((0,), cross_wire),
        cut=4,
    )
    attn_grad = nt(branch_one, out_maps[0]).astype(BF16)
    triple_grad = jnp.concatenate(
        attend_back(attn_grad, queries, keys, values, probs_one, images), 1
    )
    out_one = weight_grad(attn_one, branch_one, HD // extent, BF16)
    out_two = weight_grad(attn_two, branch_two, HD // extent, BF16)
    out_keep = jnp.stack([out_one[0], out_two[0]], 1)
    out_wire = jnp.stack([out_one[1], out_two[1]], 2)
    text_half = other_half(text_keep, text_came, WIRE)
    triple_keep, triple_wire = weight_grad(a_one, triple_grad, in_rows, WIRE)
    part = nt(triple_grad, w_qkv)
    out_wire = plain(out_wire)
    back, text_across, text_came, out_came, triple_came = collect(
        part,
        15,
        swap(((0, 4),), text_half),
        ring((1,), text_wire, text_came),
        ring((0,), out_wire),
        ring((0,), triple_wire),
        cut=4,
    )

    back, gain_zero, gain_one = norm_back(back, norm_one, norm_rows[0])
    grad_zero = grad_one + back
    looked_grad = jnp.where(chosen, 0.0, grad_zero).astype(BF16)
    triple_half = other_half(triple_keep, triple_came, WIRE)
    cross_half = other_half(cross_keep, cross_came, WIRE)
    out_half = other_half(out_keep, out_came, BF16)
    expand_shard = own_half(expand_keep, expand_came, expand_across)
    looked_grad, triple_came, cross_came, triple_across, expand_shard = spread(
        looked_grad,
        16,
        ring((1,), triple_wire, triple_came),
        ring((1,), cross_wire, cross_came),
        swap(((0, 4),), triple_half),
        exchange(plain(expand_shard), hidden_width),
        cut=4,
    )
    table_keep, table_wire = weight_grad(
        at_code.astype(BF16), looked_grad, block, BF16, table_head
    )

    position_grad = jnp.sum(grad_zero.reshape(own_images, length, -1), 0)
    mask_grad = jnp.sum(jnp.where(chosen, grad_zero, 0.0), 0)
    gains = [gain_zero, gain_one, gain_two, gain_three, gain_four, gain_five, gain_six, gain_seven]
    rows = vectors.shape[0]
    padded = -(-rows // 192) * 192
    place_of = jnp.arange(padded - length)[:, None]
    tail = sum(jnp.where(place_of == k, gain, 0.0) for k, gain in enumerate([mask_grad] + gains))
    vector_grad = jnp.concatenate([position_grad, tail], 0)

    text_shard = own_half(text_keep, text_came, text_across)
    vector_part, table_came, out_came, cross_across, out_across, text_shard = group_call(
        SCATTER,
        vector_grad.reshape(8, padded // 8, width),
        17,
        ring((0,), table_wire),
        ring((1,), out_wire, out_came),
        swap(((0, 4),), cross_half),
        swap(((0, out_half.shape[0]),), out_half),
        exchange(plain(text_shard), HD),
        cut=3,
    )
    vector_part = vector_part + send(vector_part, AX, 1, 2)
    if extent == 2:
        vector_part = vector_part + send(vector_part, DX, 1, 2)
    else:
        vector_part = lax.psum(vector_part, DX)
    table_half = other_half(table_keep, table_came, BF16)
    proj_shard = jnp.concatenate(
        [
            own_half(triple_keep, triple_came, triple_across),
            own_half(cross_keep, cross_came, cross_across),
        ],
        2,
    )
    nothing, table_came, table_across, proj_shard = group_call(
        GATHER,
        jnp.broadcast_to(weight[0], (16, 128)),
        18,
        ring((1,), table_wire, table_came),
        swap(((0, 1),), table_half),
        exchange(plain(proj_shard), HD),
    )
    contract_across = contract_across.reshape(1, block, width)
    contract_shard = own_half(contract_keep, contract_came, contract_across).reshape(block, width)
    out_shard = own_half(out_keep, out_came, out_across).reshape(out_state[0].shape)
    table_shard = own_half(table_keep, table_came, table_across).reshape(block, width)

    expand_shard = expand_shard.reshape(expand_state[0].shape)

    shards = (table_shard, proj_shard, text_shard, out_shard, expand_shard, contract_shard)
    squares = sum((jnp.sum(piece * piece) for piece in shards))
    squares = squares + jnp.sum(vector_part * vector_part) / (2 * extent)
    lanes = jnp.arange(128)[None, :]
    numbers = jnp.where(lanes == 0, squares, jnp.where(lanes == 1, loss_sum, 0.0))
    numbers, vector_grad = last_call(jnp.broadcast_to(numbers, (8, 128)), vector_part)
    loss_value = numbers[0, 1] / 8.0 / mask_total
    grad_norm = jnp.sqrt(numbers[0, 0])
    vector_grad = vector_grad.reshape(padded, width)[:rows]
    clip_scale = CLIP / jnp.maximum(grad_norm, CLIP)
    count_step = step_count[0].astype(F32)
    fix_one = 1.0 - BETA_ONE**count_step
    fix_two = 1.0 - BETA_TWO**count_step
    results = [loss_value, grad_norm]
    matrices = (table_state, proj_state, text_state, out_state, expand_state, contract_state)
    updated = [
        adamw(state, grad * clip_scale, RATE_MATRIX, DECAY, fix_one, fix_two)
        for state, grad in zip(matrices, shards)
    ]
    vector_new = adamw(
        vector_state, vector_grad * clip_scale, RATE_VECTOR, 0.0, fix_one, fix_two
    )
    updated.insert(1, vector_new)
    for entry in updated:
        results.extend(entry)
    return tuple(results)


def solution(mesh):
    grid = mesh.devices
    extent = grid.shape[0] // 8
    fine = Mesh(grid.reshape(2, 2, 2, extent, grid.shape[1]), (AX, BX, EX, DX, CX))
    rows = P((CX,) + DP, None)
    both = P(None, DP, CX)
    kinds = (rows, P(), both, both, P(None, (CX,) + DP, None), P(DP, CX), rows)
    states = tuple(kind for kind in kinds for _ in range(3))
    batch = P(None, DP, None)
    return jax.shard_map(
        body,
        mesh=fine,
        in_specs=(batch, batch, P(None, DP), P(None, DP, None, None), P()) + states,
        out_specs=(P(), P()) + states,
        check_vma=False,
    )
```

```python
import math
from functools import partial

import jax
import jax.numpy as jnp
from jax import lax
from jax.experimental import pallas as pl
from jax.experimental.layout import Layout, with_layout_constraint
from jax.experimental.pallas import tpu as pltpu
from jax.sharding import Mesh, PartitionSpec as P

HD = 128
EPS_NORM = 1e-05
CLIP = 0.01
BETA_ONE = 0.9
BETA_TWO = 0.999
ADAM_EPS = 1e-08
DECAY = 0.01
RATE_MATRIX = 0.02
RATE_VECTOR = 0.2
SCALE = HD ** (-0.5)
F32 = jnp.float32
BF16 = jnp.bfloat16
WIRE = jnp.bfloat16

AX, BX, EX, DX, CX = "a", "b", "e", "d", "c"
DP = (AX, BX, EX, DX)
QX = (BX, EX)
MX = (AX, DX)
SWAP = [(0, 1), (1, 0)]
MESH = pl.DeviceIdType.MESH


def dot(x, y, dims):
    return lax.dot_general(x, y, (dims, ((), ())), preferred_element_type=F32)


def nn(x, y):
    return dot(x, y, ((1,), (0,)))


def nt(x, y):
    return dot(x, y, ((1,), (1,)))


def tn(x, y):
    return dot(x, y, ((0,), (0,)))


SHARE, RING, SWAP, EXCHANGE, GRAD, PRODUCT = range(6)
START, FAR, THROUGH = range(3)
GATHER, SCATTER = range(2)


class Here:
    def __init__(self, extent, send, recv, local):
        self.a, self.b, self.e, self.d, self.c = (
            lax.axis_index(name) for name in (AX, BX, EX, DX, CX)
        )
        self.extent = extent
        self.to_a, self.to_b, self.to_e, self.to_c = (
            {AX: 1 - self.a},
            {BX: 1 - self.b},
            {EX: 1 - self.e},
            {CX: 1 - self.c},
        )
        self.to_far = {BX: 1 - self.b, EX: 1 - self.e}
        self.to_d = [{DX: lax.rem(self.d + step, extent)} for step in range(1, extent)]
        self.send, self.recv, self.local = send, recv, local
        self.count = self.local_count = 0
        self.waits = []

    def greet(self, peers):
        barrier = pltpu.get_barrier_semaphore()
        for peer in peers:
            pl.semaphore_signal(barrier, inc=1, device_id=peer, device_id_type=MESH)
        pl.semaphore_wait(barrier, len(peers))

    def copy(self, source, target, peer, hold=False):
        made = pltpu.make_async_remote_copy(
            src_ref=source,
            dst_ref=target,
            send_sem=self.send.at[self.count],
            recv_sem=self.recv.at[self.count],
            device_id=peer,
            device_id_type=MESH,
        )
        self.count += 1
        made.start()
        if not hold:
            self.waits.append(made.wait_send)
        return made

    def late(self, made):
        self.waits.append(made.wait_recv)

    def keep(self, source, target):
        made = pltpu.make_async_copy(source, target, self.local.at[self.local_count])
        self.local_count += 1
        made.start()
        return made

    def finish(self):
        for wait in self.waits:
            wait()


def place(b, e, c):
    return (b * 2 + e) * 2 + c


def spot(array, mode, row, column, first, count):
    if mode == 0:
        return array.at[row, column, pl.ds(first, count)]
    if mode == 1:
        return array.at[row, pl.ds(first, count), column]
    return array.at[pl.ds(first, count), row, column]


def share_start(here, block, array, mode, first, count):
    source = block.at[pl.ds(first, count)]
    target = spot(array, mode, here.a, here.d, first, count)
    here.waits.append(here.keep(source, target).wait)
    across = here.copy(source, target, here.to_a)
    for peer in here.to_d:
        here.late(here.copy(source, target, peer))
    return across


def share_far(here, array, mode, first, count):
    block = spot(array, mode, 1 - here.a, here.d, first, count)
    for peer in here.to_d:
        here.late(here.copy(block, block, peer))


def exchange_start(here, pieces, out, width=0):
    mine = here.b * 2 + here.e
    peers = (
        (None, mine),
        (here.to_e, here.b * 2 + 1 - here.e),
        (here.to_b, (1 - here.b) * 2 + here.e),
        (here.to_far, (1 - here.b) * 2 + 1 - here.e),
    )
    started = []
    for peer, there in peers:
        if width:
            moves = []
            for k in range(pieces.shape[2] // width):
                column = pl.multiple_of((k % 2 * 4 + mine) * width, 128)
                target = out.at[k // 2, :, pl.ds(column, width)]
                moves.append((pieces.at[there, :, pl.ds(k * width, width)], target))
        else:
            moves = [(pieces.at[there], out.at[mine])]
        for source, target in moves:
            if peer is None:
                started.append(here.keep(source, target).wait)
            else:
                started.append(here.copy(source, target, peer).wait_recv)
    return started


def gather_start(here, x_ref, o_ref, cut):
    first, second = pl.ds(0, cut), pl.ds(cut, x_ref.shape[0] - cut)
    me = place(here.b, here.e, here.c)
    e_first = here.copy(x_ref.at[first], o_ref.at[me, first], here.to_e)
    b_first = here.copy(x_ref.at[second], o_ref.at[me, second], here.to_b)
    here.late(here.copy(x_ref, o_ref.at[me], here.to_c))
    e_second = here.copy(x_ref.at[second], o_ref.at[me, second], here.to_e)
    b_second = here.copy(x_ref.at[first], o_ref.at[me, first], here.to_b)
    here.waits.append(here.keep(x_ref, o_ref.at[me]).wait)
    return e_first, b_first, e_second, b_second


def gather_rest(here, o_ref, cut, started):
    first, second = pl.ds(0, cut), pl.ds(cut, o_ref.shape[1] - cut)
    e_first, b_first, e_second, b_second = started
    beside = place(here.b, 1 - here.e, here.c)
    across = place(1 - here.b, here.e, here.c)
    far = place(1 - here.b, 1 - here.e, here.c)

    def on(block, peer):
        return here.copy(block, block, peer)

    e_first.wait_recv()
    b_third = on(o_ref.at[beside, first], here.to_b)
    here.late(on(o_ref.at[beside, first], here.to_c))
    b_first.wait_recv()
    e_third = on(o_ref.at[across, second], here.to_e)
    here.late(on(o_ref.at[across, second], here.to_c))
    e_second.wait_recv()
    here.late(on(o_ref.at[beside, second], here.to_c))
    b_second.wait_recv()
    here.late(on(o_ref.at[across, first], here.to_c))
    b_third.wait_recv()
    here.late(on(o_ref.at[far, first], here.to_c))
    e_third.wait_recv()
    here.late(on(o_ref.at[far, second], here.to_c))


def scatter_start(here, p_ref, paired):
    b, e, c = here.b, here.e, here.c
    order = ((1 - b, 1 - e), (1 - b, e), (b, 1 - e), (b, e))
    return [
        here.copy(p_ref.at[place(bb, ee, 1 - c)], paired.at[k], here.to_c)
        for k, (bb, ee) in enumerate(order)
    ]


def by_rows(start, count, body):
    step = 16 if start % 16 == 0 and count % 16 == 0 else 8

    def some(k, carry):
        body(lambda origin=0: pl.ds(pl.multiple_of(start - origin + k * step, step), step))
        return carry

    lax.fori_loop(0, count // step, some, 0)


def scatter_rest(here, p_ref, o_ref, cut, pairs, paired, held, from_b, from_e, last_b, last_e):
    b, e, c = here.b, here.e, here.c
    count = o_ref.shape[0]
    rest = count - cut
    parts = 2 if cut < rest and rest % 32 == 0 else 1
    chunks = [(cut + k * (rest // parts), rest // parts) for k in range(parts)]
    first, second = pl.ds(0, cut), pl.ds(cut, rest)

    def pair(k, target, spot):
        pairs[k].wait_recv()

        def body(at):
            target[at()] = p_ref[spot, at()] + paired[k, at()]

        by_rows(0, count, body)

    def add(start, size, target, source, origin):
        def body(at):
            target[at()] = target[at()] + source[at(origin)]

        by_rows(start, size, body)

    def first_over_e(k):
        start, size = chunks[k]
        target = from_e.at[0, pl.ds(start - cut, size)]
        return here.copy(held.at[0, pl.ds(start, size)], target, here.to_e, hold=True)

    pair(0, held.at[0], place(1 - b, 1 - e, c))
    moving = first_over_e(0)
    b_first = here.copy(held.at[0, first], from_b.at[0], here.to_b, hold=True)
    pair(2, held.at[2], place(b, 1 - e, c))
    pair(1, held.at[1], place(1 - b, e, c))
    pair(3, o_ref, place(b, e, c))
    b_first.wait_send()
    b_second = here.copy(held.at[1, first], from_b.at[1], here.to_b)
    thirds = []
    for k, (start, size) in enumerate(chunks):
        moving.wait_send()
        came = moving
        if k + 1 < parts:
            moving = first_over_e(k + 1)
        else:
            e_second = here.copy(held.at[2, second], from_e.at[1], here.to_e)
        came.wait_recv()
        add(start, size, held.at[1], from_e.at[0], cut)
        piece = pl.ds(start, size)
        thirds.append(
            here.copy(held.at[1, piece], last_b.at[pl.ds(start - cut, size)], here.to_b)
        )
    b_first.wait_recv()
    add(0, cut, held.at[2], from_b.at[0], 0)
    e_third = here.copy(held.at[2, first], last_e, here.to_e)
    b_second.wait_recv()
    add(0, cut, o_ref, from_b.at[1], 0)
    e_second.wait_recv()
    add(cut, rest, o_ref, from_e.at[1], cut)
    e_third.wait_recv()
    add(0, cut, o_ref, last_e, 0)
    for made, (start, size) in zip(thirds, chunks):
        made.wait_recv()
        add(start, size, o_ref, last_b, cut)


def ring_start(here, halves, source, out):
    lead = source.shape[1]
    for half in halves:
        row, count = {0: (1 - here.a, lead // 2), 1: (here.a, lead // 2)}[half]
        for step, peer in enumerate(here.to_d):
            part = pl.ds(row * count, count)
            here.late(here.copy(source.at[step, part], out.at[step, part], peer))


def columns_of(right):
    wide = min(right.shape[1], 1024)
    return wide, right.shape[1] // wide


def grad_in_kernel(here, rows, left, right, keep, wire):
    lead, extent = keep.shape[0], here.extent
    deep = rows * extent
    wide, blocks = columns_of(right)

    def some(k, carry):
        along = pl.ds(pl.multiple_of(k // blocks * deep, 128), deep)
        across = pl.ds(pl.multiple_of(lax.rem(k, blocks) * wide, 128), wide)
        value = tn(left[:, along], right[:, across])
        for column in range(extent):
            part = value[column * rows : (column + 1) * rows]
            step = lax.rem(column - here.d + extent, extent)

            @pl.when(step == 0)
            def _():
                keep[k // blocks, :, across] = part

            @pl.when(step > 0)
            def _():
                wire[step - 1, k // blocks, :, across] = part.astype(wire.dtype)

        return carry

    lax.fori_loop(0, lead * blocks, some, 0)


def product_in_kernel(left, right, out):
    wide, blocks = columns_of(right)
    deep = 512

    def some(k, carry):
        along = pl.ds(pl.multiple_of(k // blocks * deep, 128), deep)
        across = pl.ds(pl.multiple_of(lax.rem(k, blocks) * wide, 128), wide)
        out[along, across] = tn(left[:, along], right[:, across])
        return carry

    lax.fori_loop(0, left.shape[1] // deep * blocks, some, 0)


def group_kernel(kind, cut, plan, extent, in_count, out_count, *refs):
    ins, outs = list(refs[:in_count]), list(refs[in_count : in_count + out_count])
    scratch = refs[in_count + out_count :]
    here = Here(extent, *scratch[:3])
    x_ref, o_ref = ins.pop(0), outs.pop(0)
    peers = [here.to_b, here.to_e, here.to_c]
    if any(entry[0] == EXCHANGE for entry in plan):
        peers.append(here.to_far)
    if any(
        entry[0] == SWAP or entry[0] == SHARE and any(do[0] != FAR for do in entry[2])
        for entry in plan
    ):
        peers.append(here.to_a)
    if any(entry[0] in (SHARE, RING, GRAD) for entry in plan):
        peers.extend(here.to_d)
    here.greet(peers)
    if kind == GATHER:
        started = gather_start(here, x_ref, o_ref, cut)
    else:
        started = scatter_start(here, x_ref, scratch[3])
    through = []
    for entry in plan:
        if entry[0] in (GRAD, PRODUCT):
            continue
        source, out = ins.pop(0), outs.pop(0)
        if entry[3]:
            ins.pop(0)
        if entry[0] == SHARE:
            for action, first, count in entry[2]:
                if action == FAR:
                    share_far(here, out, entry[1], first, count)
                else:
                    across = share_start(here, source, out, entry[1], first, count)
                    if action == THROUGH:
                        through.append((across, out, entry[1], first, count))
                    else:
                        here.late(across)
        elif entry[0] == RING:
            ring_start(here, entry[2], source, out)
        elif entry[0] == SWAP:
            for first, count in entry[2]:
                part = pl.ds(first, count)
                here.late(here.copy(source.at[part], out.at[part], here.to_a))
        else:
            here.waits.extend(exchange_start(here, source, out, entry[1]))
    for entry in plan:
        if entry[0] == GRAD:
            left, right = ins.pop(0), ins.pop(0)
            keep, wire, out = outs.pop(0), outs.pop(0), outs.pop(0)
            grad_in_kernel(here, entry[1], left, right, keep, wire)
            ring_start(here, entry[2], wire, out)
        elif entry[0] == PRODUCT:
            product_in_kernel(ins.pop(0), ins.pop(0), outs.pop(0))
    if kind == GATHER:
        gather_rest(here, o_ref, cut, started)
    else:
        scatter_rest(here, x_ref, o_ref, cut, started, *scratch[3:])
    for across, out, mode, first, count in through:
        across.wait_recv()
        share_far(here, out, mode, first, count)
    here.finish()


def share(mode, actions, block, array=None):
    return (SHARE, mode, actions, block, array)


def ring(halves, pieces, array=None):
    return (RING, 0, halves, pieces, array)


def swap(parts, piece, array=None):
    return (SWAP, 0, parts, piece, array)


def exchange(pieces, width=0):
    return (EXCHANGE, width, (), pieces, None)


def grad(left, right, rows, wire):
    return (GRAD, rows, (0,), (left, right, wire), None)


def product(left, right):
    return (PRODUCT, 0, (), (left, right), None)


def group_call(kind, x, number, *moves, cut=2):
    extent = lax.axis_size(DX)
    if kind == GATHER:
        out = jax.ShapeDtypeStruct((8,) + x.shape, x.dtype)
        space, scratch = pl.ANY, []
        cut = x.shape[0] // cut
    else:
        shape = x.shape[1:]
        out = jax.ShapeDtypeStruct(shape, x.dtype)
        space = pltpu.VMEM
        cut = shape[0] // cut
        first, second = (cut,) + shape[1:], (shape[0] - cut,) + shape[1:]
        sizes = ((4,) + shape, (3,) + shape, (2,) + first, (2,) + second, second, first)
        scratch = [pltpu.VMEM(size, x.dtype) for size in sizes]
    operands, outs, aliases, plan, copies, locals_ = [x], [out], {}, [], 16, 2
    anywhere, vmem = pl.BlockSpec(memory_space=pl.ANY), pl.BlockSpec(memory_space=pltpu.VMEM)
    in_specs, out_specs = [pl.BlockSpec(memory_space=space)], [pl.BlockSpec(memory_space=space)]
    worked = {}
    for place_of, (what, mode, actions, source, array) in enumerate(moves):
        if what == GRAD and mode % 128:
            worked[place_of] = weight_grad(source[0], source[1], mode, source[2])
            what, source = RING, worked[place_of][1]
        if what in (GRAD, PRODUCT):
            operands.extend(source[:2])
            in_specs.extend([vmem, vmem])
            rows, columns = source[0].shape[1], source[1].shape[1]
            if what == PRODUCT:
                outs.append(jax.ShapeDtypeStruct((rows, columns), F32))
                out_specs.append(vmem)
            else:
                lead = rows // (mode * extent)
                pieces = jax.ShapeDtypeStruct((extent - 1, lead, mode, columns), source[2])
                outs.append(jax.ShapeDtypeStruct((lead, mode, columns), F32))
                outs.extend([pieces, pieces])
                out_specs.extend([vmem, vmem, anywhere])
            plan.append((what, mode, actions, False))
            copies += 2 * extent
            continue
        operands.append(source)
        if array is not None:
            aliases[len(operands)] = len(outs)
            operands.append(array)
            outs.append(jax.ShapeDtypeStruct(array.shape, array.dtype))
        elif what == SHARE:
            lead, block = source.shape[:1], source.shape[1:]
            full = ((2, extent) + lead, (2,) + lead + (extent,), lead + (2, extent))[mode]
            outs.append(jax.ShapeDtypeStruct(full + block, source.dtype))
        elif what == EXCHANGE and mode:
            parts = source.shape[2] // mode
            shape = (parts // 2, source.shape[1], 8 * mode)
            outs.append(jax.ShapeDtypeStruct(shape, source.dtype))
            copies += 3 * parts
            locals_ += parts
        else:
            outs.append(jax.ShapeDtypeStruct(source.shape, source.dtype))
        in_specs.extend([anywhere] * (len(operands) - len(in_specs)))
        out_specs.append(anywhere)
        plan.append((what, mode, actions, array is not None))
        copies += 3 + 2 * extent * len(actions)
        locals_ += 1 + len(actions)
    held = [ref for ref in scratch] + [
        ref for ref, spec in zip(operands + outs, in_specs + out_specs) if spec is vmem
    ]
    room = 6 << 20 if any(entry[0] in (GRAD, PRODUCT) for entry in plan) else 1 << 20
    if kind == SCATTER:
        held.extend([x, out])
    room += sum(math.prod(ref.shape) * jnp.dtype(ref.dtype).itemsize for ref in held)
    order = [k for k, entry in enumerate(plan) if entry[0] not in (GRAD, PRODUCT)]
    assert order == list(range(len(order)))
    results = pl.pallas_call(
        partial(group_kernel, kind, cut, plan, extent, len(operands), len(outs)),
        out_shape=tuple(outs),
        in_specs=in_specs,
        out_specs=tuple(out_specs),
        scratch_shapes=[
            pltpu.SemaphoreType.DMA((copies,)),
            pltpu.SemaphoreType.DMA((copies,)),
            pltpu.SemaphoreType.DMA((locals_,)),
        ]
        + scratch,
        input_output_aliases=aliases,
        compiler_params=pltpu.CompilerParams(
            collective_id=number, has_side_effects=True, vmem_limit_bytes=room
        ),
        cost_estimate=pl.CostEstimate(
            flops=0, bytes_accessed=80_000_000, transcendentals=0
        ),
    )(*operands)
    if not moves:
        return results[0]
    results = list(results)
    for place_of, (keep, pieces) in worked.items():
        results[place_of + 1 : place_of + 1] = [keep, pieces]
    return tuple(results)


def first_kernel(extent, *refs):
    small, text, table_ref, out_ref, proj_ref, text_ref, expand_ref, contract_ref = refs[:8]
    small_out, text_out, proj_block, table, outs = refs[8:13]
    text_pieces, expand_pieces, contract_block, out_block = refs[13:17]
    table_block, proj_pieces = refs[17:19]
    here = Here(extent, *refs[19:])
    peers = [here.to_b, here.to_e, here.to_c, here.to_far, here.to_a] + here.to_d
    here.greet(peers)
    units, rows = table_block.shape[:2]

    def table_unit(k):
        def body(at):
            table_block[k, at(k * rows)] = table_ref[at()].astype(BF16)

        by_rows(k * rows, rows, body)
        return share_start(here, table_block, table, 0, k, 1)

    def by_head(source, target):
        def body(at):
            for q in range(4):
                for kind in range(source.shape[0]):
                    for row in range(2):
                        target[q, at(), pl.ds((kind * 2 + row) * HD, HD)] = source[
                            kind, at(), pl.ds((row * 4 + q) * HD, HD)
                        ].astype(BF16)

        by_rows(0, source.shape[1], body)

    across = [table_unit(0), table_unit(1), table_unit(2)]
    small_started = gather_start(here, small, small_out, small.shape[0] // 2)
    by_head(proj_ref, proj_pieces)
    here.waits.extend(exchange_start(here, proj_pieces, proj_block))
    gather_rest(here, small_out, small.shape[0] // 2, small_started)
    text_started = gather_start(here, text, text_out, text.shape[0] // 2)
    for k in range(units):
        across[k].wait_recv()
        share_far(here, table, 0, k, 1)
        if k + 3 < units:
            across.append(table_unit(k + 3))
        elif k + 3 == units:
            out_block[...] = out_ref[...].astype(BF16)
            across.append(share_start(here, out_block, outs, 2, 0, 1))
        if k == 0:
            by_head(text_ref, text_pieces)
        elif k == 1:
            gather_rest(here, text_out, text.shape[0] // 2, text_started)
            width = expand_ref.shape[1] // 8

            def body(at):
                for q in range(4):
                    for row in range(2):
                        expand_pieces[q, at(), pl.ds(row * width, width)] = expand_ref[
                            at(), pl.ds((row * 4 + q) * width, width)
                        ].astype(BF16)

            by_rows(0, expand_ref.shape[0], body)
        elif k == 2:
            for unit in range(units):

                def body(at):
                    contract_block[unit, at(unit * rows)] = contract_ref[at()].astype(BF16)

                by_rows(unit * rows, rows, body)
    across[units].wait_recv()
    share_far(here, outs, 2, 0, 1)
    here.finish()


def first_call(small, text, table, outs, proj, text_maps, expand, contract):
    extent = lax.axis_size(DX)
    rows, width = table.shape
    kinds, in_rows, half = proj.shape

    def like(shape, kind=BF16):
        return jax.ShapeDtypeStruct(shape, kind)

    table_shape = (4, rows // 4, width)
    proj_shape = (4, in_rows, kinds * 2 * HD)
    out_shape = [
        like((8,) + small.shape, small.dtype),
        like((8,) + text.shape),
        like(proj_shape),
        like((2, extent) + table_shape),
        like((2, 2, extent) + outs.shape[1:]),
        like((4, text_maps.shape[1], 4 * HD)),
        like((4, in_rows, expand.shape[1] // 4)),
        like(table_shape),
        like(outs.shape),
    ]
    copies = 36 + 12 * extent
    anywhere, vmem = pl.BlockSpec(memory_space=pl.ANY), pl.BlockSpec(memory_space=pltpu.VMEM)
    return pl.pallas_call(
        partial(first_kernel, extent),
        out_shape=tuple(out_shape),
        in_specs=[anywhere] * 2 + [vmem] * 6,
        out_specs=tuple([anywhere] * 5 + [vmem] * 4),
        scratch_shapes=[
            pltpu.VMEM(table_shape, BF16),
            pltpu.VMEM(proj_shape, BF16),
            pltpu.SemaphoreType.DMA((copies,)),
            pltpu.SemaphoreType.DMA((copies,)),
            pltpu.SemaphoreType.DMA((12,)),
        ],
        compiler_params=pltpu.CompilerParams(
            collective_id=1, has_side_effects=True, vmem_limit_bytes=48 << 20
        ),
    )(small, text, table, outs, proj, text_maps, expand, contract)


def last_kernel(extent, tile_ref, x_ref, total_ref, o_ref, send, recv, local, held, sums):
    here = Here(extent, send, recv, local)
    near = [
        {
            BX: lax.rem(here.b + k // 4, 2),
            EX: lax.rem(here.e + k // 2 % 2, 2),
            CX: lax.rem(here.c + k % 2, 2),
        }
        for k in range(1, 8)
    ]
    away = [
        {AX: lax.rem(here.a + k // extent, 2), DX: lax.rem(here.d + k % extent, extent)}
        for k in range(1, 2 * extent)
    ]
    here.greet(near + away)
    first = [here.copy(tile_ref, held.at[k], peer) for k, peer in enumerate(near)]
    cut = x_ref.shape[0] // 3
    started = gather_start(here, x_ref, o_ref, cut)
    for made in first:
        made.wait_recv()
    terms = [tile_ref[...]] + [held[k] for k in range(7)]
    while len(terms) > 1:
        terms = [terms[k] + terms[k + 1] for k in range(0, len(terms), 2)]
    sums[...] = terms[0]
    mine = 7 + here.a * extent + here.d
    second = [here.copy(sums, held.at[mine], peer) for peer in away]
    held[mine] = terms[0]
    gather_rest(here, o_ref, cut, started)
    for made in second:
        made.wait_recv()
    total = held[7]
    for k in range(1, 2 * extent):
        total = total + held[7 + k]
    total_ref[...] = total
    here.finish()


def last_call(tile, x):
    extent = lax.axis_size(DX)
    peers = 6 + 2 * extent
    vmem, anywhere = pl.BlockSpec(memory_space=pltpu.VMEM), pl.BlockSpec(memory_space=pl.ANY)
    return pl.pallas_call(
        partial(last_kernel, extent),
        out_shape=(
            jax.ShapeDtypeStruct(tile.shape, tile.dtype),
            jax.ShapeDtypeStruct((8,) + x.shape, x.dtype),
        ),
        in_specs=[vmem, anywhere],
        out_specs=(vmem, anywhere),
        scratch_shapes=[
            pltpu.SemaphoreType.DMA((peers + 13,)),
            pltpu.SemaphoreType.DMA((peers + 13,)),
            pltpu.SemaphoreType.DMA((1,)),
            pltpu.VMEM((peers + 1,) + tile.shape, tile.dtype),
            pltpu.VMEM(tile.shape, tile.dtype),
        ],
        compiler_params=pltpu.CompilerParams(collective_id=19, has_side_effects=True),
    )(tile, x)


def spread(rows, number, *moves, cut=2):
    count, width = rows.shape
    full = group_call(GATHER, rows, number, *moves, cut=cut)
    if moves:
        return (full[0].reshape(8 * count, width),) + tuple(full[1:])
    return full.reshape(8 * count, width)


def collect(parts, number, *moves, cut=2):
    count, width = parts.shape
    parts = parts.reshape(8, count // 8, width)
    return group_call(SCATTER, parts, number, *moves, cut=cut)


def after(value, *needed):
    return lax.optimization_barrier((value, needed))[0]


def plain(x):
    return with_layout_constraint(x, Layout(tuple(range(x.ndim))))


def send(block, axis, step, extent):
    ring = [(k, (k + step) % extent) for k in range(extent)]
    return plain(lax.ppermute(plain(block), axis, ring))


def pick(array, index, axis):
    return lax.dynamic_slice_in_dim(array, index, 1, axis)


def grad_kernel(with_base, extent, rows, d_ref, left_ref, right_ref, *refs):
    keep_ref, piece_ref = refs[-2:]
    product = tn(left_ref[...], right_ref[...])
    if with_base:
        product = product + refs[0][...]
    for k in range(keep_ref.shape[0]):
        for column in range(extent):
            start = (k * extent + column) * rows
            part = product[start : start + rows]
            step = lax.rem(column - d_ref[0] + extent, extent)

            @pl.when(step == 0)
            def _():
                keep_ref[k] = part

            @pl.when(step > 0)
            def _():
                piece_ref[step - 1, k] = part.astype(piece_ref.dtype)


def weight_grad(left, right, rows, wire, base=None):
    extent = lax.axis_size(DX)
    count, columns = right.shape
    lead = left.shape[1] // (rows * extent)
    if rows % 128:
        full = tn(left, right) if base is None else tn(left, right) + base
        full = full.reshape(lead, extent, rows, columns)
        split = [
            lax.dynamic_index_in_dim(full, lax.rem(lax.axis_index(DX) + s, extent), 1, False)
            for s in range(extent)
        ]
        return split[0], jnp.stack(split[1:]).astype(wire)

    chunk = max(1, lead // 4) if rows * extent * (lead // 4) >= 512 else max(1, 512 // (rows * extent))
    deep = chunk * extent * rows
    wide = columns if columns <= 1024 else columns // 2
    in_specs = [
        pl.BlockSpec((count, deep), lambda k, j, d: (0, k)),
        pl.BlockSpec((count, wide), lambda k, j, d: (0, j)),
    ]
    operands = [left, right]
    if base is not None:
        in_specs.append(pl.BlockSpec((deep, wide), lambda k, j, d: (k, j)))
        operands.append(base)
    return pl.pallas_call(
        partial(grad_kernel, base is not None, extent, rows),
        out_shape=(
            jax.ShapeDtypeStruct((lead, rows, columns), F32),
            jax.ShapeDtypeStruct((extent - 1, lead, rows, columns), wire),
        ),
        grid_spec=pltpu.PrefetchScalarGridSpec(
            num_scalar_prefetch=1,
            grid=(lead // chunk, columns // wide),
            in_specs=in_specs,
            out_specs=(
                pl.BlockSpec((chunk, rows, wide), lambda k, j, d: (k, 0, j)),
                pl.BlockSpec((extent - 1, chunk, rows, wide), lambda k, j, d: (0, k, 0, j)),
            ),
        ),
        compiler_params=pltpu.CompilerParams(vmem_limit_bytes=48 << 20),
        cost_estimate=pl.CostEstimate(
            flops=2 * count * left.shape[1] * columns,
            bytes_accessed=left.size * 2 + right.size * 2 + left.shape[1] * columns * 4,
            transcendentals=0,
        ),
    )(lax.axis_index(DX).reshape(1), *operands)


def total_at(index, keep, pieces):
    total = pick(keep.reshape((2, -1) + keep.shape[1:]), index, 0)
    for step in range(pieces.shape[0]):
        piece = pieces[step].reshape((2, -1) + pieces.shape[2:])
        total = total + pick(piece, index, 0).astype(F32)
    return total[0]


def other_half(keep, pieces, wire):
    return total_at(1 - lax.axis_index(AX), keep, pieces).astype(wire)


def own_half(keep, pieces, across):
    return total_at(lax.axis_index(AX), keep, pieces) + across.astype(F32)


def layer_norm(inputs, gain, bias):
    average = jnp.mean(inputs, -1, keepdims=True)
    centred = inputs - average
    factor = lax.rsqrt(jnp.mean(centred * centred, -1, keepdims=True) + EPS_NORM)
    normed = centred * factor
    return (normed * gain + bias).astype(BF16), (normed, factor)


def norm_back(upstream, saved, gain):
    normed, factor = saved
    inner = upstream * gain
    back = factor * (
        inner
        - jnp.mean(inner, -1, keepdims=True)
        - normed * jnp.mean(inner * normed, -1, keepdims=True)
    )
    return back, jnp.sum(upstream * normed, 0), jnp.sum(upstream, 0)


def each_head(per, query_rows, key_rows):
    for image in range(per):
        for head in range(2):
            columns = pl.ds(head * HD, HD)
            yield pl.ds(image * query_rows, query_rows), pl.ds(image * key_rows, key_rows), columns


def probabilities(query, key):
    scores = nt(query, key) * SCALE
    top = jnp.max(scores, -1, keepdims=True)
    logsum = top + jnp.log(jnp.sum(jnp.exp(scores - top), -1, keepdims=True))
    return jnp.exp(scores - logsum)


def attend_back_kernel(per, g_ref, q_ref, k_ref, v_ref, o_ref):
    sizes = q_ref.shape[0] // per, k_ref.shape[0] // per
    for rows, key_rows, columns in each_head(per, *sizes):
        grad_out = g_ref[rows, columns]
        query, key, value = q_ref[rows, columns], k_ref[key_rows, columns], v_ref[key_rows, columns]
        probs = probabilities(query, key)
        grad_probs = nt(grad_out, value)
        inner = jnp.sum(probs * grad_probs, -1, keepdims=True)
        grad_scores = (probs * (grad_probs - inner)).astype(BF16)
        grads = (
            nn(grad_scores, key) * SCALE,
            tn(grad_scores, query) * SCALE,
            tn(probs.astype(BF16), grad_out),
        )
        for kind, grad in enumerate(grads):
            o_ref[rows, pl.ds(kind * 2 * HD + columns.start, HD)] = grad.astype(BF16)


def attend_back_joint(upstream, triple, images):
    per = 2 if images % 2 == 0 else 1
    rows = triple.shape[0] // images * per

    def spec(kind, kinds=1):
        return pl.BlockSpec((rows, kinds * 2 * HD), lambda k: (k, kind))

    return pl.pallas_call(
        partial(attend_back_kernel, per),
        out_shape=jax.ShapeDtypeStruct(triple.shape, BF16),
        grid=(images // per,),
        in_specs=[spec(0), spec(0), spec(1), spec(2)],
        out_specs=spec(0, 3),
        cost_estimate=pl.CostEstimate(
            flops=20 * triple.shape[0] * HD * HD, bytes_accessed=1 << 22, transcendentals=1 << 18
        ),
    )(upstream, triple, triple, triple)


def dot_images(x, y, x_side, y_side):
    dims = (((x_side,), (y_side,)), ((0,), (0,)))
    return lax.dot_general(x, y, dims, preferred_element_type=F32)


def heads(x, images):
    x = x.reshape(images, -1, x.shape[-1])
    return [x[..., k : k + HD] for k in range(0, x.shape[-1], HD)]


def flat(parts):
    joined = jnp.concatenate([part.astype(BF16) for part in parts], -1)
    return joined.reshape(-1, joined.shape[-1])


def attend(queries, keys, values):
    mixed, saved = [], []
    for query, key, value in zip(queries, keys, values):
        scores = dot_images(query, key, 2, 2) * SCALE
        top = jnp.max(scores, -1, keepdims=True)
        logsum = top + jnp.log(jnp.sum(jnp.exp(scores - top), -1, keepdims=True))
        probs = jnp.exp(scores - logsum)
        mixed.append(dot_images(probs.astype(BF16), value, 2, 1))
        saved.append(probs)
    return flat(mixed), saved


def attend_back(upstream, queries, keys, values, saved, images):
    grads = []
    for grad_out, query, key, value, probs in zip(
        heads(upstream, images), queries, keys, values, saved
    ):
        grad_probs = dot_images(grad_out, value, 2, 2)
        inner = jnp.sum(probs * grad_probs, -1, keepdims=True)
        grad_scores = (probs * (grad_probs - inner)).astype(BF16)
        grads.append(
            (
                dot_images(grad_scores, key, 2, 1) * SCALE,
                dot_images(grad_scores, query, 1, 1) * SCALE,
                dot_images(probs.astype(BF16), grad_out, 1, 1),
            )
        )
    return tuple(flat(parts) for parts in zip(*grads))


def adamw(state, grad, rate, decay, fix_one, fix_two):
    master, first, second = state
    first_new = BETA_ONE * first + (1.0 - BETA_ONE) * grad
    second_new = BETA_TWO * second + (1.0 - BETA_TWO) * grad * grad
    update = first_new / fix_one / (jnp.sqrt(second_new / fix_two) + ADAM_EPS)
    return master - rate * (update + decay * master), first_new, second_new


def body(image_codes, masked, null_caption, captions, step_count, *states):
    table_state, vector_state, proj_state, text_state, out_state, expand_state, contract_state = (
        states[k : k + 3] for k in range(0, 21, 3)
    )
    b, e, c = (lax.axis_index(k) for k in (BX, EX, CX))
    extent = lax.axis_size(DX)
    vectors = vector_state[0]
    length = vectors.shape[0] - 9
    norm_rows = vectors[length + 1 :]
    width = vectors.shape[1]
    block = table_state[0].shape[0]
    kinds, in_rows, half = proj_state[0].shape
    text_rows = text_state[0].shape[1]
    hidden_width = extent * block
    pair = 2 * HD

    own_images = image_codes.shape[1]
    tokens = own_images * length
    small = jnp.concatenate(
        [
            image_codes.reshape(2, -1),
            masked.reshape(2, -1),
            jnp.broadcast_to(null_caption.reshape(2, -1, 1), masked.shape).reshape(2, -1),
        ],
        1,
    )
    small = lax.dynamic_index_in_dim(small, c, 0, False)
    small = jnp.pad(small, (0, -small.shape[0] % (16 * 128)))
    own_mask, own_null = small[tokens : 2 * tokens], small[2 * tokens : 3 * tokens]
    text = lax.dynamic_index_in_dim(captions, c, 0, False)
    text = text.reshape(-1, text.shape[-1])
    gathered, group_captions, proj_block, table, outs, *rest = first_call(
        small.reshape(16, -1),
        text,
        table_state[0],
        out_state[0],
        proj_state[0],
        text_state[0],
        expand_state[0],
        contract_state[0],
    )
    text_pieces, expand_pieces, contract_block, out_block = rest
    gathered = gathered.reshape(8, -1)
    group_captions = group_captions.reshape(-1, group_captions.shape[-1])
    group_codes = gathered[:, :tokens].reshape(-1)
    weight = gathered[:, tokens : 2 * tokens].reshape(-1).astype(F32)
    chosen = own_mask[:, None] == 1
    keep_rows = 1.0 - own_null[:, None].astype(F32)
    images = 8 * own_images
    table = table.reshape(-1, width)
    codes_here = table.shape[0]

    in_half = lax.rem(group_codes, 8 * hidden_width)
    outer = in_half // block
    inside = (
        (group_codes // (8 * hidden_width) == c)
        & (lax.rem(outer // extent, 2) == e)
        & (lax.rem(outer // (2 * extent), 2) == b)
    )
    outer = (outer // (4 * extent)) * extent + lax.rem(outer, extent)
    local_code = jnp.where(inside, outer * block + lax.rem(in_half, block), -1)
    at_code = jnp.arange(codes_here)[None, :] == local_code[:, None]

    part = nn(at_code.astype(BF16), table).astype(BF16)
    looked, proj, text_block = collect(
        part, 2, share(1, ((START, 0, 3),), proj_block), exchange(text_pieces), cut=4
    )
    x_zero = jnp.where(chosen, vectors[length], looked.astype(F32))
    x_zero = x_zero + jnp.tile(vectors[:length], (own_images, 1))
    a_one, norm_one = layer_norm(x_zero, norm_rows[0], norm_rows[1])
    a_one, proj, w_text, expand_block = spread(
        a_one,
        3,
        share(1, ((THROUGH, 3, 1), (FAR, 0, 3)), proj_block, proj),
        share(1, ((START, 0, 1),), text_block),
        exchange(expand_pieces),
        cut=4,
    )
    proj = proj.reshape(width, kinds * pair)
    w_qkv, w_cross = proj[:, : 3 * pair], proj[:, 3 * pair :]
    triple = nn(a_one, w_qkv).astype(BF16)
    queries, keys, values = (
        heads(triple[:, k : k + pair], images) for k in (0, pair, 2 * pair)
    )
    attn_one, unused = attend(queries, keys, values)
    part = nn(attn_one, outs[0].reshape(pair, width))
    back, w_text, outs = collect(
        part,
        4,
        share(1, ((START, 1, 3), (FAR, 0, 1)), text_block, w_text),
        share(2, ((START, 1, 1),), out_block, outs),
        cut=4,
    )
    x_one = x_zero + back

    a_two, norm_two = layer_norm(x_one, norm_rows[2], norm_rows[3])
    a_two, w_text, outs, expand = spread(
        a_two,
        5,
        share(1, ((FAR, 1, 3),), text_block, w_text),
        share(2, ((FAR, 1, 1),), out_block, outs),
        share(1, ((START, 0, 2),), expand_block),
        cut=4,
    )
    w_text = w_text.reshape(-1, 2 * pair)
    out_maps = outs.reshape(2, pair, width)
    text_pair = nn(group_captions, w_text).astype(BF16)
    text_keys, text_values = heads(text_pair[:, :pair], images), heads(text_pair[:, pair:], images)
    cross = heads(nn(a_two, w_cross).astype(BF16), images)
    attn_two, probs_two = attend(cross, text_keys, text_values)
    part = nn(attn_two, out_maps[1])
    back, expand, contract = collect(
        part,
        6,
        share(1, ((START, 2, 2), (FAR, 0, 2)), expand_block, expand),
        share(0, ((START, 0, 2),), contract_block),
        cut=4,
    )
    x_two = x_one + keep_rows * back

    a_three, norm_three = layer_norm(x_two, norm_rows[4], norm_rows[5])
    a_three, expand, contract = spread(
        a_three,
        7,
        share(1, ((FAR, 2, 2),), expand_block, expand),
        share(0, ((FAR, 0, 2), (THROUGH, 2, 1), (THROUGH, 3, 1)), contract_block, contract),
        cut=4,
    )
    expand, contract = expand.reshape(width, -1), contract.reshape(-1, width)
    mask_total = after(jnp.broadcast_to(jnp.sum(weight), (8, 128)), x_two)
    mask_total = mask_total + send(mask_total, AX, 1, 2)
    mask_total = mask_total + sum(send(mask_total, DX, step, extent) for step in range(1, extent))
    mask_total = mask_total[0, 0]
    preact = nn(a_three, expand)
    hidden = jax.nn.gelu(preact, approximate=True).astype(BF16)
    x_three = x_two + collect(nn(hidden, contract), 8)

    a_four, norm_four = layer_norm(x_three, norm_rows[6], norm_rows[7])
    a_four = spread(a_four, 9)
    logits = nt(a_four, table)
    target = jnp.sum(jnp.where(at_code, logits, 0.0), 1)
    top = jnp.max(logits, 1)
    total = jnp.sum(jnp.exp(logits - top[:, None]), 1)
    count = target.shape[0]
    stats = jnp.stack([top, total, target, target])
    stats = group_call(GATHER, stats.reshape(16, count // 4), 10).reshape(8, 4, count)
    peak = jnp.max(stats[:, 0], 0)
    total = jnp.sum(stats[:, 1] * jnp.exp(stats[:, 0] - peak), 0)
    head_logsum = peak + jnp.log(total)
    loss_sum = jnp.sum(weight * (head_logsum - jnp.sum(stats[:, 2], 0)))

    head_probs = jnp.exp(logits - head_logsum[:, None])
    logit_grad = (head_probs - at_code.astype(F32)) * (weight / mask_total)[:, None]
    logit_grad = logit_grad.astype(BF16)
    upstream = collect(nn(logit_grad, table), 8)
    grad_three, gain_six, gain_seven = norm_back(upstream, norm_four, norm_rows[6])
    branch_three = spread(grad_three.astype(BF16), 9)

    hidden_grad = nt(branch_three, contract)
    gelu_pull = jax.vjp(partial(jax.nn.gelu, approximate=True), preact)[1]
    preact_grad = gelu_pull(hidden_grad)[0].astype(BF16)
    part = nt(preact_grad, expand)
    back, contract_keep, contract_wire, contract_came = collect(
        part, 11, grad(hidden, branch_three, block, BF16)
    )

    back, gain_four, gain_five = norm_back(back, norm_three, norm_rows[4])
    grad_two = grad_three + back
    branch_two = grad_two.astype(BF16) * keep_rows.astype(BF16)
    contract_half = other_half(contract_keep, contract_came, BF16)
    contract_half = contract_half.reshape(2, block // 2, width)
    branch_two, contract_across, expand_keep, expand_wire, expand_came = spread(
        branch_two,
        12,
        swap(((0, 1),), contract_half),
        grad(a_three, preact_grad, in_rows, BF16),
        cut=4,
    )
    attn_grad = nt(branch_two, out_maps[1]).astype(BF16)
    cross_grad, key_grad, value_grad = attend_back(
        attn_grad, cross, text_keys, text_values, probs_two, images
    )
    pair_grad = jnp.concatenate([key_grad, value_grad], 1)
    expand_half = other_half(expand_keep, expand_came, BF16)
    part = nt(cross_grad, w_cross)
    back, contract_across, contract_came, expand_across, text_keep, text_wire, text_came = collect(
        part,
        13,
        swap(((1, 1),), contract_half, contract_across),
        ring((1,), contract_wire, contract_came),
        swap(((0, 2),), expand_half),
        grad(group_captions, pair_grad, text_rows, WIRE),
        cut=4,
    )

    back, gain_two, gain_three = norm_back(back, norm_two, norm_rows[2])
    grad_one = grad_two + back
    branch_one, expand_across, expand_came, cross_keep, cross_wire, cross_came, table_head = spread(
        grad_one.astype(BF16),
        14,
        swap(((2, 2),), expand_half, expand_across),
        ring((1,), expand_wire, expand_came),
        grad(a_two, cross_grad, in_rows, WIRE),
        product(logit_grad, a_four),
        cut=4,
    )
    attn_grad = nt(branch_one, out_maps[0]).astype(BF16)
    triple_grad = attend_back_joint(attn_grad, triple, images)
    out_one = weight_grad(attn_one, branch_one, HD // extent, BF16)
    out_two = weight_grad(attn_two, branch_two, HD // extent, BF16)
    out_keep = jnp.stack([out_one[0], out_two[0]], 1)
    out_wire = jnp.stack([out_one[1], out_two[1]], 2)
    text_half = other_half(text_keep, text_came, WIRE)
    part = nt(triple_grad, w_qkv)
    out_wire = plain(out_wire)
    back, text_across, text_came, out_came, triple_keep, triple_wire, triple_came = collect(
        part,
        15,
        swap(((0, 4),), text_half),
        ring((1,), text_wire, text_came),
        ring((0,), out_wire),
        grad(a_one, triple_grad, in_rows, WIRE),
        cut=4,
    )

    back, gain_zero, gain_one = norm_back(back, norm_one, norm_rows[0])
    grad_zero = grad_one + back
    looked_grad = jnp.where(chosen, 0.0, grad_zero).astype(BF16)
    triple_half = other_half(triple_keep, triple_came, WIRE)
    cross_half = other_half(cross_keep, cross_came, WIRE)
    out_half = other_half(out_keep, out_came, BF16)
    expand_shard = own_half(expand_keep, expand_came, expand_across)
    looked_grad, triple_came, cross_came, triple_across, expand_shard = spread(
        looked_grad,
        16,
        ring((1,), triple_wire, triple_came),
        ring((1,), cross_wire, cross_came),
        swap(((0, 4),), triple_half),
        exchange(plain(expand_shard), hidden_width),
        cut=4,
    )
    table_keep, table_wire = weight_grad(
        at_code.astype(BF16), looked_grad, block, BF16, table_head
    )

    position_grad = jnp.sum(grad_zero.reshape(own_images, length, -1), 0)
    mask_grad = jnp.sum(jnp.where(chosen, grad_zero, 0.0), 0)
    gains = [gain_zero, gain_one, gain_two, gain_three, gain_four, gain_five, gain_six, gain_seven]
    rows = vectors.shape[0]
    padded = -(-rows // 192) * 192
    place_of = jnp.arange(padded - length)[:, None]
    tail = sum(jnp.where(place_of == k, gain, 0.0) for k, gain in enumerate([mask_grad] + gains))
    vector_grad = jnp.concatenate([position_grad, tail], 0)

    text_shard = own_half(text_keep, text_came, text_across)
    vector_part, table_came, out_came, cross_across, out_across, text_shard = group_call(
        SCATTER,
        vector_grad.reshape(8, padded // 8, width),
        17,
        ring((0,), table_wire),
        ring((1,), out_wire, out_came),
        swap(((0, 4),), cross_half),
        swap(((0, out_half.shape[0]),), out_half),
        exchange(plain(text_shard), HD),
        cut=3,
    )
    vector_part = vector_part + send(vector_part, AX, 1, 2)
    if extent == 2:
        vector_part = vector_part + send(vector_part, DX, 1, 2)
    else:
        vector_part = lax.psum(vector_part, DX)
    table_half = other_half(table_keep, table_came, BF16)
    proj_shard = jnp.concatenate(
        [
            own_half(triple_keep, triple_came, triple_across),
            own_half(cross_keep, cross_came, cross_across),
        ],
        2,
    )
    nothing, table_came, table_across, proj_shard = group_call(
        GATHER,
        jnp.broadcast_to(weight[0], (16, 128)),
        18,
        ring((1,), table_wire, table_came),
        swap(((0, 1),), table_half),
        exchange(plain(proj_shard), HD),
    )
    contract_across = contract_across.reshape(1, block, width)
    contract_shard = own_half(contract_keep, contract_came, contract_across).reshape(block, width)
    out_shard = own_half(out_keep, out_came, out_across).reshape(out_state[0].shape)
    table_shard = own_half(table_keep, table_came, table_across).reshape(block, width)

    expand_shard = expand_shard.reshape(expand_state[0].shape)

    shards = (table_shard, proj_shard, text_shard, out_shard, expand_shard, contract_shard)
    squares = sum((jnp.sum(piece * piece) for piece in shards))
    squares = squares + jnp.sum(vector_part * vector_part) / (2 * extent)
    lanes = jnp.arange(128)[None, :]
    numbers = jnp.where(lanes == 0, squares, jnp.where(lanes == 1, loss_sum, 0.0))
    numbers, vector_grad = last_call(jnp.broadcast_to(numbers, (8, 128)), vector_part)
    loss_value = numbers[0, 1] / 8.0 / mask_total
    grad_norm = jnp.sqrt(numbers[0, 0])
    vector_grad = vector_grad.reshape(padded, width)[:rows]
    clip_scale = CLIP / jnp.maximum(grad_norm, CLIP)
    count_step = step_count[0].astype(F32)
    fix_one = 1.0 - BETA_ONE**count_step
    fix_two = 1.0 - BETA_TWO**count_step
    results = [loss_value, grad_norm]
    matrices = (table_state, proj_state, text_state, out_state, expand_state, contract_state)
    updated = [
        adamw(state, grad * clip_scale, RATE_MATRIX, DECAY, fix_one, fix_two)
        for state, grad in zip(matrices, shards)
    ]
    vector_new = adamw(
        vector_state, vector_grad * clip_scale, RATE_VECTOR, 0.0, fix_one, fix_two
    )
    updated.insert(1, vector_new)
    for entry in updated:
        results.extend(entry)
    return tuple(results)


def solution(mesh):
    grid = mesh.devices
    extent = grid.shape[0] // 8
    fine = Mesh(grid.reshape(2, 2, 2, extent, grid.shape[1]), (AX, BX, EX, DX, CX))
    rows = P((CX,) + DP, None)
    both = P(None, DP, CX)
    kinds = (rows, P(), both, both, P(None, (CX,) + DP, None), P(DP, CX), rows)
    states = tuple(kind for kind in kinds for _ in range(3))
    batch = P(None, DP, None)
    return jax.shard_map(
        body,
        mesh=fine,
        in_specs=(batch, batch, P(None, DP), P(None, DP, None, None), P()) + states,
        out_specs=(P(), P()) + states,
        check_vma=False,
    )
```

```python
import math
from functools import partial

import jax
import jax.numpy as jnp
from jax import lax
from jax.experimental import pallas as pl
from jax.experimental.layout import Layout, with_layout_constraint
from jax.experimental.pallas import tpu as pltpu
from jax.sharding import Mesh, PartitionSpec as P

HD = 128
EPS_NORM = 1e-05
CLIP = 0.01
BETA_ONE = 0.9
BETA_TWO = 0.999
ADAM_EPS = 1e-08
DECAY = 0.01
RATE_MATRIX = 0.02
RATE_VECTOR = 0.2
SCALE = HD ** (-0.5)
F32 = jnp.float32
BF16 = jnp.bfloat16
WIRE = jnp.bfloat16

AX, BX, EX, DX, CX = "a", "b", "e", "d", "c"
DP = (AX, BX, EX, DX)
QX = (BX, EX)
MX = (AX, DX)
SWAP = [(0, 1), (1, 0)]
MESH = pl.DeviceIdType.MESH


def dot(x, y, dims):
    return lax.dot_general(x, y, (dims, ((), ())), preferred_element_type=F32)


def nn(x, y):
    return dot(x, y, ((1,), (0,)))


def nt(x, y):
    return dot(x, y, ((1,), (1,)))


def tn(x, y):
    return dot(x, y, ((0,), (0,)))


SHARE, RING, SWAP, EXCHANGE, GRAD, PRODUCT = range(6)
START, FAR, THROUGH = range(3)
GATHER, SCATTER = range(2)


class Here:
    def __init__(self, extent, send, recv, local):
        self.a, self.b, self.e, self.d, self.c = (
            lax.axis_index(name) for name in (AX, BX, EX, DX, CX)
        )
        self.extent = extent
        self.to_a, self.to_b, self.to_e, self.to_c = (
            {AX: 1 - self.a},
            {BX: 1 - self.b},
            {EX: 1 - self.e},
            {CX: 1 - self.c},
        )
        self.to_far = {BX: 1 - self.b, EX: 1 - self.e}
        self.to_d = [{DX: lax.rem(self.d + step, extent)} for step in range(1, extent)]
        self.send, self.recv, self.local = send, recv, local
        self.count = self.local_count = 0
        self.waits = []

    def greet(self, peers):
        barrier = pltpu.get_barrier_semaphore()
        for peer in peers:
            pl.semaphore_signal(barrier, inc=1, device_id=peer, device_id_type=MESH)
        pl.semaphore_wait(barrier, len(peers))

    def copy(self, source, target, peer, hold=False):
        made = pltpu.make_async_remote_copy(
            src_ref=source,
            dst_ref=target,
            send_sem=self.send.at[self.count],
            recv_sem=self.recv.at[self.count],
            device_id=peer,
            device_id_type=MESH,
        )
        self.count += 1
        made.start()
        if not hold:
            self.waits.append(made.wait_send)
        return made

    def late(self, made):
        self.waits.append(made.wait_recv)

    def keep(self, source, target):
        made = pltpu.make_async_copy(source, target, self.local.at[self.local_count])
        self.local_count += 1
        made.start()
        return made

    def finish(self):
        for wait in self.waits:
            wait()


def place(b, e, c):
    return (b * 2 + e) * 2 + c


def spot(array, mode, row, column, first, count):
    if mode == 0:
        return array.at[row, column, pl.ds(first, count)]
    if mode == 1:
        return array.at[row, pl.ds(first, count), column]
    return array.at[pl.ds(first, count), row, column]


def share_start(here, block, array, mode, first, count):
    source = block.at[pl.ds(first, count)]
    target = spot(array, mode, here.a, here.d, first, count)
    here.waits.append(here.keep(source, target).wait)
    across = here.copy(source, target, here.to_a)
    for peer in here.to_d:
        here.late(here.copy(source, target, peer))
    return across


def share_far(here, array, mode, first, count):
    block = spot(array, mode, 1 - here.a, here.d, first, count)
    for peer in here.to_d:
        here.late(here.copy(block, block, peer))


def exchange_start(here, pieces, out, width=0):
    mine = here.b * 2 + here.e
    peers = (
        (None, mine),
        (here.to_e, here.b * 2 + 1 - here.e),
        (here.to_b, (1 - here.b) * 2 + here.e),
        (here.to_far, (1 - here.b) * 2 + 1 - here.e),
    )
    started = []
    for peer, there in peers:
        if width:
            moves = []
            for k in range(pieces.shape[2] // width):
                column = pl.multiple_of((k % 2 * 4 + mine) * width, 128)
                target = out.at[k // 2, :, pl.ds(column, width)]
                moves.append((pieces.at[there, :, pl.ds(k * width, width)], target))
        else:
            moves = [(pieces.at[there], out.at[mine])]
        for source, target in moves:
            if peer is None:
                started.append(here.keep(source, target).wait)
            else:
                started.append(here.copy(source, target, peer).wait_recv)
    return started


def gather_start(here, x_ref, o_ref, cut):
    first, second = pl.ds(0, cut), pl.ds(cut, x_ref.shape[0] - cut)
    me = place(here.b, here.e, here.c)
    e_first = here.copy(x_ref.at[first], o_ref.at[me, first], here.to_e)
    b_first = here.copy(x_ref.at[second], o_ref.at[me, second], here.to_b)
    here.late(here.copy(x_ref, o_ref.at[me], here.to_c))
    e_second = here.copy(x_ref.at[second], o_ref.at[me, second], here.to_e)
    b_second = here.copy(x_ref.at[first], o_ref.at[me, first], here.to_b)
    here.waits.append(here.keep(x_ref, o_ref.at[me]).wait)
    return e_first, b_first, e_second, b_second


def gather_rest(here, o_ref, cut, started):
    first, second = pl.ds(0, cut), pl.ds(cut, o_ref.shape[1] - cut)
    e_first, b_first, e_second, b_second = started
    beside = place(here.b, 1 - here.e, here.c)
    across = place(1 - here.b, here.e, here.c)
    far = place(1 - here.b, 1 - here.e, here.c)

    def on(block, peer):
        return here.copy(block, block, peer)

    e_first.wait_recv()
    b_third = on(o_ref.at[beside, first], here.to_b)
    here.late(on(o_ref.at[beside, first], here.to_c))
    b_first.wait_recv()
    e_third = on(o_ref.at[across, second], here.to_e)
    here.late(on(o_ref.at[across, second], here.to_c))
    e_second.wait_recv()
    here.late(on(o_ref.at[beside, second], here.to_c))
    b_second.wait_recv()
    here.late(on(o_ref.at[across, first], here.to_c))
    b_third.wait_recv()
    here.late(on(o_ref.at[far, first], here.to_c))
    e_third.wait_recv()
    here.late(on(o_ref.at[far, second], here.to_c))


def scatter_start(here, p_ref, paired):
    b, e, c = here.b, here.e, here.c
    order = ((1 - b, 1 - e), (1 - b, e), (b, 1 - e), (b, e))
    return [
        here.copy(p_ref.at[place(bb, ee, 1 - c)], paired.at[k], here.to_c)
        for k, (bb, ee) in enumerate(order)
    ]


def by_rows(start, count, body):
    step = 16 if start % 16 == 0 and count % 16 == 0 else 8

    def some(k, carry):
        body(lambda origin=0: pl.ds(pl.multiple_of(start - origin + k * step, step), step))
        return carry

    lax.fori_loop(0, count // step, some, 0)


def scatter_rest(here, p_ref, o_ref, cut, pairs, paired, held, from_b, from_e, last_b, last_e):
    b, e, c = here.b, here.e, here.c
    count = o_ref.shape[0]
    rest = count - cut
    parts = 2 if cut < rest and rest % 32 == 0 else 1
    chunks = [(cut + k * (rest // parts), rest // parts) for k in range(parts)]
    first, second = pl.ds(0, cut), pl.ds(cut, rest)

    def pair(k, target, spot):
        pairs[k].wait_recv()

        def body(at):
            target[at()] = p_ref[spot, at()] + paired[k, at()]

        by_rows(0, count, body)

    def add(start, size, target, source, origin):
        def body(at):
            target[at()] = target[at()] + source[at(origin)]

        by_rows(start, size, body)

    def first_over_e(k):
        start, size = chunks[k]
        target = from_e.at[0, pl.ds(start - cut, size)]
        return here.copy(held.at[0, pl.ds(start, size)], target, here.to_e, hold=True)

    pair(0, held.at[0], place(1 - b, 1 - e, c))
    moving = first_over_e(0)
    b_first = here.copy(held.at[0, first], from_b.at[0], here.to_b, hold=True)
    pair(2, held.at[2], place(b, 1 - e, c))
    pair(1, held.at[1], place(1 - b, e, c))
    pair(3, o_ref, place(b, e, c))
    b_first.wait_send()
    b_second = here.copy(held.at[1, first], from_b.at[1], here.to_b)
    thirds = []
    for k, (start, size) in enumerate(chunks):
        moving.wait_send()
        came = moving
        if k + 1 < parts:
            moving = first_over_e(k + 1)
        else:
            e_second = here.copy(held.at[2, second], from_e.at[1], here.to_e)
        came.wait_recv()
        add(start, size, held.at[1], from_e.at[0], cut)
        piece = pl.ds(start, size)
        thirds.append(
            here.copy(held.at[1, piece], last_b.at[pl.ds(start - cut, size)], here.to_b)
        )
    b_first.wait_recv()
    add(0, cut, held.at[2], from_b.at[0], 0)
    e_third = here.copy(held.at[2, first], last_e, here.to_e)
    b_second.wait_recv()
    add(0, cut, o_ref, from_b.at[1], 0)
    e_second.wait_recv()
    add(cut, rest, o_ref, from_e.at[1], cut)
    e_third.wait_recv()
    add(0, cut, o_ref, last_e, 0)
    for made, (start, size) in zip(thirds, chunks):
        made.wait_recv()
        add(start, size, o_ref, last_b, cut)


def ring_start(here, halves, source, out):
    lead = source.shape[1]
    for half in halves:
        row, count = {0: (1 - here.a, lead // 2), 1: (here.a, lead // 2)}[half]
        for step, peer in enumerate(here.to_d):
            part = pl.ds(row * count, count)
            here.late(here.copy(source.at[step, part], out.at[step, part], peer))


def columns_of(right):
    wide = min(right.shape[1], 1024)
    return wide, right.shape[1] // wide


def grad_in_kernel(here, rows, left, right, keep, wire):
    lead, extent = keep.shape[0], here.extent
    deep = rows * extent
    wide, blocks = columns_of(right)

    def some(k, carry):
        along = pl.ds(pl.multiple_of(k // blocks * deep, 128), deep)
        across = pl.ds(pl.multiple_of(lax.rem(k, blocks) * wide, 128), wide)
        value = tn(left[:, along], right[:, across])
        for column in range(extent):
            part = value[column * rows : (column + 1) * rows]
            step = lax.rem(column - here.d + extent, extent)

            @pl.when(step == 0)
            def _():
                keep[k // blocks, :, across] = part

            @pl.when(step > 0)
            def _():
                wire[step - 1, k // blocks, :, across] = part.astype(wire.dtype)

        return carry

    lax.fori_loop(0, lead * blocks, some, 0)


def product_in_kernel(left, right, out):
    wide, blocks = columns_of(right)
    deep = 512

    def some(k, carry):
        along = pl.ds(pl.multiple_of(k // blocks * deep, 128), deep)
        across = pl.ds(pl.multiple_of(lax.rem(k, blocks) * wide, 128), wide)
        out[along, across] = tn(left[:, along], right[:, across])
        return carry

    lax.fori_loop(0, left.shape[1] // deep * blocks, some, 0)


def group_kernel(kind, cut, plan, extent, in_count, out_count, *refs):
    ins, outs = list(refs[:in_count]), list(refs[in_count : in_count + out_count])
    scratch = refs[in_count + out_count :]
    here = Here(extent, *scratch[:3])
    x_ref, o_ref = ins.pop(0), outs.pop(0)
    peers = [here.to_b, here.to_e, here.to_c]
    if any(entry[0] == EXCHANGE for entry in plan):
        peers.append(here.to_far)
    if any(
        entry[0] == SWAP or entry[0] == SHARE and any(do[0] != FAR for do in entry[2])
        for entry in plan
    ):
        peers.append(here.to_a)
    if any(entry[0] in (SHARE, RING, GRAD) for entry in plan):
        peers.extend(here.to_d)
    here.greet(peers)
    if kind == GATHER:
        started = gather_start(here, x_ref, o_ref, cut)
    else:
        started = scatter_start(here, x_ref, scratch[3])
    through = []
    for entry in plan:
        if entry[0] in (GRAD, PRODUCT):
            continue
        source, out = ins.pop(0), outs.pop(0)
        if entry[3]:
            ins.pop(0)
        if entry[0] == SHARE:
            for action, first, count in entry[2]:
                if action == FAR:
                    share_far(here, out, entry[1], first, count)
                else:
                    across = share_start(here, source, out, entry[1], first, count)
                    if action == THROUGH:
                        through.append((across, out, entry[1], first, count))
                    else:
                        here.late(across)
        elif entry[0] == RING:
            ring_start(here, entry[2], source, out)
        elif entry[0] == SWAP:
            for first, count in entry[2]:
                part = pl.ds(first, count)
                here.late(here.copy(source.at[part], out.at[part], here.to_a))
        else:
            here.waits.extend(exchange_start(here, source, out, entry[1]))
    for entry in plan:
        if entry[0] == GRAD:
            left, right = ins.pop(0), ins.pop(0)
            keep, wire, out = outs.pop(0), outs.pop(0), outs.pop(0)
            grad_in_kernel(here, entry[1], left, right, keep, wire)
            ring_start(here, entry[2], wire, out)
        elif entry[0] == PRODUCT:
            product_in_kernel(ins.pop(0), ins.pop(0), outs.pop(0))
    if kind == GATHER:
        gather_rest(here, o_ref, cut, started)
    else:
        scatter_rest(here, x_ref, o_ref, cut, started, *scratch[3:])
    for across, out, mode, first, count in through:
        across.wait_recv()
        share_far(here, out, mode, first, count)
    here.finish()


def share(mode, actions, block, array=None):
    return (SHARE, mode, actions, block, array)


def ring(halves, pieces, array=None):
    return (RING, 0, halves, pieces, array)


def swap(parts, piece, array=None):
    return (SWAP, 0, parts, piece, array)


def exchange(pieces, width=0):
    return (EXCHANGE, width, (), pieces, None)


def grad(left, right, rows, wire, halves=(0,)):
    return (GRAD, rows, halves, (left, right, wire), None)


def product(left, right):
    return (PRODUCT, 0, (), (left, right), None)


def group_call(kind, x, number, *moves, cut=2):
    extent = lax.axis_size(DX)
    if kind == GATHER:
        out = jax.ShapeDtypeStruct((8,) + x.shape, x.dtype)
        space, scratch = pl.ANY, []
        cut = x.shape[0] // cut
    else:
        shape = x.shape[1:]
        out = jax.ShapeDtypeStruct(shape, x.dtype)
        space = pltpu.VMEM
        cut = shape[0] // cut
        first, second = (cut,) + shape[1:], (shape[0] - cut,) + shape[1:]
        sizes = ((4,) + shape, (3,) + shape, (2,) + first, (2,) + second, second, first)
        scratch = [pltpu.VMEM(size, x.dtype) for size in sizes]
    operands, outs, aliases, plan, copies, locals_ = [x], [out], {}, [], 16, 2
    anywhere, vmem = pl.BlockSpec(memory_space=pl.ANY), pl.BlockSpec(memory_space=pltpu.VMEM)
    in_specs, out_specs = [pl.BlockSpec(memory_space=space)], [pl.BlockSpec(memory_space=space)]
    worked = {}
    for place_of, (what, mode, actions, source, array) in enumerate(moves):
        if what == GRAD and mode % 128:
            worked[place_of] = weight_grad(source[0], source[1], mode, source[2])
            what, source = RING, worked[place_of][1]
        if what in (GRAD, PRODUCT):
            operands.extend(source[:2])
            in_specs.extend([vmem, vmem])
            rows, columns = source[0].shape[1], source[1].shape[1]
            if what == PRODUCT:
                outs.append(jax.ShapeDtypeStruct((rows, columns), F32))
                out_specs.append(vmem)
            else:
                lead = rows // (mode * extent)
                pieces = jax.ShapeDtypeStruct((extent - 1, lead, mode, columns), source[2])
                outs.append(jax.ShapeDtypeStruct((lead, mode, columns), F32))
                outs.extend([pieces, pieces])
                out_specs.extend([vmem, vmem, anywhere])
            plan.append((what, mode, actions, False))
            copies += 2 * extent
            continue
        operands.append(source)
        if array is not None:
            aliases[len(operands)] = len(outs)
            operands.append(array)
            outs.append(jax.ShapeDtypeStruct(array.shape, array.dtype))
        elif what == SHARE:
            lead, block = source.shape[:1], source.shape[1:]
            full = ((2, extent) + lead, (2,) + lead + (extent,), lead + (2, extent))[mode]
            outs.append(jax.ShapeDtypeStruct(full + block, source.dtype))
        elif what == EXCHANGE and mode:
            parts = source.shape[2] // mode
            shape = (parts // 2, source.shape[1], 8 * mode)
            outs.append(jax.ShapeDtypeStruct(shape, source.dtype))
            copies += 3 * parts
            locals_ += parts
        else:
            outs.append(jax.ShapeDtypeStruct(source.shape, source.dtype))
        in_specs.extend([anywhere] * (len(operands) - len(in_specs)))
        out_specs.append(anywhere)
        plan.append((what, mode, actions, array is not None))
        copies += 3 + 2 * extent * len(actions)
        locals_ += 1 + len(actions)
    held = [ref for ref in scratch] + [
        ref for ref, spec in zip(operands + outs, in_specs + out_specs) if spec is vmem
    ]
    room = 6 << 20 if any(entry[0] in (GRAD, PRODUCT) for entry in plan) else 1 << 20
    if kind == SCATTER:
        held.extend([x, out])
    room += sum(math.prod(ref.shape) * jnp.dtype(ref.dtype).itemsize for ref in held)
    order = [k for k, entry in enumerate(plan) if entry[0] not in (GRAD, PRODUCT)]
    assert order == list(range(len(order)))
    results = pl.pallas_call(
        partial(group_kernel, kind, cut, plan, extent, len(operands), len(outs)),
        out_shape=tuple(outs),
        in_specs=in_specs,
        out_specs=tuple(out_specs),
        scratch_shapes=[
            pltpu.SemaphoreType.DMA((copies,)),
            pltpu.SemaphoreType.DMA((copies,)),
            pltpu.SemaphoreType.DMA((locals_,)),
        ]
        + scratch,
        input_output_aliases=aliases,
        compiler_params=pltpu.CompilerParams(
            collective_id=number, has_side_effects=True, vmem_limit_bytes=room
        ),
        cost_estimate=pl.CostEstimate(
            flops=0, bytes_accessed=80_000_000, transcendentals=0
        ),
    )(*operands)
    if not moves:
        return results[0]
    results = list(results)
    for place_of, (keep, pieces) in worked.items():
        results[place_of + 1 : place_of + 1] = [keep, pieces]
    return tuple(results)


def first_kernel(extent, *refs):
    small, text, table_ref, out_ref, proj_ref, text_ref, expand_ref, contract_ref = refs[:8]
    small_out, text_out, proj_block, table, outs = refs[8:13]
    text_pieces, expand_pieces, contract_block, out_block = refs[13:17]
    table_block, proj_pieces = refs[17:19]
    here = Here(extent, *refs[19:])
    peers = [here.to_b, here.to_e, here.to_c, here.to_far, here.to_a] + here.to_d
    here.greet(peers)
    units, rows = table_block.shape[:2]

    def table_unit(k):
        def body(at):
            table_block[k, at(k * rows)] = table_ref[at()].astype(BF16)

        by_rows(k * rows, rows, body)
        return share_start(here, table_block, table, 0, k, 1)

    def by_head(source, target):
        def body(at):
            for q in range(4):
                for kind in range(source.shape[0]):
                    for row in range(2):
                        target[q, at(), pl.ds((kind * 2 + row) * HD, HD)] = source[
                            kind, at(), pl.ds((row * 4 + q) * HD, HD)
                        ].astype(BF16)

        by_rows(0, source.shape[1], body)

    across = [table_unit(0), table_unit(1), table_unit(2)]
    small_started = gather_start(here, small, small_out, small.shape[0] // 2)
    by_head(proj_ref, proj_pieces)
    here.waits.extend(exchange_start(here, proj_pieces, proj_block))
    gather_rest(here, small_out, small.shape[0] // 2, small_started)
    text_started = gather_start(here, text, text_out, text.shape[0] // 2)
    for k in range(units):
        across[k].wait_recv()
        share_far(here, table, 0, k, 1)
        if k + 3 < units:
            across.append(table_unit(k + 3))
        elif k + 3 == units:
            out_block[...] = out_ref[...].astype(BF16)
            across.append(share_start(here, out_block, outs, 2, 0, 1))
        if k == 0:
            by_head(text_ref, text_pieces)
        elif k == 1:
            gather_rest(here, text_out, text.shape[0] // 2, text_started)
            width = expand_ref.shape[1] // 8

            def body(at):
                for q in range(4):
                    for row in range(2):
                        expand_pieces[q, at(), pl.ds(row * width, width)] = expand_ref[
                            at(), pl.ds((row * 4 + q) * width, width)
                        ].astype(BF16)

            by_rows(0, expand_ref.shape[0], body)
        elif k == 2:
            for unit in range(units):

                def body(at):
                    contract_block[unit, at(unit * rows)] = contract_ref[at()].astype(BF16)

                by_rows(unit * rows, rows, body)
    across[units].wait_recv()
    share_far(here, outs, 2, 0, 1)
    here.finish()


def first_call(small, text, table, outs, proj, text_maps, expand, contract):
    extent = lax.axis_size(DX)
    rows, width = table.shape
    kinds, in_rows, half = proj.shape

    def like(shape, kind=BF16):
        return jax.ShapeDtypeStruct(shape, kind)

    table_shape = (4, rows // 4, width)
    proj_shape = (4, in_rows, kinds * 2 * HD)
    out_shape = [
        like((8,) + small.shape, small.dtype),
        like((8,) + text.shape),
        like(proj_shape),
        like((2, extent) + table_shape),
        like((2, 2, extent) + outs.shape[1:]),
        like((4, text_maps.shape[1], 4 * HD)),
        like((4, in_rows, expand.shape[1] // 4)),
        like(table_shape),
        like(outs.shape),
    ]
    copies = 36 + 12 * extent
    anywhere, vmem = pl.BlockSpec(memory_space=pl.ANY), pl.BlockSpec(memory_space=pltpu.VMEM)
    return pl.pallas_call(
        partial(first_kernel, extent),
        out_shape=tuple(out_shape),
        in_specs=[anywhere] * 2 + [vmem] * 6,
        out_specs=tuple([anywhere] * 5 + [vmem] * 4),
        scratch_shapes=[
            pltpu.VMEM(table_shape, BF16),
            pltpu.VMEM(proj_shape, BF16),
            pltpu.SemaphoreType.DMA((copies,)),
            pltpu.SemaphoreType.DMA((copies,)),
            pltpu.SemaphoreType.DMA((12,)),
        ],
        compiler_params=pltpu.CompilerParams(
            collective_id=1, has_side_effects=True, vmem_limit_bytes=48 << 20
        ),
    )(small, text, table, outs, proj, text_maps, expand, contract)


def last_kernel(extent, tile_ref, x_ref, total_ref, o_ref, send, recv, local, held, sums):
    here = Here(extent, send, recv, local)
    near = [
        {
            BX: lax.rem(here.b + k // 4, 2),
            EX: lax.rem(here.e + k // 2 % 2, 2),
            CX: lax.rem(here.c + k % 2, 2),
        }
        for k in range(1, 8)
    ]
    away = [
        {AX: lax.rem(here.a + k // extent, 2), DX: lax.rem(here.d + k % extent, extent)}
        for k in range(1, 2 * extent)
    ]
    here.greet(near + away)
    first = [here.copy(tile_ref, held.at[k], peer) for k, peer in enumerate(near)]
    cut = x_ref.shape[0] // 3
    started = gather_start(here, x_ref, o_ref, cut)
    for made in first:
        made.wait_recv()
    terms = [tile_ref[...]] + [held[k] for k in range(7)]
    while len(terms) > 1:
        terms = [terms[k] + terms[k + 1] for k in range(0, len(terms), 2)]
    sums[...] = terms[0]
    mine = 7 + here.a * extent + here.d
    second = [here.copy(sums, held.at[mine], peer) for peer in away]
    held[mine] = terms[0]
    gather_rest(here, o_ref, cut, started)
    for made in second:
        made.wait_recv()
    total = held[7]
    for k in range(1, 2 * extent):
        total = total + held[7 + k]
    total_ref[...] = total
    here.finish()


def last_call(tile, x):
    extent = lax.axis_size(DX)
    peers = 6 + 2 * extent
    vmem, anywhere = pl.BlockSpec(memory_space=pltpu.VMEM), pl.BlockSpec(memory_space=pl.ANY)
    return pl.pallas_call(
        partial(last_kernel, extent),
        out_shape=(
            jax.ShapeDtypeStruct(tile.shape, tile.dtype),
            jax.ShapeDtypeStruct((8,) + x.shape, x.dtype),
        ),
        in_specs=[vmem, anywhere],
        out_specs=(vmem, anywhere),
        scratch_shapes=[
            pltpu.SemaphoreType.DMA((peers + 13,)),
            pltpu.SemaphoreType.DMA((peers + 13,)),
            pltpu.SemaphoreType.DMA((1,)),
            pltpu.VMEM((peers + 1,) + tile.shape, tile.dtype),
            pltpu.VMEM(tile.shape, tile.dtype),
        ],
        compiler_params=pltpu.CompilerParams(collective_id=19, has_side_effects=True),
    )(tile, x)


def spread(rows, number, *moves, cut=2):
    count, width = rows.shape
    full = group_call(GATHER, rows, number, *moves, cut=cut)
    if moves:
        return (full[0].reshape(8 * count, width),) + tuple(full[1:])
    return full.reshape(8 * count, width)


def collect(parts, number, *moves, cut=2):
    count, width = parts.shape
    parts = parts.reshape(8, count // 8, width)
    return group_call(SCATTER, parts, number, *moves, cut=cut)


def after(value, *needed):
    return lax.optimization_barrier((value, needed))[0]


def plain(x):
    return with_layout_constraint(x, Layout(tuple(range(x.ndim))))


def send(block, axis, step, extent):
    ring = [(k, (k + step) % extent) for k in range(extent)]
    return plain(lax.ppermute(plain(block), axis, ring))


def pick(array, index, axis):
    return lax.dynamic_slice_in_dim(array, index, 1, axis)


def grad_kernel(with_base, extent, rows, d_ref, left_ref, right_ref, *refs):
    keep_ref, piece_ref = refs[-2:]
    product = tn(left_ref[...], right_ref[...])
    if with_base:
        product = product + refs[0][...]
    for k in range(keep_ref.shape[0]):
        for column in range(extent):
            start = (k * extent + column) * rows
            part = product[start : start + rows]
            step = lax.rem(column - d_ref[0] + extent, extent)

            @pl.when(step == 0)
            def _():
                keep_ref[k] = part

            @pl.when(step > 0)
            def _():
                piece_ref[step - 1, k] = part.astype(piece_ref.dtype)


def weight_grad(left, right, rows, wire, base=None):
    extent = lax.axis_size(DX)
    count, columns = right.shape
    lead = left.shape[1] // (rows * extent)
    if rows % 128:
        full = tn(left, right) if base is None else tn(left, right) + base
        full = full.reshape(lead, extent, rows, columns)
        split = [
            lax.dynamic_index_in_dim(full, lax.rem(lax.axis_index(DX) + s, extent), 1, False)
            for s in range(extent)
        ]
        return split[0], jnp.stack(split[1:]).astype(wire)

    chunk = max(1, lead // 4) if rows * extent * (lead // 4) >= 512 else max(1, 512 // (rows * extent))
    deep = chunk * extent * rows
    wide = columns if columns <= 1024 else columns // 2
    in_specs = [
        pl.BlockSpec((count, deep), lambda k, j, d: (0, k)),
        pl.BlockSpec((count, wide), lambda k, j, d: (0, j)),
    ]
    operands = [left, right]
    if base is not None:
        in_specs.append(pl.BlockSpec((deep, wide), lambda k, j, d: (k, j)))
        operands.append(base)
    return pl.pallas_call(
        partial(grad_kernel, base is not None, extent, rows),
        out_shape=(
            jax.ShapeDtypeStruct((lead, rows, columns), F32),
            jax.ShapeDtypeStruct((extent - 1, lead, rows, columns), wire),
        ),
        grid_spec=pltpu.PrefetchScalarGridSpec(
            num_scalar_prefetch=1,
            grid=(lead // chunk, columns // wide),
            in_specs=in_specs,
            out_specs=(
                pl.BlockSpec((chunk, rows, wide), lambda k, j, d: (k, 0, j)),
                pl.BlockSpec((extent - 1, chunk, rows, wide), lambda k, j, d: (0, k, 0, j)),
            ),
        ),
        compiler_params=pltpu.CompilerParams(vmem_limit_bytes=48 << 20),
        cost_estimate=pl.CostEstimate(
            flops=2 * count * left.shape[1] * columns,
            bytes_accessed=left.size * 2 + right.size * 2 + left.shape[1] * columns * 4,
            transcendentals=0,
        ),
    )(lax.axis_index(DX).reshape(1), *operands)


def total_at(index, keep, pieces):
    total = pick(keep.reshape((2, -1) + keep.shape[1:]), index, 0)
    for step in range(pieces.shape[0]):
        piece = pieces[step].reshape((2, -1) + pieces.shape[2:])
        total = total + pick(piece, index, 0).astype(F32)
    return total[0]


def other_half(keep, pieces, wire):
    return total_at(1 - lax.axis_index(AX), keep, pieces).astype(wire)


def own_half(keep, pieces, across):
    return total_at(lax.axis_index(AX), keep, pieces) + across.astype(F32)


def layer_norm(inputs, gain, bias):
    average = jnp.mean(inputs, -1, keepdims=True)
    centred = inputs - average
    factor = lax.rsqrt(jnp.mean(centred * centred, -1, keepdims=True) + EPS_NORM)
    normed = centred * factor
    return (normed * gain + bias).astype(BF16), (normed, factor)


def norm_back(upstream, saved, gain):
    normed, factor = saved
    inner = upstream * gain
    back = factor * (
        inner
        - jnp.mean(inner, -1, keepdims=True)
        - normed * jnp.mean(inner * normed, -1, keepdims=True)
    )
    return back, jnp.sum(upstream * normed, 0), jnp.sum(upstream, 0)


def each_head(per, query_rows, key_rows):
    for image in range(per):
        for head in range(2):
            columns = pl.ds(head * HD, HD)
            yield pl.ds(image * query_rows, query_rows), pl.ds(image * key_rows, key_rows), columns


def probabilities(query, key):
    scores = nt(query, key) * SCALE
    top = jnp.max(scores, -1, keepdims=True)
    logsum = top + jnp.log(jnp.sum(jnp.exp(scores - top), -1, keepdims=True))
    return jnp.exp(scores - logsum)


def attend_back_kernel(per, g_ref, q_ref, k_ref, v_ref, o_ref):
    sizes = q_ref.shape[0] // per, k_ref.shape[0] // per
    for rows, key_rows, columns in each_head(per, *sizes):
        grad_out = g_ref[rows, columns]
        query, key, value = q_ref[rows, columns], k_ref[key_rows, columns], v_ref[key_rows, columns]
        probs = probabilities(query, key)
        grad_probs = nt(grad_out, value)
        inner = jnp.sum(probs * grad_probs, -1, keepdims=True)
        grad_scores = (probs * (grad_probs - inner)).astype(BF16)
        grads = (
            nn(grad_scores, key) * SCALE,
            tn(grad_scores, query) * SCALE,
            tn(probs.astype(BF16), grad_out),
        )
        for kind, grad in enumerate(grads):
            o_ref[rows, pl.ds(kind * 2 * HD + columns.start, HD)] = grad.astype(BF16)


def attend_back_joint(upstream, triple, images):
    per = 2 if images % 2 == 0 else 1
    rows = triple.shape[0] // images * per

    def spec(kind, kinds=1):
        return pl.BlockSpec((rows, kinds * 2 * HD), lambda k: (k, kind))

    return pl.pallas_call(
        partial(attend_back_kernel, per),
        out_shape=jax.ShapeDtypeStruct(triple.shape, BF16),
        grid=(images // per,),
        in_specs=[spec(0), spec(0), spec(1), spec(2)],
        out_specs=spec(0, 3),
        cost_estimate=pl.CostEstimate(
            flops=20 * triple.shape[0] * HD * HD, bytes_accessed=1 << 22, transcendentals=1 << 18
        ),
    )(upstream, triple, triple, triple)


def dot_images(x, y, x_side, y_side):
    dims = (((x_side,), (y_side,)), ((0,), (0,)))
    return lax.dot_general(x, y, dims, preferred_element_type=F32)


def heads(x, images):
    x = x.reshape(images, -1, x.shape[-1])
    return [x[..., k : k + HD] for k in range(0, x.shape[-1], HD)]


def flat(parts):
    joined = jnp.concatenate([part.astype(BF16) for part in parts], -1)
    return joined.reshape(-1, joined.shape[-1])


def attend(queries, keys, values):
    mixed, saved = [], []
    for query, key, value in zip(queries, keys, values):
        scores = dot_images(query, key, 2, 2) * SCALE
        top = jnp.max(scores, -1, keepdims=True)
        logsum = top + jnp.log(jnp.sum(jnp.exp(scores - top), -1, keepdims=True))
        probs = jnp.exp(scores - logsum)
        mixed.append(dot_images(probs.astype(BF16), value, 2, 1))
        saved.append(probs)
    return flat(mixed), saved


def attend_back(upstream, queries, keys, values, saved, images):
    grads = []
    for grad_out, query, key, value, probs in zip(
        heads(upstream, images), queries, keys, values, saved
    ):
        grad_probs = dot_images(grad_out, value, 2, 2)
        inner = jnp.sum(probs * grad_probs, -1, keepdims=True)
        grad_scores = (probs * (grad_probs - inner)).astype(BF16)
        grads.append(
            (
                dot_images(grad_scores, key, 2, 1) * SCALE,
                dot_images(grad_scores, query, 1, 1) * SCALE,
                dot_images(probs.astype(BF16), grad_out, 1, 1),
            )
        )
    return tuple(flat(parts) for parts in zip(*grads))


def adamw(state, grad, rate, decay, fix_one, fix_two):
    master, first, second = state
    first_new = BETA_ONE * first + (1.0 - BETA_ONE) * grad
    second_new = BETA_TWO * second + (1.0 - BETA_TWO) * grad * grad
    update = first_new / fix_one / (jnp.sqrt(second_new / fix_two) + ADAM_EPS)
    return master - rate * (update + decay * master), first_new, second_new


def body(image_codes, masked, null_caption, captions, step_count, *states):
    table_state, vector_state, proj_state, text_state, out_state, expand_state, contract_state = (
        states[k : k + 3] for k in range(0, 21, 3)
    )
    b, e, c = (lax.axis_index(k) for k in (BX, EX, CX))
    extent = lax.axis_size(DX)
    vectors = vector_state[0]
    length = vectors.shape[0] - 9
    norm_rows = vectors[length + 1 :]
    width = vectors.shape[1]
    block = table_state[0].shape[0]
    kinds, in_rows, half = proj_state[0].shape
    text_rows = text_state[0].shape[1]
    hidden_width = extent * block
    pair = 2 * HD

    own_images = image_codes.shape[1]
    tokens = own_images * length
    small = jnp.concatenate(
        [
            image_codes.reshape(2, -1),
            masked.reshape(2, -1),
            jnp.broadcast_to(null_caption.reshape(2, -1, 1), masked.shape).reshape(2, -1),
        ],
        1,
    )
    small = lax.dynamic_index_in_dim(small, c, 0, False)
    small = jnp.pad(small, (0, -small.shape[0] % (16 * 128)))
    own_mask, own_null = small[tokens : 2 * tokens], small[2 * tokens : 3 * tokens]
    text = lax.dynamic_index_in_dim(captions, c, 0, False)
    text = text.reshape(-1, text.shape[-1])
    gathered, group_captions, proj_block, table, outs, *rest = first_call(
        small.reshape(16, -1),
        text,
        table_state[0],
        out_state[0],
        proj_state[0],
        text_state[0],
        expand_state[0],
        contract_state[0],
    )
    text_pieces, expand_pieces, contract_block, out_block = rest
    gathered = gathered.reshape(8, -1)
    group_captions = group_captions.reshape(-1, group_captions.shape[-1])
    group_codes = gathered[:, :tokens].reshape(-1)
    weight = gathered[:, tokens : 2 * tokens].reshape(-1).astype(F32)
    chosen = own_mask[:, None] == 1
    keep_rows = 1.0 - own_null[:, None].astype(F32)
    images = 8 * own_images
    table = table.reshape(-1, width)
    codes_here = table.shape[0]

    in_half = lax.rem(group_codes, 8 * hidden_width)
    outer = in_half // block
    inside = (
        (group_codes // (8 * hidden_width) == c)
        & (lax.rem(outer // extent, 2) == e)
        & (lax.rem(outer // (2 * extent), 2) == b)
    )
    outer = (outer // (4 * extent)) * extent + lax.rem(outer, extent)
    local_code = jnp.where(inside, outer * block + lax.rem(in_half, block), -1)
    at_code = jnp.arange(codes_here)[None, :] == local_code[:, None]

    part = nn(at_code.astype(BF16), table).astype(BF16)
    looked, proj, text_block = collect(
        part, 2, share(1, ((START, 0, 3),), proj_block), exchange(text_pieces), cut=4
    )
    x_zero = jnp.where(chosen, vectors[length], looked.astype(F32))
    x_zero = x_zero + jnp.tile(vectors[:length], (own_images, 1))
    a_one, norm_one = layer_norm(x_zero, norm_rows[0], norm_rows[1])
    a_one, proj, w_text, expand_block = spread(
        a_one,
        3,
        share(1, ((THROUGH, 3, 1), (FAR, 0, 3)), proj_block, proj),
        share(1, ((START, 0, 1),), text_block),
        exchange(expand_pieces),
        cut=4,
    )
    proj = proj.reshape(width, kinds * pair)
    w_qkv, w_cross = proj[:, : 3 * pair], proj[:, 3 * pair :]
    triple = nn(a_one, w_qkv).astype(BF16)
    queries, keys, values = (
        heads(triple[:, k : k + pair], images) for k in (0, pair, 2 * pair)
    )
    attn_one, unused = attend(queries, keys, values)
    part = nn(attn_one, outs[0].reshape(pair, width))
    back, w_text, outs = collect(
        part,
        4,
        share(1, ((START, 1, 3), (FAR, 0, 1)), text_block, w_text),
        share(2, ((START, 1, 1),), out_block, outs),
        cut=4,
    )
    x_one = x_zero + back

    a_two, norm_two = layer_norm(x_one, norm_rows[2], norm_rows[3])
    a_two, w_text, outs, expand = spread(
        a_two,
        5,
        share(1, ((FAR, 1, 3),), text_block, w_text),
        share(2, ((FAR, 1, 1),), out_block, outs),
        share(1, ((START, 0, 2),), expand_block),
        cut=4,
    )
    w_text = w_text.reshape(-1, 2 * pair)
    out_maps = outs.reshape(2, pair, width)
    text_pair = nn(group_captions, w_text).astype(BF16)
    text_keys, text_values = heads(text_pair[:, :pair], images), heads(text_pair[:, pair:], images)
    cross = heads(nn(a_two, w_cross).astype(BF16), images)
    attn_two, probs_two = attend(cross, text_keys, text_values)
    part = nn(attn_two, out_maps[1])
    back, expand, contract = collect(
        part,
        6,
        share(1, ((START, 2, 2), (FAR, 0, 2)), expand_block, expand),
        share(0, ((START, 0, 2),), contract_block),
        cut=4,
    )
    x_two = x_one + keep_rows * back

    a_three, norm_three = layer_norm(x_two, norm_rows[4], norm_rows[5])
    a_three, expand, contract = spread(
        a_three,
        7,
        share(1, ((FAR, 2, 2),), expand_block, expand),
        share(0, ((FAR, 0, 2), (THROUGH, 2, 1), (THROUGH, 3, 1)), contract_block, contract),
        cut=4,
    )
    expand, contract = expand.reshape(width, -1), contract.reshape(-1, width)
    mask_total = after(jnp.broadcast_to(jnp.sum(weight), (8, 128)), x_two)
    mask_total = mask_total + send(mask_total, AX, 1, 2)
    mask_total = mask_total + sum(send(mask_total, DX, step, extent) for step in range(1, extent))
    mask_total = mask_total[0, 0]
    preact = nn(a_three, expand)
    hidden = jax.nn.gelu(preact, approximate=True).astype(BF16)
    x_three = x_two + collect(nn(hidden, contract), 8)

    a_four, norm_four = layer_norm(x_three, norm_rows[6], norm_rows[7])
    a_four = spread(a_four, 9)
    logits = nt(a_four, table)
    target = jnp.sum(jnp.where(at_code, logits, 0.0), 1)
    top = jnp.max(logits, 1)
    total = jnp.sum(jnp.exp(logits - top[:, None]), 1)
    count = target.shape[0]
    stats = jnp.stack([top, total, target, target])
    stats = group_call(GATHER, stats.reshape(16, count // 4), 10).reshape(8, 4, count)
    peak = jnp.max(stats[:, 0], 0)
    total = jnp.sum(stats[:, 1] * jnp.exp(stats[:, 0] - peak), 0)
    head_logsum = peak + jnp.log(total)
    loss_sum = jnp.sum(weight * (head_logsum - jnp.sum(stats[:, 2], 0)))

    head_probs = jnp.exp(logits - head_logsum[:, None])
    logit_grad = (head_probs - at_code.astype(F32)) * (weight / mask_total)[:, None]
    logit_grad = logit_grad.astype(BF16)
    upstream = collect(nn(logit_grad, table), 8)
    grad_three, gain_six, gain_seven = norm_back(upstream, norm_four, norm_rows[6])
    branch_three = spread(grad_three.astype(BF16), 9)

    hidden_grad = nt(branch_three, contract)
    gelu_pull = jax.vjp(partial(jax.nn.gelu, approximate=True), preact)[1]
    preact_grad = gelu_pull(hidden_grad)[0].astype(BF16)
    part = nt(preact_grad, expand)
    back, contract_keep, contract_wire, contract_came = collect(
        part, 11, grad(hidden, branch_three, block, BF16, (0, 1))
    )

    back, gain_four, gain_five = norm_back(back, norm_three, norm_rows[4])
    grad_two = grad_three + back
    branch_two = grad_two.astype(BF16) * keep_rows.astype(BF16)
    contract_half = other_half(contract_keep, contract_came, BF16)
    contract_half = contract_half.reshape(2, block // 2, width)
    branch_two, contract_across, expand_keep, expand_wire, expand_came = spread(
        branch_two,
        12,
        swap(((0, 1),), contract_half),
        grad(a_three, preact_grad, in_rows, BF16),
        cut=4,
    )
    attn_grad = nt(branch_two, out_maps[1]).astype(BF16)
    cross_grad, key_grad, value_grad = attend_back(
        attn_grad, cross, text_keys, text_values, probs_two, images
    )
    pair_grad = jnp.concatenate([key_grad, value_grad], 1)
    expand_half = other_half(expand_keep, expand_came, BF16)
    part = nt(cross_grad, w_cross)
    back, contract_across, expand_across, text_keep, text_wire, text_came = collect(
        part,
        13,
        swap(((1, 1),), contract_half, contract_across),
        swap(((0, 2),), expand_half),
        grad(group_captions, pair_grad, text_rows, F32),
        cut=4,
    )

    back, gain_two, gain_three = norm_back(back, norm_two, norm_rows[2])
    grad_one = grad_two + back
    branch_one, expand_across, expand_came, cross_keep, cross_wire, cross_came, table_head = spread(
        grad_one.astype(BF16),
        14,
        swap(((2, 2),), expand_half, expand_across),
        ring((1,), expand_wire, expand_came),
        grad(a_two, cross_grad, in_rows, WIRE),
        product(logit_grad, a_four),
        cut=4,
    )
    attn_grad = nt(branch_one, out_maps[0]).astype(BF16)
    triple_grad = attend_back_joint(attn_grad, triple, images)
    out_one = weight_grad(attn_one, branch_one, HD // extent, BF16)
    out_two = weight_grad(attn_two, branch_two, HD // extent, BF16)
    out_keep = jnp.stack([out_one[0], out_two[0]], 1)
    out_wire = jnp.stack([out_one[1], out_two[1]], 2)
    text_half = other_half(text_keep, text_came, F32)
    part = nt(triple_grad, w_qkv)
    out_wire = plain(out_wire)
    back, text_across, out_came, triple_keep, triple_wire, triple_came = collect(
        part,
        15,
        swap(((0, 2),), text_half),
        ring((0,), out_wire),
        grad(a_one, triple_grad, in_rows, WIRE),
        cut=4,
    )

    back, gain_zero, gain_one = norm_back(back, norm_one, norm_rows[0])
    grad_zero = grad_one + back
    looked_grad = jnp.where(chosen, 0.0, grad_zero).astype(BF16)
    triple_half = other_half(triple_keep, triple_came, WIRE)
    cross_half = other_half(cross_keep, cross_came, WIRE)
    out_half = other_half(out_keep, out_came, BF16)
    expand_shard = own_half(expand_keep, expand_came, expand_across)
    looked_grad, text_across, text_came, triple_came, cross_came, triple_across, expand_shard = spread(
        looked_grad,
        16,
        swap(((2, 2),), text_half, text_across),
        ring((1,), text_wire, text_came),
        ring((1,), triple_wire, triple_came),
        ring((1,), cross_wire, cross_came),
        swap(((0, 4),), triple_half),
        exchange(plain(expand_shard), hidden_width),
        cut=4,
    )
    table_keep, table_wire = weight_grad(
        at_code.astype(BF16), looked_grad, block, BF16, table_head
    )

    position_grad = jnp.sum(grad_zero.reshape(own_images, length, -1), 0)
    mask_grad = jnp.sum(jnp.where(chosen, grad_zero, 0.0), 0)
    gains = [gain_zero, gain_one, gain_two, gain_three, gain_four, gain_five, gain_six, gain_seven]
    rows = vectors.shape[0]
    padded = -(-rows // 192) * 192
    place_of = jnp.arange(padded - length)[:, None]
    tail = sum(jnp.where(place_of == k, gain, 0.0) for k, gain in enumerate([mask_grad] + gains))
    vector_grad = jnp.concatenate([position_grad, tail], 0)

    text_shard = own_half(text_keep, text_came, text_across)
    vector_part, table_came, out_came, cross_across, out_across, text_shard = group_call(
        SCATTER,
        vector_grad.reshape(8, padded // 8, width),
        17,
        ring((0,), table_wire),
        ring((1,), out_wire, out_came),
        swap(((0, 4),), cross_half),
        swap(((0, out_half.shape[0]),), out_half),
        exchange(plain(text_shard), HD),
        cut=3,
    )
    vector_part = vector_part + send(vector_part, AX, 1, 2)
    if extent == 2:
        vector_part = vector_part + send(vector_part, DX, 1, 2)
    else:
        vector_part = lax.psum(vector_part, DX)
    table_half = other_half(table_keep, table_came, BF16)
    proj_shard = jnp.concatenate(
        [
            own_half(triple_keep, triple_came, triple_across),
            own_half(cross_keep, cross_came, cross_across),
        ],
        2,
    )
    nothing, table_came, table_across, proj_shard = group_call(
        GATHER,
        jnp.broadcast_to(weight[0], (16, 128)),
        18,
        ring((1,), table_wire, table_came),
        swap(((0, 1),), table_half),
        exchange(plain(proj_shard), HD),
    )
    contract_across = contract_across.reshape(1, block, width)
    contract_shard = own_half(contract_keep, contract_came, contract_across).reshape(block, width)
    out_shard = own_half(out_keep, out_came, out_across).reshape(out_state[0].shape)
    table_shard = own_half(table_keep, table_came, table_across).reshape(block, width)

    expand_shard = expand_shard.reshape(expand_state[0].shape)

    shards = (table_shard, proj_shard, text_shard, out_shard, expand_shard, contract_shard)
    squares = sum((jnp.sum(piece * piece) for piece in shards))
    squares = squares + jnp.sum(vector_part * vector_part) / (2 * extent)
    lanes = jnp.arange(128)[None, :]
    numbers = jnp.where(lanes == 0, squares, jnp.where(lanes == 1, loss_sum, 0.0))
    numbers, vector_grad = last_call(jnp.broadcast_to(numbers, (8, 128)), vector_part)
    loss_value = numbers[0, 1] / 8.0 / mask_total
    grad_norm = jnp.sqrt(numbers[0, 0])
    vector_grad = vector_grad.reshape(padded, width)[:rows]
    clip_scale = CLIP / jnp.maximum(grad_norm, CLIP)
    count_step = step_count[0].astype(F32)
    fix_one = 1.0 - BETA_ONE**count_step
    fix_two = 1.0 - BETA_TWO**count_step
    results = [loss_value, grad_norm]
    matrices = (table_state, proj_state, text_state, out_state, expand_state, contract_state)
    updated = [
        adamw(state, grad * clip_scale, RATE_MATRIX, DECAY, fix_one, fix_two)
        for state, grad in zip(matrices, shards)
    ]
    vector_new = adamw(
        vector_state, vector_grad * clip_scale, RATE_VECTOR, 0.0, fix_one, fix_two
    )
    updated.insert(1, vector_new)
    for entry in updated:
        results.extend(entry)
    return tuple(results)


def solution(mesh):
    grid = mesh.devices
    extent = grid.shape[0] // 8
    fine = Mesh(grid.reshape(2, 2, 2, extent, grid.shape[1]), (AX, BX, EX, DX, CX))
    rows = P((CX,) + DP, None)
    both = P(None, DP, CX)
    kinds = (rows, P(), both, both, P(None, (CX,) + DP, None), P(DP, CX), rows)
    states = tuple(kind for kind in kinds for _ in range(3))
    batch = P(None, DP, None)
    return jax.shard_map(
        body,
        mesh=fine,
        in_specs=(batch, batch, P(None, DP), P(None, DP, None, None), P()) + states,
        out_specs=(P(), P()) + states,
        check_vma=False,
    )
```

```python
import math
from functools import partial

import jax
import jax.numpy as jnp
from jax import lax
from jax.experimental import pallas as pl
from jax.experimental.layout import Layout, with_layout_constraint
from jax.experimental.pallas import tpu as pltpu
from jax.sharding import Mesh, PartitionSpec as P

HD = 128
EPS_NORM = 1e-05
CLIP = 0.01
BETA_ONE = 0.9
BETA_TWO = 0.999
ADAM_EPS = 1e-08
DECAY = 0.01
RATE_MATRIX = 0.02
RATE_VECTOR = 0.2
SCALE = HD ** (-0.5)
F32 = jnp.float32
BF16 = jnp.bfloat16
WIRE = jnp.bfloat16

AX, BX, EX, DX, CX = "a", "b", "e", "d", "c"
DP = (AX, BX, EX, DX)
QX = (BX, EX)
MX = (AX, DX)
SWAP = [(0, 1), (1, 0)]
MESH = pl.DeviceIdType.MESH


def dot(x, y, dims):
    return lax.dot_general(x, y, (dims, ((), ())), preferred_element_type=F32)


def nn(x, y):
    return dot(x, y, ((1,), (0,)))


def nt(x, y):
    return dot(x, y, ((1,), (1,)))


def tn(x, y):
    return dot(x, y, ((0,), (0,)))


SHARE, RING, SWAP, EXCHANGE, GRAD, PRODUCT = range(6)
START, FAR, THROUGH = range(3)
GATHER, SCATTER = range(2)


class Here:
    def __init__(self, extent, send, recv, local):
        self.a, self.b, self.e, self.d, self.c = (
            lax.axis_index(name) for name in (AX, BX, EX, DX, CX)
        )
        self.extent = extent
        self.to_a, self.to_b, self.to_e, self.to_c = (
            {AX: 1 - self.a},
            {BX: 1 - self.b},
            {EX: 1 - self.e},
            {CX: 1 - self.c},
        )
        self.to_far = {BX: 1 - self.b, EX: 1 - self.e}
        self.to_d = [{DX: lax.rem(self.d + step, extent)} for step in range(1, extent)]
        self.send, self.recv, self.local = send, recv, local
        self.count = self.local_count = 0
        self.waits = []

    def greet(self, peers):
        barrier = pltpu.get_barrier_semaphore()
        for peer in peers:
            pl.semaphore_signal(barrier, inc=1, device_id=peer, device_id_type=MESH)
        pl.semaphore_wait(barrier, len(peers))

    def copy(self, source, target, peer, hold=False):
        made = pltpu.make_async_remote_copy(
            src_ref=source,
            dst_ref=target,
            send_sem=self.send.at[self.count],
            recv_sem=self.recv.at[self.count],
            device_id=peer,
            device_id_type=MESH,
        )
        self.count += 1
        made.start()
        if not hold:
            self.waits.append(made.wait_send)
        return made

    def late(self, made):
        self.waits.append(made.wait_recv)

    def keep(self, source, target):
        made = pltpu.make_async_copy(source, target, self.local.at[self.local_count])
        self.local_count += 1
        made.start()
        return made

    def finish(self):
        for wait in self.waits:
            wait()


def place(b, e, c):
    return (b * 2 + e) * 2 + c


def spot(array, mode, row, column, first, count):
    if mode == 0:
        return array.at[row, column, pl.ds(first, count)]
    if mode == 1:
        return array.at[row, pl.ds(first, count), column]
    return array.at[pl.ds(first, count), row, column]


def share_start(here, block, array, mode, first, count):
    source = block.at[pl.ds(first, count)]
    target = spot(array, mode, here.a, here.d, first, count)
    here.waits.append(here.keep(source, target).wait)
    across = here.copy(source, target, here.to_a)
    for peer in here.to_d:
        here.late(here.copy(source, target, peer))
    return across


def share_far(here, array, mode, first, count):
    block = spot(array, mode, 1 - here.a, here.d, first, count)
    for peer in here.to_d:
        here.late(here.copy(block, block, peer))


def exchange_start(here, pieces, out, width=0):
    mine = here.b * 2 + here.e
    peers = (
        (None, mine),
        (here.to_e, here.b * 2 + 1 - here.e),
        (here.to_b, (1 - here.b) * 2 + here.e),
        (here.to_far, (1 - here.b) * 2 + 1 - here.e),
    )
    started = []
    for peer, there in peers:
        if width:
            moves = []
            for k in range(pieces.shape[2] // width):
                column = pl.multiple_of((k % 2 * 4 + mine) * width, 128)
                target = out.at[k // 2, :, pl.ds(column, width)]
                moves.append((pieces.at[there, :, pl.ds(k * width, width)], target))
        else:
            moves = [(pieces.at[there], out.at[mine])]
        for source, target in moves:
            if peer is None:
                started.append(here.keep(source, target).wait)
            else:
                started.append(here.copy(source, target, peer).wait_recv)
    return started


def gather_start(here, x_ref, o_ref, cut):
    first, second = pl.ds(0, cut), pl.ds(cut, x_ref.shape[0] - cut)
    me = place(here.b, here.e, here.c)
    e_first = here.copy(x_ref.at[first], o_ref.at[me, first], here.to_e)
    b_first = here.copy(x_ref.at[second], o_ref.at[me, second], here.to_b)
    here.late(here.copy(x_ref, o_ref.at[me], here.to_c))
    e_second = here.copy(x_ref.at[second], o_ref.at[me, second], here.to_e)
    b_second = here.copy(x_ref.at[first], o_ref.at[me, first], here.to_b)
    here.waits.append(here.keep(x_ref, o_ref.at[me]).wait)
    return e_first, b_first, e_second, b_second


def gather_rest(here, o_ref, cut, started):
    first, second = pl.ds(0, cut), pl.ds(cut, o_ref.shape[1] - cut)
    e_first, b_first, e_second, b_second = started
    beside = place(here.b, 1 - here.e, here.c)
    across = place(1 - here.b, here.e, here.c)
    far = place(1 - here.b, 1 - here.e, here.c)

    def on(block, peer):
        return here.copy(block, block, peer)

    e_first.wait_recv()
    b_third = on(o_ref.at[beside, first], here.to_b)
    here.late(on(o_ref.at[beside, first], here.to_c))
    b_first.wait_recv()
    e_third = on(o_ref.at[across, second], here.to_e)
    here.late(on(o_ref.at[across, second], here.to_c))
    e_second.wait_recv()
    here.late(on(o_ref.at[beside, second], here.to_c))
    b_second.wait_recv()
    here.late(on(o_ref.at[across, first], here.to_c))
    b_third.wait_recv()
    here.late(on(o_ref.at[far, first], here.to_c))
    e_third.wait_recv()
    here.late(on(o_ref.at[far, second], here.to_c))


def scatter_start(here, p_ref, paired):
    b, e, c = here.b, here.e, here.c
    order = ((1 - b, 1 - e), (1 - b, e), (b, 1 - e), (b, e))
    return [
        here.copy(p_ref.at[place(bb, ee, 1 - c)], paired.at[k], here.to_c)
        for k, (bb, ee) in enumerate(order)
    ]


def by_rows(start, count, body):
    step = 16 if start % 16 == 0 and count % 16 == 0 else 8

    def some(k, carry):
        body(lambda origin=0: pl.ds(pl.multiple_of(start - origin + k * step, step), step))
        return carry

    lax.fori_loop(0, count // step, some, 0)


def scatter_rest(here, p_ref, o_ref, cut, pairs, paired, held, from_b, from_e, last_b, last_e):
    b, e, c = here.b, here.e, here.c
    count = o_ref.shape[0]
    rest = count - cut
    parts = 2 if cut < rest and rest % 32 == 0 else 1
    chunks = [(cut + k * (rest // parts), rest // parts) for k in range(parts)]
    first, second = pl.ds(0, cut), pl.ds(cut, rest)

    def pair(k, target, spot):
        pairs[k].wait_recv()

        def body(at):
            target[at()] = p_ref[spot, at()] + paired[k, at()]

        by_rows(0, count, body)

    def add(start, size, target, source, origin):
        def body(at):
            target[at()] = target[at()] + source[at(origin)]

        by_rows(start, size, body)

    def first_over_e(k):
        start, size = chunks[k]
        target = from_e.at[0, pl.ds(start - cut, size)]
        return here.copy(held.at[0, pl.ds(start, size)], target, here.to_e, hold=True)

    pair(0, held.at[0], place(1 - b, 1 - e, c))
    moving = first_over_e(0)
    b_first = here.copy(held.at[0, first], from_b.at[0], here.to_b, hold=True)
    pair(2, held.at[2], place(b, 1 - e, c))
    pair(1, held.at[1], place(1 - b, e, c))
    pair(3, o_ref, place(b, e, c))
    b_first.wait_send()
    b_second = here.copy(held.at[1, first], from_b.at[1], here.to_b)
    thirds = []
    for k, (start, size) in enumerate(chunks):
        moving.wait_send()
        came = moving
        if k + 1 < parts:
            moving = first_over_e(k + 1)
        else:
            e_second = here.copy(held.at[2, second], from_e.at[1], here.to_e)
        came.wait_recv()
        add(start, size, held.at[1], from_e.at[0], cut)
        piece = pl.ds(start, size)
        thirds.append(
            here.copy(held.at[1, piece], last_b.at[pl.ds(start - cut, size)], here.to_b)
        )
    b_first.wait_recv()
    add(0, cut, held.at[2], from_b.at[0], 0)
    e_third = here.copy(held.at[2, first], last_e, here.to_e)
    b_second.wait_recv()
    add(0, cut, o_ref, from_b.at[1], 0)
    e_second.wait_recv()
    add(cut, rest, o_ref, from_e.at[1], cut)
    e_third.wait_recv()
    add(0, cut, o_ref, last_e, 0)
    for made, (start, size) in zip(thirds, chunks):
        made.wait_recv()
        add(start, size, o_ref, last_b, cut)


def ring_start(here, halves, source, out):
    lead = source.shape[1]
    for half in halves:
        row, count = {0: (1 - here.a, lead // 2), 1: (here.a, lead // 2)}[half]
        for step, peer in enumerate(here.to_d):
            part = pl.ds(row * count, count)
            here.late(here.copy(source.at[step, part], out.at[step, part], peer))


def columns_of(right):
    wide = min(right.shape[1], 1024)
    return wide, right.shape[1] // wide


def grad_in_kernel(here, rows, left, right, keep, wire):
    lead, extent = keep.shape[0], here.extent
    deep = rows * extent
    wide, blocks = columns_of(right)

    def some(k, carry):
        along = pl.ds(pl.multiple_of(k // blocks * deep, 128), deep)
        across = pl.ds(pl.multiple_of(lax.rem(k, blocks) * wide, 128), wide)
        value = tn(left[:, along], right[:, across])
        for column in range(extent):
            part = value[column * rows : (column + 1) * rows]
            step = lax.rem(column - here.d + extent, extent)

            @pl.when(step == 0)
            def _():
                keep[k // blocks, :, across] = part

            @pl.when(step > 0)
            def _():
                wire[step - 1, k // blocks, :, across] = part.astype(wire.dtype)

        return carry

    lax.fori_loop(0, lead * blocks, some, 0)


def product_in_kernel(left, right, out):
    wide, blocks = columns_of(right)
    deep = 512

    def some(k, carry):
        along = pl.ds(pl.multiple_of(k // blocks * deep, 128), deep)
        across = pl.ds(pl.multiple_of(lax.rem(k, blocks) * wide, 128), wide)
        out[along, across] = tn(left[:, along], right[:, across])
        return carry

    lax.fori_loop(0, left.shape[1] // deep * blocks, some, 0)


def group_kernel(kind, cut, plan, extent, in_count, out_count, *refs):
    ins, outs = list(refs[:in_count]), list(refs[in_count : in_count + out_count])
    scratch = refs[in_count + out_count :]
    here = Here(extent, *scratch[:3])
    x_ref, o_ref = ins.pop(0), outs.pop(0)
    peers = [here.to_b, here.to_e, here.to_c]
    if any(entry[0] == EXCHANGE for entry in plan):
        peers.append(here.to_far)
    if any(
        entry[0] == SWAP or entry[0] == SHARE and any(do[0] != FAR for do in entry[2])
        for entry in plan
    ):
        peers.append(here.to_a)
    if any(entry[0] in (SHARE, RING, GRAD) for entry in plan):
        peers.extend(here.to_d)
    here.greet(peers)
    if kind == GATHER:
        started = gather_start(here, x_ref, o_ref, cut)
    else:
        started = scatter_start(here, x_ref, scratch[3])
    through = []
    for entry in plan:
        if entry[0] in (GRAD, PRODUCT):
            continue
        source, out = ins.pop(0), outs.pop(0)
        if entry[3]:
            ins.pop(0)
        if entry[0] == SHARE:
            for action, first, count in entry[2]:
                if action == FAR:
                    share_far(here, out, entry[1], first, count)
                else:
                    across = share_start(here, source, out, entry[1], first, count)
                    if action == THROUGH:
                        through.append((across, out, entry[1], first, count))
                    else:
                        here.late(across)
        elif entry[0] == RING:
            ring_start(here, entry[2], source, out)
        elif entry[0] == SWAP:
            for first, count in entry[2]:
                part = pl.ds(first, count)
                here.late(here.copy(source.at[part], out.at[part], here.to_a))
        else:
            here.waits.extend(exchange_start(here, source, out, entry[1]))
    for entry in plan:
        if entry[0] == GRAD:
            left, right = ins.pop(0), ins.pop(0)
            keep, wire, out = outs.pop(0), outs.pop(0), outs.pop(0)
            grad_in_kernel(here, entry[1], left, right, keep, wire)
            ring_start(here, entry[2], wire, out)
        elif entry[0] == PRODUCT:
            product_in_kernel(ins.pop(0), ins.pop(0), outs.pop(0))
    if kind == GATHER:
        gather_rest(here, o_ref, cut, started)
    else:
        scatter_rest(here, x_ref, o_ref, cut, started, *scratch[3:])
    for across, out, mode, first, count in through:
        across.wait_recv()
        share_far(here, out, mode, first, count)
    here.finish()


def share(mode, actions, block, array=None):
    return (SHARE, mode, actions, block, array)


def ring(halves, pieces, array=None):
    return (RING, 0, halves, pieces, array)


def swap(parts, piece, array=None):
    return (SWAP, 0, parts, piece, array)


def exchange(pieces, width=0):
    return (EXCHANGE, width, (), pieces, None)


def grad(left, right, rows, wire, halves=(0,)):
    return (GRAD, rows, halves, (left, right, wire), None)


def product(left, right):
    return (PRODUCT, 0, (), (left, right), None)


def group_call(kind, x, number, *moves, cut=2):
    extent = lax.axis_size(DX)
    if kind == GATHER:
        out = jax.ShapeDtypeStruct((8,) + x.shape, x.dtype)
        space, scratch = pl.ANY, []
        cut = x.shape[0] // cut
    else:
        shape = x.shape[1:]
        out = jax.ShapeDtypeStruct(shape, x.dtype)
        space = pltpu.VMEM
        cut = shape[0] // cut
        first, second = (cut,) + shape[1:], (shape[0] - cut,) + shape[1:]
        sizes = ((4,) + shape, (3,) + shape, (2,) + first, (2,) + second, second, first)
        scratch = [pltpu.VMEM(size, x.dtype) for size in sizes]
    operands, outs, aliases, plan, copies, locals_ = [x], [out], {}, [], 16, 2
    anywhere, vmem = pl.BlockSpec(memory_space=pl.ANY), pl.BlockSpec(memory_space=pltpu.VMEM)
    in_specs, out_specs = [pl.BlockSpec(memory_space=space)], [pl.BlockSpec(memory_space=space)]
    worked = {}
    for place_of, (what, mode, actions, source, array) in enumerate(moves):
        if what == GRAD and mode % 128:
            worked[place_of] = weight_grad(source[0], source[1], mode, source[2])
            what, source = RING, worked[place_of][1]
        if what in (GRAD, PRODUCT):
            operands.extend(source[:2])
            in_specs.extend([vmem, vmem])
            rows, columns = source[0].shape[1], source[1].shape[1]
            if what == PRODUCT:
                outs.append(jax.ShapeDtypeStruct((rows, columns), F32))
                out_specs.append(vmem)
            else:
                lead = rows // (mode * extent)
                pieces = jax.ShapeDtypeStruct((extent - 1, lead, mode, columns), source[2])
                outs.append(jax.ShapeDtypeStruct((lead, mode, columns), F32))
                outs.extend([pieces, pieces])
                out_specs.extend([vmem, vmem, anywhere])
            plan.append((what, mode, actions, False))
            copies += 2 * extent
            continue
        operands.append(source)
        if array is not None:
            aliases[len(operands)] = len(outs)
            operands.append(array)
            outs.append(jax.ShapeDtypeStruct(array.shape, array.dtype))
        elif what == SHARE:
            lead, block = source.shape[:1], source.shape[1:]
            full = ((2, extent) + lead, (2,) + lead + (extent,), lead + (2, extent))[mode]
            outs.append(jax.ShapeDtypeStruct(full + block, source.dtype))
        elif what == EXCHANGE and mode:
            parts = source.shape[2] // mode
            shape = (parts // 2, source.shape[1], 8 * mode)
            outs.append(jax.ShapeDtypeStruct(shape, source.dtype))
            copies += 3 * parts
            locals_ += parts
        else:
            outs.append(jax.ShapeDtypeStruct(source.shape, source.dtype))
        in_specs.extend([anywhere] * (len(operands) - len(in_specs)))
        out_specs.append(anywhere)
        plan.append((what, mode, actions, array is not None))
        copies += 3 + 2 * extent * len(actions)
        locals_ += 1 + len(actions)
    held = [ref for ref in scratch] + [
        ref for ref, spec in zip(operands + outs, in_specs + out_specs) if spec is vmem
    ]
    room = 6 << 20 if any(entry[0] in (GRAD, PRODUCT) for entry in plan) else 1 << 20
    if kind == SCATTER:
        held.extend([x, out])
    room += sum(math.prod(ref.shape) * jnp.dtype(ref.dtype).itemsize for ref in held)
    order = [k for k, entry in enumerate(plan) if entry[0] not in (GRAD, PRODUCT)]
    assert order == list(range(len(order)))
    results = pl.pallas_call(
        partial(group_kernel, kind, cut, plan, extent, len(operands), len(outs)),
        out_shape=tuple(outs),
        in_specs=in_specs,
        out_specs=tuple(out_specs),
        scratch_shapes=[
            pltpu.SemaphoreType.DMA((copies,)),
            pltpu.SemaphoreType.DMA((copies,)),
            pltpu.SemaphoreType.DMA((locals_,)),
        ]
        + scratch,
        input_output_aliases=aliases,
        compiler_params=pltpu.CompilerParams(
            collective_id=number, has_side_effects=True, vmem_limit_bytes=room
        ),
        cost_estimate=pl.CostEstimate(
            flops=0, bytes_accessed=80_000_000, transcendentals=0
        ),
    )(*operands)
    if not moves:
        return results[0]
    results = list(results)
    for place_of, (keep, pieces) in worked.items():
        results[place_of + 1 : place_of + 1] = [keep, pieces]
    return tuple(results)


def first_kernel(extent, *refs):
    small, text, table_ref, out_ref, proj_ref, text_ref, expand_ref, contract_ref = refs[:8]
    small_out, text_out, proj_block, table, outs = refs[8:13]
    text_pieces, expand_pieces, contract_block, out_block = refs[13:17]
    table_block, proj_pieces = refs[17:19]
    here = Here(extent, *refs[19:])
    peers = [here.to_b, here.to_e, here.to_c, here.to_far, here.to_a] + here.to_d
    here.greet(peers)
    units, rows = table_block.shape[:2]

    def table_unit(k):
        def body(at):
            table_block[k, at(k * rows)] = table_ref[at()].astype(BF16)

        by_rows(k * rows, rows, body)
        return share_start(here, table_block, table, 0, k, 1)

    def by_head(source, target):
        def body(at):
            for q in range(4):
                for kind in range(source.shape[0]):
                    for row in range(2):
                        target[q, at(), pl.ds((kind * 2 + row) * HD, HD)] = source[
                            kind, at(), pl.ds((row * 4 + q) * HD, HD)
                        ].astype(BF16)

        by_rows(0, source.shape[1], body)

    across = [table_unit(0), table_unit(1), table_unit(2)]
    small_started = gather_start(here, small, small_out, small.shape[0] // 2)
    by_head(proj_ref, proj_pieces)
    here.waits.extend(exchange_start(here, proj_pieces, proj_block))
    gather_rest(here, small_out, small.shape[0] // 2, small_started)
    text_started = gather_start(here, text, text_out, text.shape[0] // 2)
    for k in range(units):
        across[k].wait_recv()
        share_far(here, table, 0, k, 1)
        if k + 3 < units:
            across.append(table_unit(k + 3))
        elif k + 3 == units:
            out_block[...] = out_ref[...].astype(BF16)
            across.append(share_start(here, out_block, outs, 2, 0, 1))
        if k == 0:
            by_head(text_ref, text_pieces)
        elif k == 1:
            gather_rest(here, text_out, text.shape[0] // 2, text_started)
            width = expand_ref.shape[1] // 8

            def body(at):
                for q in range(4):
                    for row in range(2):
                        expand_pieces[q, at(), pl.ds(row * width, width)] = expand_ref[
                            at(), pl.ds((row * 4 + q) * width, width)
                        ].astype(BF16)

            by_rows(0, expand_ref.shape[0], body)
        elif k == 2:
            for unit in range(units):

                def body(at):
                    contract_block[unit, at(unit * rows)] = contract_ref[at()].astype(BF16)

                by_rows(unit * rows, rows, body)
    across[units].wait_recv()
    share_far(here, outs, 2, 0, 1)
    here.finish()


def first_call(small, text, table, outs, proj, text_maps, expand, contract):
    extent = lax.axis_size(DX)
    rows, width = table.shape
    kinds, in_rows, half = proj.shape

    def like(shape, kind=BF16):
        return jax.ShapeDtypeStruct(shape, kind)

    table_shape = (4, rows // 4, width)
    proj_shape = (4, in_rows, kinds * 2 * HD)
    out_shape = [
        like((8,) + small.shape, small.dtype),
        like((8,) + text.shape),
        like(proj_shape),
        like((2, extent) + table_shape),
        like((2, 2, extent) + outs.shape[1:]),
        like((4, text_maps.shape[1], 4 * HD)),
        like((4, in_rows, expand.shape[1] // 4)),
        like(table_shape),
        like(outs.shape),
    ]
    copies = 36 + 12 * extent
    anywhere, vmem = pl.BlockSpec(memory_space=pl.ANY), pl.BlockSpec(memory_space=pltpu.VMEM)
    return pl.pallas_call(
        partial(first_kernel, extent),
        out_shape=tuple(out_shape),
        in_specs=[anywhere] * 2 + [vmem] * 6,
        out_specs=tuple([anywhere] * 5 + [vmem] * 4),
        scratch_shapes=[
            pltpu.VMEM(table_shape, BF16),
            pltpu.VMEM(proj_shape, BF16),
            pltpu.SemaphoreType.DMA((copies,)),
            pltpu.SemaphoreType.DMA((copies,)),
            pltpu.SemaphoreType.DMA((12,)),
        ],
        compiler_params=pltpu.CompilerParams(
            collective_id=1, has_side_effects=True, vmem_limit_bytes=48 << 20
        ),
    )(small, text, table, outs, proj, text_maps, expand, contract)


def last_kernel(extent, tile_ref, x_ref, total_ref, o_ref, send, recv, local, held, sums):
    here = Here(extent, send, recv, local)
    near = [
        {
            BX: lax.rem(here.b + k // 4, 2),
            EX: lax.rem(here.e + k // 2 % 2, 2),
            CX: lax.rem(here.c + k % 2, 2),
        }
        for k in range(1, 8)
    ]
    away = [
        {AX: lax.rem(here.a + k // extent, 2), DX: lax.rem(here.d + k % extent, extent)}
        for k in range(1, 2 * extent)
    ]
    here.greet(near + away)
    first = [here.copy(tile_ref, held.at[k], peer) for k, peer in enumerate(near)]
    cut = x_ref.shape[0] // 3
    started = gather_start(here, x_ref, o_ref, cut)
    for made in first:
        made.wait_recv()
    terms = [tile_ref[...]] + [held[k] for k in range(7)]
    while len(terms) > 1:
        terms = [terms[k] + terms[k + 1] for k in range(0, len(terms), 2)]
    sums[...] = terms[0]
    mine = 7 + here.a * extent + here.d
    second = [here.copy(sums, held.at[mine], peer) for peer in away]
    held[mine] = terms[0]
    gather_rest(here, o_ref, cut, started)
    for made in second:
        made.wait_recv()
    total = held[7]
    for k in range(1, 2 * extent):
        total = total + held[7 + k]
    total_ref[...] = total
    here.finish()


def last_call(tile, x):
    extent = lax.axis_size(DX)
    peers = 6 + 2 * extent
    vmem, anywhere = pl.BlockSpec(memory_space=pltpu.VMEM), pl.BlockSpec(memory_space=pl.ANY)
    return pl.pallas_call(
        partial(last_kernel, extent),
        out_shape=(
            jax.ShapeDtypeStruct(tile.shape, tile.dtype),
            jax.ShapeDtypeStruct((8,) + x.shape, x.dtype),
        ),
        in_specs=[vmem, anywhere],
        out_specs=(vmem, anywhere),
        scratch_shapes=[
            pltpu.SemaphoreType.DMA((peers + 13,)),
            pltpu.SemaphoreType.DMA((peers + 13,)),
            pltpu.SemaphoreType.DMA((1,)),
            pltpu.VMEM((peers + 1,) + tile.shape, tile.dtype),
            pltpu.VMEM(tile.shape, tile.dtype),
        ],
        compiler_params=pltpu.CompilerParams(collective_id=19, has_side_effects=True),
    )(tile, x)


def spread(rows, number, *moves, cut=2):
    count, width = rows.shape
    full = group_call(GATHER, rows, number, *moves, cut=cut)
    if moves:
        return (full[0].reshape(8 * count, width),) + tuple(full[1:])
    return full.reshape(8 * count, width)


def collect(parts, number, *moves, cut=2):
    count, width = parts.shape
    parts = parts.reshape(8, count // 8, width)
    return group_call(SCATTER, parts, number, *moves, cut=cut)


def after(value, *needed):
    return lax.optimization_barrier((value, needed))[0]


def plain(x):
    return with_layout_constraint(x, Layout(tuple(range(x.ndim))))


def send(block, axis, step, extent):
    ring = [(k, (k + step) % extent) for k in range(extent)]
    return plain(lax.ppermute(plain(block), axis, ring))


def pick(array, index, axis):
    return lax.dynamic_slice_in_dim(array, index, 1, axis)


def grad_kernel(with_base, extent, rows, d_ref, left_ref, right_ref, *refs):
    keep_ref, piece_ref = refs[-2:]
    product = tn(left_ref[...], right_ref[...])
    if with_base:
        product = product + refs[0][...]
    for k in range(keep_ref.shape[0]):
        for column in range(extent):
            start = (k * extent + column) * rows
            part = product[start : start + rows]
            step = lax.rem(column - d_ref[0] + extent, extent)

            @pl.when(step == 0)
            def _():
                keep_ref[k] = part

            @pl.when(step > 0)
            def _():
                piece_ref[step - 1, k] = part.astype(piece_ref.dtype)


def weight_grad(left, right, rows, wire, base=None):
    extent = lax.axis_size(DX)
    count, columns = right.shape
    lead = left.shape[1] // (rows * extent)
    if rows % 128:
        full = tn(left, right) if base is None else tn(left, right) + base
        full = full.reshape(lead, extent, rows, columns)
        split = [
            lax.dynamic_index_in_dim(full, lax.rem(lax.axis_index(DX) + s, extent), 1, False)
            for s in range(extent)
        ]
        return split[0], jnp.stack(split[1:]).astype(wire)

    chunk = max(1, lead // 4) if rows * extent * (lead // 4) >= 512 else max(1, 512 // (rows * extent))
    deep = chunk * extent * rows
    wide = columns if columns <= 1024 else columns // 2
    in_specs = [
        pl.BlockSpec((count, deep), lambda k, j, d: (0, k)),
        pl.BlockSpec((count, wide), lambda k, j, d: (0, j)),
    ]
    operands = [left, right]
    if base is not None:
        in_specs.append(pl.BlockSpec((deep, wide), lambda k, j, d: (k, j)))
        operands.append(base)
    return pl.pallas_call(
        partial(grad_kernel, base is not None, extent, rows),
        out_shape=(
            jax.ShapeDtypeStruct((lead, rows, columns), F32),
            jax.ShapeDtypeStruct((extent - 1, lead, rows, columns), wire),
        ),
        grid_spec=pltpu.PrefetchScalarGridSpec(
            num_scalar_prefetch=1,
            grid=(lead // chunk, columns // wide),
            in_specs=in_specs,
            out_specs=(
                pl.BlockSpec((chunk, rows, wide), lambda k, j, d: (k, 0, j)),
                pl.BlockSpec((extent - 1, chunk, rows, wide), lambda k, j, d: (0, k, 0, j)),
            ),
        ),
        compiler_params=pltpu.CompilerParams(vmem_limit_bytes=48 << 20),
        cost_estimate=pl.CostEstimate(
            flops=2 * count * left.shape[1] * columns,
            bytes_accessed=left.size * 2 + right.size * 2 + left.shape[1] * columns * 4,
            transcendentals=0,
        ),
    )(lax.axis_index(DX).reshape(1), *operands)


def total_at(index, keep, pieces):
    total = pick(keep.reshape((2, -1) + keep.shape[1:]), index, 0)
    for step in range(pieces.shape[0]):
        piece = pieces[step].reshape((2, -1) + pieces.shape[2:])
        total = total + pick(piece, index, 0).astype(F32)
    return total[0]


def other_half(keep, pieces, wire):
    return total_at(1 - lax.axis_index(AX), keep, pieces).astype(wire)


def own_half(keep, pieces, across):
    return total_at(lax.axis_index(AX), keep, pieces) + across.astype(F32)


def layer_norm(inputs, gain, bias):
    average = jnp.mean(inputs, -1, keepdims=True)
    centred = inputs - average
    factor = lax.rsqrt(jnp.mean(centred * centred, -1, keepdims=True) + EPS_NORM)
    normed = centred * factor
    return (normed * gain + bias).astype(BF16), (normed, factor)


def norm_back(upstream, saved, gain):
    normed, factor = saved
    inner = upstream * gain
    back = factor * (
        inner
        - jnp.mean(inner, -1, keepdims=True)
        - normed * jnp.mean(inner * normed, -1, keepdims=True)
    )
    return back, jnp.sum(upstream * normed, 0), jnp.sum(upstream, 0)


def each_head(per, query_rows, key_rows):
    for image in range(per):
        for head in range(2):
            columns = pl.ds(head * HD, HD)
            yield pl.ds(image * query_rows, query_rows), pl.ds(image * key_rows, key_rows), columns


def probabilities(query, key):
    scores = nt(query, key) * SCALE
    top = jnp.max(scores, -1, keepdims=True)
    logsum = top + jnp.log(jnp.sum(jnp.exp(scores - top), -1, keepdims=True))
    return jnp.exp(scores - logsum)


def attend_back_kernel(per, g_ref, q_ref, k_ref, v_ref, o_ref):
    sizes = q_ref.shape[0] // per, k_ref.shape[0] // per
    for rows, key_rows, columns in each_head(per, *sizes):
        grad_out = g_ref[rows, columns]
        query, key, value = q_ref[rows, columns], k_ref[key_rows, columns], v_ref[key_rows, columns]
        probs = probabilities(query, key)
        grad_probs = nt(grad_out, value)
        inner = jnp.sum(probs * grad_probs, -1, keepdims=True)
        grad_scores = (probs * (grad_probs - inner)).astype(BF16)
        grads = (
            nn(grad_scores, key) * SCALE,
            tn(grad_scores, query) * SCALE,
            tn(probs.astype(BF16), grad_out),
        )
        for kind, grad in enumerate(grads):
            o_ref[rows, pl.ds(kind * 2 * HD + columns.start, HD)] = grad.astype(BF16)


def attend_back_joint(upstream, triple, images):
    per = 2 if images % 2 == 0 else 1
    rows = triple.shape[0] // images * per

    def spec(kind, kinds=1):
        return pl.BlockSpec((rows, kinds * 2 * HD), lambda k: (k, kind))

    return pl.pallas_call(
        partial(attend_back_kernel, per),
        out_shape=jax.ShapeDtypeStruct(triple.shape, BF16),
        grid=(images // per,),
        in_specs=[spec(0), spec(0), spec(1), spec(2)],
        out_specs=spec(0, 3),
        cost_estimate=pl.CostEstimate(
            flops=20 * triple.shape[0] * HD * HD, bytes_accessed=1 << 22, transcendentals=1 << 18
        ),
    )(upstream, triple, triple, triple)


def dot_images(x, y, x_side, y_side):
    dims = (((x_side,), (y_side,)), ((0,), (0,)))
    return lax.dot_general(x, y, dims, preferred_element_type=F32)


def heads(x, images):
    x = x.reshape(images, -1, x.shape[-1])
    return [x[..., k : k + HD] for k in range(0, x.shape[-1], HD)]


def flat(parts):
    joined = jnp.concatenate([part.astype(BF16) for part in parts], -1)
    return joined.reshape(-1, joined.shape[-1])


def attend(queries, keys, values):
    mixed, saved = [], []
    for query, key, value in zip(queries, keys, values):
        scores = dot_images(query, key, 2, 2) * SCALE
        top = jnp.max(scores, -1, keepdims=True)
        logsum = top + jnp.log(jnp.sum(jnp.exp(scores - top), -1, keepdims=True))
        probs = jnp.exp(scores - logsum)
        mixed.append(dot_images(probs.astype(BF16), value, 2, 1))
        saved.append(probs)
    return flat(mixed), saved


def attend_back(upstream, queries, keys, values, saved, images):
    grads = []
    for grad_out, query, key, value, probs in zip(
        heads(upstream, images), queries, keys, values, saved
    ):
        grad_probs = dot_images(grad_out, value, 2, 2)
        inner = jnp.sum(probs * grad_probs, -1, keepdims=True)
        grad_scores = (probs * (grad_probs - inner)).astype(BF16)
        grads.append(
            (
                dot_images(grad_scores, key, 2, 1) * SCALE,
                dot_images(grad_scores, query, 1, 1) * SCALE,
                dot_images(probs.astype(BF16), grad_out, 1, 1),
            )
        )
    return tuple(flat(parts) for parts in zip(*grads))


def adamw(state, grad, rate, decay, fix_one, fix_two):
    master, first, second = state
    first_new = BETA_ONE * first + (1.0 - BETA_ONE) * grad
    second_new = BETA_TWO * second + (1.0 - BETA_TWO) * grad * grad
    update = first_new / fix_one / (jnp.sqrt(second_new / fix_two) + ADAM_EPS)
    return master - rate * (update + decay * master), first_new, second_new


def body(image_codes, masked, null_caption, captions, step_count, *states):
    table_state, vector_state, proj_state, text_state, out_state, expand_state, contract_state = (
        states[k : k + 3] for k in range(0, 21, 3)
    )
    b, e, c = (lax.axis_index(k) for k in (BX, EX, CX))
    extent = lax.axis_size(DX)
    vectors = vector_state[0]
    length = vectors.shape[0] - 9
    norm_rows = vectors[length + 1 :]
    width = vectors.shape[1]
    block = table_state[0].shape[0]
    kinds, in_rows, half = proj_state[0].shape
    text_rows = text_state[0].shape[1]
    hidden_width = extent * block
    pair = 2 * HD

    own_images = image_codes.shape[1]
    tokens = own_images * length
    small = jnp.concatenate(
        [
            image_codes.reshape(2, -1),
            masked.reshape(2, -1),
            jnp.broadcast_to(null_caption.reshape(2, -1, 1), masked.shape).reshape(2, -1),
        ],
        1,
    )
    small = lax.dynamic_index_in_dim(small, c, 0, False)
    small = jnp.pad(small, (0, -small.shape[0] % (16 * 128)))
    own_mask, own_null = small[tokens : 2 * tokens], small[2 * tokens : 3 * tokens]
    text = lax.dynamic_index_in_dim(captions, c, 0, False)
    text = text.reshape(-1, text.shape[-1])
    gathered, group_captions, proj_block, table, outs, *rest = first_call(
        small.reshape(16, -1),
        text,
        table_state[0],
        out_state[0],
        proj_state[0],
        text_state[0],
        expand_state[0],
        contract_state[0],
    )
    text_pieces, expand_pieces, contract_block, out_block = rest
    gathered = gathered.reshape(8, -1)
    group_captions = group_captions.reshape(-1, group_captions.shape[-1])
    group_codes = gathered[:, :tokens].reshape(-1)
    weight = gathered[:, tokens : 2 * tokens].reshape(-1).astype(F32)
    chosen = own_mask[:, None] == 1
    keep_rows = 1.0 - own_null[:, None].astype(F32)
    images = 8 * own_images
    table = table.reshape(-1, width)
    codes_here = table.shape[0]

    in_half = lax.rem(group_codes, 8 * hidden_width)
    outer = in_half // block
    inside = (
        (group_codes // (8 * hidden_width) == c)
        & (lax.rem(outer // extent, 2) == e)
        & (lax.rem(outer // (2 * extent), 2) == b)
    )
    outer = (outer // (4 * extent)) * extent + lax.rem(outer, extent)
    local_code = jnp.where(inside, outer * block + lax.rem(in_half, block), -1)
    at_code = jnp.arange(codes_here)[None, :] == local_code[:, None]

    part = nn(at_code.astype(BF16), table).astype(BF16)
    looked, proj, text_block = collect(
        part, 2, share(1, ((START, 0, 3),), proj_block), exchange(text_pieces), cut=4
    )
    x_zero = jnp.where(chosen, vectors[length], looked.astype(F32))
    x_zero = x_zero + jnp.tile(vectors[:length], (own_images, 1))
    a_one, norm_one = layer_norm(x_zero, norm_rows[0], norm_rows[1])
    a_one, proj, w_text, expand_block = spread(
        a_one,
        3,
        share(1, ((THROUGH, 3, 1), (FAR, 0, 3)), proj_block, proj),
        share(1, ((START, 0, 1),), text_block),
        exchange(expand_pieces),
        cut=4,
    )
    proj = proj.reshape(width, kinds * pair)
    w_qkv, w_cross = proj[:, : 3 * pair], proj[:, 3 * pair :]
    triple = nn(a_one, w_qkv).astype(BF16)
    queries, keys, values = (
        heads(triple[:, k : k + pair], images) for k in (0, pair, 2 * pair)
    )
    attn_one, unused = attend(queries, keys, values)
    part = nn(attn_one, outs[0].reshape(pair, width))
    back, w_text, outs = collect(
        part,
        4,
        share(1, ((START, 1, 3), (FAR, 0, 1)), text_block, w_text),
        share(2, ((START, 1, 1),), out_block, outs),
        cut=4,
    )
    x_one = x_zero + back

    a_two, norm_two = layer_norm(x_one, norm_rows[2], norm_rows[3])
    a_two, w_text, outs, expand = spread(
        a_two,
        5,
        share(1, ((FAR, 1, 3),), text_block, w_text),
        share(2, ((FAR, 1, 1),), out_block, outs),
        share(1, ((START, 0, 2),), expand_block),
        cut=4,
    )
    w_text = w_text.reshape(-1, 2 * pair)
    out_maps = outs.reshape(2, pair, width)
    text_pair = nn(group_captions, w_text).astype(BF16)
    text_keys, text_values = heads(text_pair[:, :pair], images), heads(text_pair[:, pair:], images)
    cross = heads(nn(a_two, w_cross).astype(BF16), images)
    attn_two, probs_two = attend(cross, text_keys, text_values)
    part = nn(attn_two, out_maps[1])
    back, expand, contract = collect(
        part,
        6,
        share(1, ((START, 2, 2), (FAR, 0, 2)), expand_block, expand),
        share(0, ((START, 0, 2),), contract_block),
        cut=4,
    )
    x_two = x_one + keep_rows * back

    a_three, norm_three = layer_norm(x_two, norm_rows[4], norm_rows[5])
    a_three, expand, contract = spread(
        a_three,
        7,
        share(1, ((FAR, 2, 2),), expand_block, expand),
        share(0, ((FAR, 0, 2), (THROUGH, 2, 1), (THROUGH, 3, 1)), contract_block, contract),
        cut=4,
    )
    expand, contract = expand.reshape(width, -1), contract.reshape(-1, width)
    mask_total = after(jnp.broadcast_to(jnp.sum(weight), (8, 128)), x_two)
    mask_total = mask_total + send(mask_total, AX, 1, 2)
    mask_total = mask_total + sum(send(mask_total, DX, step, extent) for step in range(1, extent))
    mask_total = mask_total[0, 0]
    preact = nn(a_three, expand)
    hidden = jax.nn.gelu(preact, approximate=True).astype(BF16)
    x_three = x_two + collect(nn(hidden, contract), 8)

    a_four, norm_four = layer_norm(x_three, norm_rows[6], norm_rows[7])
    a_four = spread(a_four, 9)
    logits = nt(a_four, table)
    target = jnp.sum(jnp.where(at_code, logits, 0.0), 1)
    top = jnp.max(logits, 1)
    total = jnp.sum(jnp.exp(logits - top[:, None]), 1)
    count = target.shape[0]
    stats = jnp.stack([top, total, target, target])
    stats = group_call(GATHER, stats.reshape(16, count // 4), 10).reshape(8, 4, count)
    peak = jnp.max(stats[:, 0], 0)
    total = jnp.sum(stats[:, 1] * jnp.exp(stats[:, 0] - peak), 0)
    head_logsum = peak + jnp.log(total)
    loss_sum = jnp.sum(weight * (head_logsum - jnp.sum(stats[:, 2], 0)))

    head_probs = jnp.exp(logits - head_logsum[:, None])
    logit_grad = (head_probs - at_code.astype(F32)) * (weight / mask_total)[:, None]
    logit_grad = logit_grad.astype(BF16)
    upstream = collect(nn(logit_grad, table), 8)
    grad_three, gain_six, gain_seven = norm_back(upstream, norm_four, norm_rows[6])
    branch_three = spread(grad_three.astype(BF16), 9)

    hidden_grad = nt(branch_three, contract)
    gelu_pull = jax.vjp(partial(jax.nn.gelu, approximate=True), preact)[1]
    preact_grad = gelu_pull(hidden_grad)[0].astype(BF16)
    part = nt(preact_grad, expand)
    back, contract_keep, contract_wire, contract_came = collect(
        part, 11, grad(hidden, branch_three, block, BF16, (0, 1))
    )

    back, gain_four, gain_five = norm_back(back, norm_three, norm_rows[4])
    grad_two = grad_three + back
    branch_two = grad_two.astype(BF16) * keep_rows.astype(BF16)
    contract_half = other_half(contract_keep, contract_came, BF16)
    contract_half = contract_half.reshape(2, block // 2, width)
    branch_two, contract_across, expand_keep, expand_wire, expand_came = spread(
        branch_two,
        12,
        swap(((0, 1),), contract_half),
        grad(a_three, preact_grad, in_rows, BF16),
        cut=4,
    )
    attn_grad = nt(branch_two, out_maps[1]).astype(BF16)
    cross_grad, key_grad, value_grad = attend_back(
        attn_grad, cross, text_keys, text_values, probs_two, images
    )
    pair_grad = jnp.concatenate([key_grad, value_grad], 1)
    expand_half = other_half(expand_keep, expand_came, BF16)
    part = nt(cross_grad, w_cross)
    back, contract_across, expand_across, text_keep, text_wire, text_came = collect(
        part,
        13,
        swap(((1, 1),), contract_half, contract_across),
        swap(((0, 2),), expand_half),
        grad(group_captions, pair_grad, text_rows, F32),
        cut=4,
    )

    back, gain_two, gain_three = norm_back(back, norm_two, norm_rows[2])
    grad_one = grad_two + back
    branch_one, expand_across, expand_came, cross_keep, cross_wire, cross_came, table_head = spread(
        grad_one.astype(BF16),
        14,
        swap(((2, 2),), expand_half, expand_across),
        ring((1,), expand_wire, expand_came),
        grad(a_two, cross_grad, in_rows, WIRE),
        product(logit_grad, a_four),
        cut=4,
    )
    attn_grad = nt(branch_one, out_maps[0]).astype(BF16)
    triple_grad = attend_back_joint(attn_grad, triple, images)
    out_one = weight_grad(attn_one, branch_one, HD // extent, BF16)
    out_two = weight_grad(attn_two, branch_two, HD // extent, BF16)
    out_keep = jnp.stack([out_one[0], out_two[0]], 1)
    out_wire = jnp.stack([out_one[1], out_two[1]], 2)
    text_half = other_half(text_keep, text_came, F32)
    part = nt(triple_grad, w_qkv)
    out_wire = plain(out_wire)
    back, text_across, out_came, triple_keep, triple_wire, triple_came = collect(
        part,
        15,
        swap(((0, 2),), text_half),
        ring((0,), out_wire),
        grad(a_one, triple_grad, in_rows, WIRE),
        cut=4,
    )

    back, gain_zero, gain_one = norm_back(back, norm_one, norm_rows[0])
    grad_zero = grad_one + back
    looked_grad = jnp.where(chosen, 0.0, grad_zero).astype(BF16)
    triple_half = other_half(triple_keep, triple_came, WIRE)
    cross_half = other_half(cross_keep, cross_came, WIRE)
    out_half = other_half(out_keep, out_came, BF16)
    expand_shard = own_half(expand_keep, expand_came, expand_across)
    looked_grad, text_across, text_came, triple_came, cross_came, triple_across, expand_shard = spread(
        looked_grad,
        16,
        swap(((2, 2),), text_half, text_across),
        ring((1,), text_wire, text_came),
        ring((1,), triple_wire, triple_came),
        ring((1,), cross_wire, cross_came),
        swap(((0, 2),), triple_half),
        exchange(plain(expand_shard), hidden_width),
        cut=4,
    )
    table_keep, table_wire = weight_grad(
        at_code.astype(BF16), looked_grad, block, BF16, table_head
    )

    position_grad = jnp.sum(grad_zero.reshape(own_images, length, -1), 0)
    mask_grad = jnp.sum(jnp.where(chosen, grad_zero, 0.0), 0)
    gains = [gain_zero, gain_one, gain_two, gain_three, gain_four, gain_five, gain_six, gain_seven]
    rows = vectors.shape[0]
    padded = -(-rows // 192) * 192
    place_of = jnp.arange(padded - length)[:, None]
    tail = sum(jnp.where(place_of == k, gain, 0.0) for k, gain in enumerate([mask_grad] + gains))
    vector_grad = jnp.concatenate([position_grad, tail], 0)

    text_shard = own_half(text_keep, text_came, text_across)
    vector_part, table_came, out_came, triple_across, cross_across, out_across, text_shard = group_call(
        SCATTER,
        vector_grad.reshape(8, padded // 8, width),
        17,
        ring((0,), table_wire),
        ring((1,), out_wire, out_came),
        swap(((2, 2),), triple_half, triple_across),
        swap(((0, 4),), cross_half),
        swap(((0, out_half.shape[0]),), out_half),
        exchange(plain(text_shard), HD),
        cut=3,
    )
    vector_part = vector_part + send(vector_part, AX, 1, 2)
    if extent == 2:
        vector_part = vector_part + send(vector_part, DX, 1, 2)
    else:
        vector_part = lax.psum(vector_part, DX)
    table_half = other_half(table_keep, table_came, BF16)
    proj_shard = jnp.concatenate(
        [
            own_half(triple_keep, triple_came, triple_across),
            own_half(cross_keep, cross_came, cross_across),
        ],
        2,
    )
    nothing, table_came, table_across, proj_shard = group_call(
        GATHER,
        jnp.broadcast_to(weight[0], (16, 128)),
        18,
        ring((1,), table_wire, table_came),
        swap(((0, 1),), table_half),
        exchange(plain(proj_shard), HD),
    )
    contract_across = contract_across.reshape(1, block, width)
    contract_shard = own_half(contract_keep, contract_came, contract_across).reshape(block, width)
    out_shard = own_half(out_keep, out_came, out_across).reshape(out_state[0].shape)
    table_shard = own_half(table_keep, table_came, table_across).reshape(block, width)

    expand_shard = expand_shard.reshape(expand_state[0].shape)

    shards = (table_shard, proj_shard, text_shard, out_shard, expand_shard, contract_shard)
    squares = sum((jnp.sum(piece * piece) for piece in shards))
    squares = squares + jnp.sum(vector_part * vector_part) / (2 * extent)
    lanes = jnp.arange(128)[None, :]
    numbers = jnp.where(lanes == 0, squares, jnp.where(lanes == 1, loss_sum, 0.0))
    numbers, vector_grad = last_call(jnp.broadcast_to(numbers, (8, 128)), vector_part)
    loss_value = numbers[0, 1] / 8.0 / mask_total
    grad_norm = jnp.sqrt(numbers[0, 0])
    vector_grad = vector_grad.reshape(padded, width)[:rows]
    clip_scale = CLIP / jnp.maximum(grad_norm, CLIP)
    count_step = step_count[0].astype(F32)
    fix_one = 1.0 - BETA_ONE**count_step
    fix_two = 1.0 - BETA_TWO**count_step
    results = [loss_value, grad_norm]
    matrices = (table_state, proj_state, text_state, out_state, expand_state, contract_state)
    updated = [
        adamw(state, grad * clip_scale, RATE_MATRIX, DECAY, fix_one, fix_two)
        for state, grad in zip(matrices, shards)
    ]
    vector_new = adamw(
        vector_state, vector_grad * clip_scale, RATE_VECTOR, 0.0, fix_one, fix_two
    )
    updated.insert(1, vector_new)
    for entry in updated:
        results.extend(entry)
    return tuple(results)


def solution(mesh):
    grid = mesh.devices
    extent = grid.shape[0] // 8
    fine = Mesh(grid.reshape(2, 2, 2, extent, grid.shape[1]), (AX, BX, EX, DX, CX))
    rows = P((CX,) + DP, None)
    both = P(None, DP, CX)
    kinds = (rows, P(), both, both, P(None, (CX,) + DP, None), P(DP, CX), rows)
    states = tuple(kind for kind in kinds for _ in range(3))
    batch = P(None, DP, None)
    return jax.shard_map(
        body,
        mesh=fine,
        in_specs=(batch, batch, P(None, DP), P(None, DP, None, None), P()) + states,
        out_specs=(P(), P()) + states,
        check_vma=False,
    )
```
